512 devices in a mesh: slab: 64 (over z, x), shot: 8 (over y, core).
Axes of the slice: x: 4, y: 4, z: 16, core: 2. Of those that a mesh axis runs over, the one named last changes fastest.
Arguments:
- pressure_init: float32 [16, 512, 32, 256], P('shot', 'slab'), may hold values from -6 to 6
- adjoint_init: float32 [16, 512, 32, 256], P('shot', 'slab'), may hold values from -1.5 to 1.5
- density: float32 [512, 32, 256], P('slab'), may hold values from 0.5 to 2
- speed: float32 [512, 32, 256], P('slab'), may hold values from 0.6 to 1.1
- admittance: float32 [512, 32, 256], P('slab'), may hold values from 0.05 to 0.5
- bound_mask: int32 [512, 32, 256], P('slab'), may hold values 0 or 1
- rec_cells: int32 [192, 32], P('slab'), may hold values from 0 to 65535, as said below
- rec_live: int32 [192], P('slab'), may hold values from 0 to 1, as said below
- encoder: float32 [32, 25], replicated, may hold values from -1 to 1
- target: float32 [192, 16, 2, 25], P('slab', 'shot'), may hold values from -6 to 6
Outputs:
- recording: float32 [192, 16, 2, 25], P('slab', 'shot')
- gradient: float32 [512, 32, 256], P('slab')
The draws below stay inside these ranges and needn't reach their ends.
Inputs may be any that keep to these rules, and one draw needn't show every extreme that they name: `rec_live`: in each aligned group of four slabs the numbers of live slots are 3, 1, 0 and 0 in an order drawn from the seed; a slab's live slots come first. `rec_cells`: each slot's 32 capsule cells form a block of 2 x 4 x 4 cells (z, x, y) inside its own slab.
All inputs are finite; a program needn't handle non-finite values. No bound on the sum of `bound_mask` on one device may be relied on, other than what follows from the above.
Results may differ from the reference program's by a relative error of at most 0.00017.
Values sent between devices are 32-bit elements; how exact they have to be, the bound alone decides.
No kernel may reach another device: no remote copies, remote signals or barrier semaphores. Data moves between devices by JAX's collectives and lax.ppermute only.
A program may use at most 64 MiB of HBM per device.

```python
import math
import jax
import jax.numpy as jnp
from jax import lax

CZ = 8
NX = 32
NY = 256
STEPS = 2
CAPS = 32
CH = 25
RSLOT = 3
NZ = 512
SHOTS = 16
REC_SLOTS = 192


def draw_rec_live(key, part):
    slabs = REC_SLOTS // RSLOT
    groups = slabs // 4
    pattern = jnp.array([RSLOT, 1, 0, 0], dtype=jnp.int32)
    keys = jax.random.split(key, groups)
    orders = jax.vmap(lambda single: jax.random.permutation(single, 4))(keys)
    counts = pattern[orders].reshape(-1)
    slots = jnp.arange(RSLOT, dtype=jnp.int32)[None, :]
    return (slots < counts[:, None]).astype(jnp.int32).reshape(-1)


def draw_rec_cells(key, part):
    first, second, third = jax.random.split(jax.random.fold_in(key, 7), 3)
    corner_z = jax.random.randint(first, (REC_SLOTS, 1), 0, CZ - 1)
    corner_x = jax.random.randint(second, (REC_SLOTS, 1), 0, NX - 3)
    corner_y = jax.random.randint(third, (REC_SLOTS, 1), 0, NY - 3)
    corner_z = corner_z.at[0, 0].set(CZ - 2).at[1, 0].set(0)
    corner_x = corner_x.at[0, 0].set(NX - 4).at[1, 0].set(0)
    corner_y = corner_y.at[0, 0].set(NY - 4).at[1, 0].set(0)
    offsets = jnp.arange(32, dtype=jnp.int32)[None, :]
    step_z = offsets // 16
    step_x = offsets // 4 % 4
    step_y = offsets % 4
    flat = (corner_z + step_z) * NX * NY + (corner_x + step_x) * NY + (corner_y + step_y)
    return flat.astype(jnp.int32)


def with_ends(result, rng, smallest, high):
    longest = result.shape.index(max(result.shape))
    spots = []
    for shift in (0, 1):
        where = [jax.random.randint(jax.random.fold_in(rng, axis), (), 0, length) for axis, length in enumerate(result.shape)]
        where[longest] = (where[longest] + shift) % result.shape[longest]
        spots.append(tuple(where))
    return result.at[spots[0]].set(smallest).at[spots[1]].set(high)


def steps_of(rng, dims, shards, smallest, top_value):
    def one(axis_at, shards_of):
        heights = jax.random.uniform(jax.random.fold_in(jax.random.fold_in(rng, 6), axis_at), (shards_of,), jnp.float32, smallest / len(shards), top_value / len(shards))
        return jnp.repeat(jnp.exp(heights), dims[axis_at] // shards_of).reshape((-1,) + (1,) * (len(dims) - axis_at - 1))

    level = one(*shards[0])
    for cut in shards[1:]:
        level = level * one(*cut)
    return level


def centred(stream_key, dims, scale, reach, shards=(), held_as=jnp.bfloat16):
    drawn = jax.random.normal(stream_key, dims, jnp.float32) * scale
    if len(shards) > 0:
        drawn = steps_of(stream_key, dims, shards, -0.22, 0.18) * drawn
    return jnp.clip(drawn, min=-reach, max=reach).astype(held_as)


def setup_inputs(seed: int = 0) -> dict:
    arg_keys = jax.random.split(jax.random.key(seed), 11)
    pressure_init = centred(arg_keys[0], (SHOTS, NZ, NX, NY), 1.0, 6.0, ((0, 8), (1, 64)), jnp.float32)
    adjoint_init = centred(arg_keys[1], (SHOTS, NZ, NX, NY), 0.1, 1.5, ((0, 8), (1, 64)), jnp.float32)
    density = jnp.clip(jnp.exp(math.log(2.0) - 1.3862944 * jax.random.uniform(arg_keys[2], (NZ, NX, NY), jnp.float32) ** steps_of(arg_keys[2], (NZ, NX, NY), ((0, 64),), -0.2, 0.2)), 0.5, 2.0)
    speed = jnp.clip(0.6 + 0.5 * jax.random.uniform(arg_keys[3], (NZ, NX, NY), jnp.float32) ** steps_of(arg_keys[3], (NZ, NX, NY), ((0, 64),), -0.2, 0.2), 0.6, 1.1)
    admittance = jnp.clip(jnp.exp(math.log(0.5) - 2.3025851 * jax.random.uniform(arg_keys[4], (NZ, NX, NY), jnp.float32) ** steps_of(arg_keys[4], (NZ, NX, NY), ((0, 64),), -0.2, 0.2)), 0.05, 0.5)
    bound_mask = with_ends((jax.random.randint(arg_keys[5], (NZ, NX, NY), 0, 2) < 1).astype(jnp.int32), jax.random.fold_in(arg_keys[5], 1), 0, 1)
    rec_cells = draw_rec_cells(jax.random.fold_in(arg_keys[10], 71), 0)
    rec_live = draw_rec_live(jax.random.fold_in(arg_keys[10], 71), 0)
    encoder = centred(arg_keys[8], (CAPS, CH), CAPS ** -0.5, 1.0, (), jnp.float32)
    target = centred(arg_keys[9], (REC_SLOTS, SHOTS, STEPS, CH), 1.0, 6.0, ((0, 64), (1, 8)), jnp.float32)
    return dict(pressure_init=pressure_init, adjoint_init=adjoint_init, density=density, speed=speed, admittance=admittance, bound_mask=bound_mask, rec_cells=rec_cells, rec_live=rec_live, encoder=encoder, target=target)


def rise(values, along):
    widths = [(0, 0)] * values.ndim
    widths[along] = (0, 1)
    padded = jnp.pad(values, widths)
    return lax.slice_in_dim(padded, 1, values.shape[along] + 1, axis=along) - values


def fall(values, along):
    widths = [(0, 0)] * values.ndim
    widths[along] = (1, 0)
    padded = jnp.pad(values, widths)
    return values - lax.slice_in_dim(padded, 0, values.shape[along], axis=along)


def reference(pressure_init, adjoint_init, density, speed, admittance, bound_mask, rec_cells, rec_live, encoder, target):
    wall = bound_mask.astype(jnp.float32)
    vel_coef = 0.5 / density
    pres_coef = 0.5 * density * speed * speed
    damping = 1.0 - admittance * wall
    shots = pressure_init.shape[0]
    slab_cells = CZ * NX * NY
    owner = jnp.arange(REC_SLOTS, dtype=jnp.int32) // RSLOT
    cells = (rec_cells + (owner * slab_cells)[:, None]).astype(jnp.int32)
    live = rec_live.astype(jnp.float32)[:, None, None]
    pressure = pressure_init
    flow_x = jnp.zeros_like(pressure)
    flow_y = jnp.zeros_like(pressure)
    flow_z = jnp.zeros_like(pressure)
    saved = []
    misfit = []
    records = []
    for moment in range(STEPS):
        flow_x = flow_x - vel_coef * rise(pressure, 2)
        flow_y = flow_y - vel_coef * rise(pressure, 3)
        flow_z = flow_z - vel_coef * rise(pressure, 1)
        before = pressure - pres_coef * (fall(flow_x, 2) + fall(flow_y, 3) + fall(flow_z, 1))
        pressure = before * damping
        saved.append(before)
        sampled = pressure.reshape(shots, -1)[:, cells]
        encoded = jnp.einsum("src,ck->rsk", sampled, encoder, precision=lax.Precision.HIGHEST) * live
        records.append(encoded)
        misfit.append(encoded - target[:, :, moment, :] * live)
    recording = jnp.stack(records, axis=2)
    adjoint = adjoint_init
    back_x = jnp.zeros_like(adjoint)
    back_y = jnp.zeros_like(adjoint)
    back_z = jnp.zeros_like(adjoint)
    gradient = jnp.zeros(density.shape, jnp.float32)
    for moment in reversed(range(STEPS)):
        sources = jnp.einsum("rsk,ck->src", misfit[moment], encoder, precision=lax.Precision.HIGHEST)
        flat = adjoint.reshape(shots, -1).at[:, cells.reshape(-1)].add(sources.reshape(shots, -1))
        adjoint = flat.reshape(adjoint_init.shape)
        gradient = gradient - wall * jnp.sum(saved[moment] * adjoint, axis=0)
        if moment > 0:
            scaled = adjoint * damping
            weighted = pres_coef * scaled
            back_x = back_x - rise(weighted, 2)
            back_y = back_y - rise(weighted, 3)
            back_z = back_z - rise(weighted, 1)
            adjoint = scaled - (fall(vel_coef * back_x, 2) + fall(vel_coef * back_y, 3) + fall(vel_coef * back_z, 1))
    return recording, gradient
```

```python
import functools

import jax
import jax.numpy as jnp
from jax import lax
from jax.experimental import pallas as pl
from jax.experimental.pallas import tpu as pltpu
from jax.sharding import PartitionSpec as P

LANES = 128
FAR = float(1 << 20)
TINY = 16
VMEM = pltpu.VMEM
F32 = jnp.float32


def dot(a, b, contract):
    return lax.dot_general(
        a, b, ((contract[:1], contract[1:]), ((), ())),
        precision=lax.Precision.HIGHEST, preferred_element_type=F32,
    )


def edge_masks(shape):
    row = lax.broadcasted_iota(jnp.int32, shape, 0)
    col = lax.broadcasted_iota(jnp.int32, shape, 1)
    return row > 0, row < shape[0] - 1, col > 0, col < shape[1] - 1


def plane_weights(vel, masks):
    low_x, high_x, low_y, high_y = masks
    xp = jnp.where(high_x, vel, 0.0)
    xm = jnp.where(low_x, pltpu.roll(vel, 1, 0), 0.0)
    yp = jnp.where(high_y, vel, 0.0)
    ym = jnp.where(low_y, pltpu.roll(vel, 1, 1), 0.0)
    return xp, xm, yp, ym, 2.0 * vel + xm + ym


def plane_part(u, weights):
    xp, xm, yp, ym, centre = weights
    rows, cols = u.shape
    return (
        xp * pltpu.roll(u, rows - 1, 0) + xm * pltpu.roll(u, 1, 0)
        + yp * pltpu.roll(u, cols - 1, 1) + ym * pltpu.roll(u, 1, 1)
        - centre * u
    )


def pick_columns(cols, width):
    return (lax.broadcasted_iota(jnp.int32, (width, cols.shape[1]), 0) == cols).astype(F32)


def pick_rows(rows, count):
    return (lax.broadcasted_iota(jnp.int32, (count, rows.shape[1]), 0) == rows).astype(F32)


def split_cells(cells, width_x, width_y):
    whole = cells.astype(jnp.int32)
    plane = lax.div(whole, width_x * width_y)
    row = lax.div(whole, width_y)
    return plane, row, row - plane * width_x, whole - row * width_y


def edge_kernel(
    p0, adj_low, adj_high, density, speed, admittance, mask, aux,
    first, up, down, vel_s, pd_s, stack,
):
    shots, depth, width_x, width_y = p0.shape
    masks = edge_masks((width_x, width_y))
    last = depth - 1

    def weights(z):
        return plane_weights(vel_s[z], masks)

    for z in range(depth):
        dens = density[z]
        vel = 0.5 / dens
        spd = speed[z]
        pres = 0.5 * dens * spd * spd
        vel_s[z] = vel
        damp = 1.0 - admittance[z] * mask[z].astype(F32)
        pd_s[z] = pres * damp
        w = plane_weights(vel, masks)
        for s in range(shots):
            here = p0[s, z]
            total = plane_part(here, w)
            if z < last:
                total += vel * (p0[s, z + 1] - here)
            if z > 0:
                total -= vel_s[z - 1] * (here - p0[s, z - 1])
            first[s, z] = here + pres * total

    def damp_of(z):
        return 1.0 - admittance[z] * mask[z].astype(F32)

    plane, _, row_x, col = split_cells(aux[0:1, :], width_x, width_y)
    for side in range(2):
        if side == 0:
            out, near, far, third, adj = down, 0, 1, 2, adj_low
            vel_out = vel_s[0]
        else:
            out, near, far, third, adj = up, last, last - 1, last - 2, adj_high
            vel_out = vel_s[last - 1]
        damp_near, damp_far = damp_of(near), damp_of(far)
        pd_near, pd_far = pd_s[near], pd_s[far]
        vel_near = vel_s[near]
        w_far = weights(far)
        beyond = vel_s[far] if side == 0 else vel_s[third]
        damp_third = damp_of(third)
        base = side * 7 * width_x

        def put(k, value):
            stack[base + k * width_x : base + (k + 1) * width_x, :] = value

        for s in range(shots):
            out[s * width_x : (s + 1) * width_x, :] = p0[s, near]
            out[(2 + s) * width_x : (3 + s) * width_x, :] = damp_near * first[s, near]
            out[(4 + s) * width_x : (5 + s) * width_x, :] = pd_near * adj[s, 0]
            p1_far = damp_far * first[s, far]
            q_far = p0[s, far] + p1_far
            q_third = p0[s, third] + damp_third * first[s, third]
            total = plane_part(q_far, w_far) + beyond * (q_third - q_far) - vel_out * q_far
            put(s, pd_near * vel_out * q_far)
            put(4 + s, damp_far * p1_far + pd_far * total)
        out[6 * width_x : 7 * width_x, :] = vel_near
        out[7 * width_x : 8 * width_x, :] = pd_near
        put(2, damp_near)
        put(3, pd_near * vel_out)
        put(6, pd_far * vel_out)
    columns = pick_columns(col, width_y)
    rows = pick_rows(row_x, width_x)
    found = dot(stack[...], columns, (1, 0))
    for side in range(2):
        out, near, far = (down, 0, 1) if side == 0 else (up, last, last - 1)
        is_near = (plane == near).astype(F32)
        is_far = (plane == far).astype(F32)

        def got(k):
            start = (side * 7 + k) * width_x
            return jnp.sum(found[start : start + width_x, :] * rows, axis=0, keepdims=True)

        tiny = [is_near * got(s) + is_far * got(4 + s) for s in range(shots)]
        tiny += [
            is_near * got(2), is_far * got(6) - is_near * got(3), is_near,
            row_x.astype(F32), col.astype(F32), aux[1:2, :], aux[4:5, :], aux[5:6, :],
        ]
        tiny.append(jnp.zeros((TINY - len(tiny), LANES), F32))
        start = 8 * width_x
        out[start : start + TINY, :] = jnp.zeros((TINY, width_y), F32)
        out[start : start + TINY, 0:LANES] = jnp.concatenate(tiny, axis=0)


def main_kernel(
    core, p0, adj, first, density, speed, admittance, mask, below, above, aux, bd,
    keep, send, coded,
    vel_s, pres_s, damp_s, q_s, p1_s, b2_s, p2_s, w_s, halo_s, src_s, grad_s, b1_edge,
):
    shots, depth, width_x, width_y = p0.shape
    masks = edge_masks((width_x, width_y))
    last = depth - 1
    plane_cells = depth * width_x
    encode = bd[...]
    for z in range(depth):
        dens = density[z]
        spd = speed[z]
        vel_s[z] = 0.5 / dens
        pres_s[z] = 0.5 * dens * spd * spd
        damp_s[z] = 1.0 - admittance[z] * mask[z].astype(F32)

    def halo(ref, k):
        return ref[k * width_x : (k + 1) * width_x, :]

    q_halo, flux = [], []
    for side, (ref, edge, sign) in enumerate(((below, 0, 1.0), (above, last, -1.0))):
        vel_h, pd_h = halo(ref, 6), halo(ref, 7)
        w_h = plane_weights(vel_h, masks)
        vel_b = vel_h if side == 0 else vel_s[last]
        for s in range(shots):
            here, out = p0[s, edge], halo(ref, s)
            step = vel_b * (here - out)
            fixed = first[s, edge] - pres_s[edge] * step
            p1_h = halo(ref, 2 + s) + pd_h * step
            q_h = out + p1_h
            q_edge = here + damp_s[edge] * fixed
            step2 = vel_b * (q_edge - q_h)
            x_h = pd_h * (plane_part(q_h, w_h) + step2)
            base = side * 6 * width_x
            halo_s[base + s * width_x : base + (s + 1) * width_x, :] = p1_h
            halo_s[base + (2 + s) * width_x : base + (3 + s) * width_x, :] = q_h
            halo_s[base + (4 + s) * width_x : base + (5 + s) * width_x, :] = x_h
            b1_edge[s, side] = fixed
            flux.append(step2)
    def b1_of(s, z):
        return b1_edge[s, min(z, 1)] if z in (0, last) else first[s, z]

    for s in range(shots):
        for z in range(depth):
            p1 = damp_s[z] * b1_of(s, z)
            row = s * plane_cells + z * width_x
            p1_s[row : row + width_x, :] = p1
            q_s[s, z] = p0[s, z] + p1
    for z in range(depth):
        vel = vel_s[z]
        w = plane_weights(vel, masks)
        for s in range(shots):
            row = s * plane_cells + z * width_x
            here = q_s[s, z]
            total = plane_part(here, w)
            if z < last:
                total += vel * (q_s[s, z + 1] - here)
            else:
                total -= flux[shots + s]
            if z > 0:
                total -= vel_s[z - 1] * (here - q_s[s, z - 1])
            else:
                total -= flux[s]
            b2 = p1_s[row : row + width_x, :] + pres_s[z] * total
            b2_s[s, z] = b2
            p2_s[row : row + width_x, :] = damp_s[z] * b2
    plane, row, _, col = split_cells(aux[0:1, :], width_x, width_y)
    columns = pick_columns(col, width_y)
    rows = pick_rows(row, plane_cells)
    live = aux[1:2, :]
    for n, field in enumerate((p1_s, p2_s)):
        found = dot(field[...], columns, (1, 0))
        lines = [
            jnp.sum(found[s * plane_cells : (s + 1) * plane_cells, :] * rows, axis=0, keepdims=True)
            for s in range(shots)
        ]
        got = jnp.concatenate(lines + [jnp.zeros((8 - shots, LANES), F32)], axis=0)
        signals = dot(got, encode, (1, 0)) * live
        coded[n * 8 : (n + 1) * 8, :] = signals
        goal = jnp.concatenate(
            [aux[2 + 2 * n : 4 + 2 * n, :], jnp.zeros((8 - shots, LANES), F32)], axis=0
        )
        source = dot(signals - goal, encode, (1, 1))
        spread = jnp.concatenate([rows * source[s : s + 1, :] for s in range(shots)], axis=0)
        src_s[n] = dot(spread, columns, (1, 1))
    w_halo = []
    for side, ref in enumerate((below, above)):
        start = 8 * width_x
        tiny = ref[start : start + TINY, 0:LANES]
        near = tiny[4:5, :]
        rows_h = pick_rows(tiny[5:6, :].astype(jnp.int32), width_x)
        columns_h = pick_columns(tiny[6:7, :].astype(jnp.int32), width_y)
        base = side * 6 * width_x
        found = dot(halo_s[base : base + 6 * width_x, :], columns_h, (1, 0))

        def got_h(k):
            return jnp.sum(found[k * width_x : (k + 1) * width_x, :] * rows_h, axis=0, keepdims=True)

        lines = [
            tiny[s : s + 1, :] + tiny[2:3, :] * got_h(s) + tiny[3:4, :] * got_h(2 + s) + near * got_h(4 + s)
            for s in range(shots)
        ]
        got = jnp.concatenate(lines + [jnp.zeros((8 - shots, LANES), F32)], axis=0)
        goal = jnp.concatenate([tiny[8:10, :], jnp.zeros((8 - shots, LANES), F32)], axis=0)
        misfit = dot(got, encode, (1, 0)) * tiny[7:8, :] - goal
        source = dot(misfit, encode, (1, 1)) * near
        spread = jnp.concatenate([rows_h * source[s : s + 1, :] for s in range(shots)], axis=0)
        placed = dot(spread, columns_h, (1, 1))
        pd_h = halo(ref, 7)
        for s in range(shots):
            w_halo.append(halo(ref, 4 + s) + pd_h * placed[s * width_x : (s + 1) * width_x, :])
    for s in range(shots):
        for z in range(depth):
            row = s * plane_cells + z * width_x
            scaled = damp_s[z] * (adj[s, z] + src_s[1, row : row + width_x, :])
            q_s[s, z] = scaled
            w_s[s, z] = pres_s[z] * scaled
    for z in range(depth):
        vel = vel_s[z]
        w = plane_weights(vel, masks)
        grad = jnp.zeros((width_x, width_y), F32)
        for s in range(shots):
            row = s * plane_cells + z * width_x
            here = w_s[s, z]
            above_w = w_s[s, z + 1] if z < last else w_halo[shots + s]
            total = plane_part(here, w) + vel * (above_w - here)
            if z > 0:
                total -= vel_s[z - 1] * (here - w_s[s, z - 1])
            else:
                total -= halo(below, 6) * (here - w_halo[s])
            back = q_s[s, z] + total + src_s[0, row : row + width_x, :]
            adj1 = adj[s, z] + src_s[1, row : row + width_x, :]
            grad += b2_s[s, z] * adj1 + b1_of(s, z) * back
        grad_s[z] = -(mask[z].astype(F32) * grad)
    half = depth // 2
    mine = core[0] * half
    other = half - mine
    for z in range(half):
        keep[z] = grad_s[mine + z]
        send[z] = grad_s[other + z]


def whole(shape):
    return pl.BlockSpec(shape, lambda i: (0,) * len(shape))


def body(
    pressure_init, adjoint_init, density, speed, admittance, bound_mask,
    rec_cells, rec_live, encoder, target,
):
    shots, depth, width_x, width_y = pressure_init.shape
    slots, capsules = rec_cells.shape
    steps, channels = target.shape[2:]
    slabs, peers = lax.axis_size("slab"), lax.axis_size("shot")
    field = (shots, depth, width_x, width_y)
    slab = (depth, width_x, width_y)
    plane_rows = width_x
    message = (8 * plane_rows + TINY, width_y)

    spare = LANES - slots * capsules
    cells = jnp.pad(rec_cells.reshape(1, -1).astype(F32), ((0, 0), (0, spare)), constant_values=FAR)
    live = rec_live.astype(F32)[:, None]
    live_row = jnp.pad(jnp.broadcast_to(live, (slots, capsules)).reshape(1, -1), ((0, 0), (0, spare)))
    goal = jnp.transpose(target * live[:, :, None, None], (2, 1, 0, 3))
    goal = jnp.pad(goal, ((0, 0),) * 3 + ((0, capsules - channels),)).reshape(steps * shots, -1)
    goal = jnp.pad(goal, ((0, 2), (0, spare)))
    aux = jnp.concatenate([cells, live_row, goal], axis=0)
    padded = jnp.pad(encoder, ((0, 0), (0, capsules - channels)))
    bd = jnp.einsum("ab,ck->acbk", jnp.eye(slots, dtype=F32), padded)
    bd = jnp.pad(bd.reshape(slots * capsules, -1), ((0, spare), (0, spare)))

    edge_plane = (shots, 1, width_x, width_y)
    first, up, down = pl.pallas_call(
        edge_kernel,
        grid=(1,),
        in_specs=[
            whole(field),
            pl.BlockSpec(edge_plane, lambda i: (0, 0, 0, 0)),
            pl.BlockSpec(edge_plane, lambda i: (0, depth - 1, 0, 0)),
            whole(slab), whole(slab), whole(slab), whole(slab), whole(aux.shape),
        ],
        out_specs=[whole(field), whole(message), whole(message)],
        out_shape=[
            jax.ShapeDtypeStruct(field, F32),
            jax.ShapeDtypeStruct(message, F32),
            jax.ShapeDtypeStruct(message, F32),
        ],
        scratch_shapes=[VMEM(slab, F32), VMEM(slab, F32), VMEM((14 * plane_rows, width_y), F32)],
        name="edge",
    )(pressure_init, adjoint_init, adjoint_init, density, speed, admittance, bound_mask, aux)

    below = lax.ppermute(up, "slab", [(i, i + 1) for i in range(slabs - 1)])
    above = lax.ppermute(down, "slab", [(i + 1, i) for i in range(slabs - 1)])

    place = lax.axis_index("shot")
    core = lax.rem(place, 2)
    half = (depth // 2, width_x, width_y)
    flat = (shots * depth * width_x, width_y)
    keep, send, coded = pl.pallas_call(
        main_kernel,
        grid=(1,),
        in_specs=[
            pl.BlockSpec(memory_space=pltpu.SMEM),
            whole(field), whole(field), whole(field),
            whole(slab), whole(slab), whole(slab), whole(slab),
            whole(message), whole(message), whole(aux.shape), whole(bd.shape),
        ],
        out_specs=[whole(half), whole(half), whole((8 * steps, LANES))],
        out_shape=[
            jax.ShapeDtypeStruct(half, F32),
            jax.ShapeDtypeStruct(half, F32),
            jax.ShapeDtypeStruct((8 * steps, LANES), F32),
        ],
        scratch_shapes=[
            VMEM(slab, F32), VMEM(slab, F32), VMEM(slab, F32),
            VMEM(field, F32), VMEM(flat, F32), VMEM(field, F32), VMEM(flat, F32), VMEM(field, F32),
            VMEM((12 * plane_rows, width_y), F32), VMEM((steps, *flat), F32), VMEM(slab, F32),
            VMEM((shots, 2, width_x, width_y), F32),
        ],
        name="main",
    )(
        core[None], pressure_init, adjoint_init, first, density, speed, admittance, bound_mask,
        below, above, aux, bd,
    )

    pairs = [(i, i ^ 1) for i in range(peers)]
    groups = [list(range(c, peers, 2)) for c in range(2)]
    total = keep + lax.ppermute(send, "shot", pairs)
    copies = jnp.broadcast_to(total, (peers // 2, *half))
    total = lax.all_to_all(
        copies, "shot", split_axis=0, concat_axis=0, tiled=True, axis_index_groups=groups
    ).sum(axis=0)
    other = lax.ppermute(total, "shot", pairs)
    gradient = jnp.where(
        core == 0, jnp.concatenate([total, other], 0), jnp.concatenate([other, total], 0)
    )
    signals = coded.reshape(steps, 8, LANES)[:, :shots, : slots * capsules]
    signals = signals.reshape(steps, shots, slots, capsules)[..., :channels]
    return jnp.transpose(signals, (2, 1, 0, 3)), gradient


def solution(mesh):
    placed = (
        P("shot", "slab", None, None), P("shot", "slab", None, None),
        P("slab", None, None), P("slab", None, None), P("slab", None, None), P("slab", None, None),
        P("slab", None), P("slab"), P(), P("slab", "shot", None, None),
    )
    return jax.shard_map(
        body, mesh=mesh, in_specs=placed,
        out_specs=(P("slab", "shot", None, None), P("slab", None, None)),
        check_vma=False,
    )
```

```python
import functools

import jax
import jax.numpy as jnp
from jax import lax
from jax.experimental import pallas as pl
from jax.experimental.pallas import tpu as pltpu
from jax.sharding import PartitionSpec as P

LANES = 128
FAR = float(1 << 20)
WINDOW = 16
VMEM_LIMIT = 20 << 20
EDGE_LIMIT = 62 << 20
TINY = 16
VMEM = pltpu.VMEM
F32 = jnp.float32


def dot(a, b, contract):
    return lax.dot_general(
        a, b, ((contract[:1], contract[1:]), ((), ())), preferred_element_type=F32
    )


def halves(a):
    high = a.astype(jnp.bfloat16)
    return high, (a - high.astype(F32)).astype(jnp.bfloat16)


def pick(a, onehot, contract):
    high, low = halves(a)
    return dot(high, onehot, contract) + dot(low, onehot, contract)


def edge_masks(shape):
    row = lax.broadcasted_iota(jnp.int32, shape, 0)
    col = lax.broadcasted_iota(jnp.int32, shape, 1)
    return row > 0, row < shape[0] - 1, col > 0, col < shape[1] - 1


def plane_weights(vel, masks):
    low_x, high_x, low_y, high_y = masks
    xp = jnp.where(high_x, vel, 0.0)
    xm = jnp.where(low_x, pltpu.roll(vel, 1, 0), 0.0)
    yp = jnp.where(high_y, vel, 0.0)
    ym = jnp.where(low_y, pltpu.roll(vel, 1, 1), 0.0)
    return xp, xm, yp, ym, 2.0 * vel + xm + ym


def plane_part(u, weights):
    xp, xm, yp, ym, centre = weights
    rows, cols = u.shape
    return (
        xp * pltpu.roll(u, rows - 1, 0) + xm * pltpu.roll(u, 1, 0)
        + yp * pltpu.roll(u, cols - 1, 1) + ym * pltpu.roll(u, 1, 1)
        - centre * u
    )


def pick_columns(cols, width):
    return (lax.broadcasted_iota(jnp.int32, (width, cols.shape[1]), 0) == cols).astype(jnp.bfloat16)


def pick_rows(rows, count):
    return (lax.broadcasted_iota(jnp.int32, (count, rows.shape[1]), 0) == rows).astype(F32)


def split_cells(cells, width_x, width_y):
    plane = lax.div(cells, width_x * width_y)
    row = lax.div(cells, width_y)
    return plane, row, row - plane * width_x, cells - row * width_y


def in_lanes(pieces, width, fill=0.0):
    parts = []
    for piece in pieces:
        parts.append(piece)
        if piece.shape[1] < width:
            parts.append(jnp.full((1, width - piece.shape[1]), fill, piece.dtype))
    used = width * len(pieces)
    parts.append(jnp.full((1, LANES - used), fill, pieces[0].dtype))
    return jnp.concatenate(parts, axis=1)


def live_lanes(rec_live, slots, capsules):
    slot = lax.div(lax.broadcasted_iota(jnp.int32, (1, LANES), 1), capsules)
    row = jnp.zeros((1, LANES), F32)
    for r in range(slots):
        row = jnp.where(slot == r, rec_live[r].astype(F32), row)
    return row


def cell_lanes(rec_cells):
    slots, capsules = rec_cells.shape
    return in_lanes([rec_cells[r : r + 1, :] for r in range(slots)], capsules, int(FAR))


def goal_lanes(target, s, n, capsules):
    return in_lanes([target[r, s, n : n + 1, :] for r in range(target.shape[0])], capsules)


def edge_kernel(
    rec_live, rec_cells, target, p0_h, adj_h, density_h, speed_h, admittance_h, mask_h,
    up, down, p0, adj, density, speed, admittance, mask, vel_s, pd_s, stack, sems,
):
    shots, depth, width_x, width_y = p0.shape
    slots, capsules = rec_cells.shape
    half = depth // 2
    last = depth - 1
    copies = []
    for side in range(2):
        some = pl.ds(side * half, half)
        pairs = [(h.at[some], v.at[some]) for h, v in (
            (density_h, density), (speed_h, speed), (admittance_h, admittance), (mask_h, mask))]
        pairs.insert(0, (p0_h.at[:, some], p0.at[:, some]))
        pairs.append((adj_h.at[:, pl.ds(side * last, 1)], adj.at[:, pl.ds(side, 1)]))
        copies.append([
            pltpu.make_async_copy(a, b, sems.at[side, k]) for k, (a, b) in enumerate(pairs)
        ])
    for copy in copies[0] + copies[1]:
        copy.start()
    masks = edge_masks((width_x, width_y))
    plane, _, row_x, col = split_cells(cell_lanes(rec_cells), width_x, width_y)
    live = live_lanes(rec_live, slots, capsules)
    columns = pick_columns(col, width_y)
    rows = pick_rows(row_x, width_x)
    for side in range(2):
        for copy in copies[side]:
            copy.wait()
        if side == 0:
            out, planes, lowest, inward = down, (0, 1, 2), 0, 1
        else:
            out, planes, lowest, inward = up, (last, last - 1, last - 2), half, -1
        near, far, third = planes
        span = range(lowest, lowest + half)
        weights, pres, damp = {}, {}, {}
        for z in span:
            vel_s[z] = 0.5 / density[z]
        for z in planes:
            spd = speed[z]
            pres[z] = 0.5 * density[z] * spd * spd
            damp[z] = 1.0 - admittance[z] * mask[z].astype(F32)
            weights[z] = plane_weights(vel_s[z], masks)
        for z in (near, far):
            pd_s[z] = pres[z] * damp[z]
        wall_low = min(near, far)
        base = side * 7 * width_x

        def put(k, value):
            stack[base + k * width_x : base + (k + 1) * width_x, :] = value

        for s in range(shots):
            first = {}
            for z in planes:
                here = p0[s, z]
                total = plane_part(here, weights[z])
                if z + 1 in span:
                    total += vel_s[z] * (p0[s, z + 1] - here)
                if z - 1 in span:
                    total -= vel_s[z - 1] * (here - p0[s, z - 1])
                first[z] = damp[z] * (here + pres[z] * total)
            out[s * width_x : (s + 1) * width_x, :] = p0[s, near]
            out[(2 + s) * width_x : (3 + s) * width_x, :] = first[near]
            out[(4 + s) * width_x : (5 + s) * width_x, :] = pd_s[near] * adj[s, side]
            q_far = p0[s, far] + first[far]
            q_third = p0[s, third] + first[third]
            beyond = vel_s[min(far, third)]
            total = plane_part(q_far, weights[far]) + beyond * (q_third - q_far)
            total -= vel_s[wall_low] * q_far
            put(s, pd_s[near] * vel_s[wall_low] * q_far)
            put(4 + s, damp[far] * first[far] + pd_s[far] * total)
        out[6 * width_x : 7 * width_x, :] = vel_s[near]
        out[7 * width_x : 8 * width_x, :] = pd_s[near]
        put(2, damp[near])
        put(3, pd_s[near] * vel_s[wall_low])
        put(6, pd_s[far] * vel_s[wall_low])
        found = pick(stack[base : base + 7 * width_x, :], columns, (1, 0))
        is_near = (plane == near).astype(F32)
        is_far = (plane == far).astype(F32)

        def got(k):
            return jnp.sum(found[k * width_x : (k + 1) * width_x, :] * rows, axis=0, keepdims=True)

        tiny = [is_near * got(s) + is_far * got(4 + s) for s in range(shots)]
        tiny += [
            is_near * got(2), is_far * got(6) - is_near * got(3), is_near,
            row_x.astype(F32), col.astype(F32), live,
        ]
        tiny += [live * goal_lanes(target, s, 1, capsules) for s in range(shots)]
        tiny.append(jnp.zeros((TINY - len(tiny), LANES), F32))
        start = 8 * width_x
        out[start : start + TINY, :] = jnp.zeros((TINY, width_y), F32)
        out[start : start + TINY, 0:LANES] = jnp.concatenate(tiny, axis=0)


def middle_kernel(
    rec_live, rec_cells, target, encoder, p0, adj, density, speed, admittance, mask,
    b1, b2, vel_s, pres_s, damp_s, pd_s, back_e, grad, rows_out, code_high, code_low,
    q_s, w_s,
):
    shots, depth, width_x, width_y = p0.shape
    slots, capsules = rec_cells.shape
    steps, channels = target.shape[2:]
    masks = edge_masks((width_x, width_y))
    last = depth - 1
    edges = (0, 1, last - 1, last)
    for z in range(depth):
        dens = density[z]
        spd = speed[z]
        vel = 0.5 / dens
        pres = 0.5 * dens * spd * spd
        damp = 1.0 - admittance[z] * mask[z].astype(F32)
        vel_s[z] = vel
        pres_s[z] = pres
        damp_s[z] = damp
        pd_s[z] = pres * damp
        w = plane_weights(vel, masks)
        for s in range(shots):
            here = p0[s, z]
            total = plane_part(here, w)
            if z < last:
                total += vel * (p0[s, z + 1] - here)
            if z > 0:
                total -= vel_s[z - 1] * (here - p0[s, z - 1])
            value = here + pres * total
            b1[s, z] = value
            q_s[s, z] = here + damp * value
            w_s[s, z] = pd_s[z] * adj[s, z]
    for z in range(depth):
        vel = vel_s[z]
        w = plane_weights(vel, masks)
        sums = jnp.zeros((width_x, width_y), F32)
        for s in range(shots):
            here, weighted = q_s[s, z], w_s[s, z]
            total = plane_part(here, w)
            back = plane_part(weighted, w)
            if z < last:
                total += vel * (q_s[s, z + 1] - here)
                back += vel * (w_s[s, z + 1] - weighted)
            if z > 0:
                total -= vel_s[z - 1] * (here - q_s[s, z - 1])
                back -= vel_s[z - 1] * (weighted - w_s[s, z - 1])
            value = damp_s[z] * b1[s, z] + pres_s[z] * total
            b2[s, z] = value
            back += damp_s[z] * adj[s, z]
            if z in edges:
                back_e[s, edges.index(z)] = back
            else:
                sums += value * adj[s, z] + b1[s, z] * back
        grad[z] = -(mask[z].astype(F32) * sums)
    lane = lax.broadcasted_iota(jnp.int32, (LANES, LANES), 1)
    line = lax.broadcasted_iota(jnp.int32, (LANES, LANES), 0)
    same = (lax.div(lane, capsules) == lax.div(line, capsules)) & (line < slots * capsules)
    code = jnp.concatenate([encoder[...], jnp.zeros((capsules, capsules - channels), F32)], axis=1)
    code = jnp.concatenate([code] * (LANES // capsules), axis=1)
    code = jnp.where(same, jnp.concatenate([code] * (LANES // capsules), axis=0), 0.0)
    square = lax.dot_general(
        code, code, (((1,), (1,)), ((), ())),
        precision=lax.Precision.HIGHEST, preferred_element_type=F32,
    )
    both = jnp.concatenate([code, square], axis=1)
    code_high[...], code_low[...] = halves(both)
    live = live_lanes(rec_live, slots, capsules)
    goal = [live * goal_lanes(target, s, n, capsules) for n in range(steps) for s in range(shots)]
    goal = jnp.concatenate(goal + [jnp.zeros((8 - len(goal), LANES), F32)], axis=0)
    rows_out[0:8, :] = lax.dot_general(
        goal, code, (((1,), (1,)), ((), ())),
        precision=lax.Precision.HIGHEST, preferred_element_type=F32,
    )
    rows_out[8:16, :] = jnp.concatenate(
        [cell_lanes(rec_cells).astype(F32), live, jnp.zeros((6, LANES), F32)], axis=0
    )


def window_part(u, vel, masks):
    low_x, high_x, low_y, high_y = masks
    rows, cols = u.shape
    flow_x = vel * (jnp.where(high_x, pltpu.roll(u, rows - 1, 0), 0.0) - u)
    flow_y = vel * (jnp.where(high_y, pltpu.roll(u, cols - 1, 1), 0.0) - u)
    fall_x = flow_x - jnp.where(low_x, pltpu.roll(flow_x, 1, 0), 0.0)
    return fall_x + flow_y - jnp.where(low_y, pltpu.roll(flow_y, 1, 1), 0.0)


def last_kernel(
    capsules, core, corners, below, above, p0, adj, mask, vel_s, pres_s, damp_s, pd_s, back_e,
    rows_in, code_high, code_low, b1_in, b2_in, grad_in,
    keep, send, coded, b1, b2, grad,
    halo_s, stack, spread,
):
    shots, depth, width_x, width_y = p0.shape
    slots = corners.shape[0]
    masks = edge_masks((width_x, width_y))
    last = depth - 1
    edges = (0, 1, last - 1, last)
    sides = ((below, 0, 1), (above, last, last - 1))
    blank = jnp.zeros((1, LANES), F32)

    def halo(ref, k):
        return ref[k * width_x : (k + 1) * width_x, :]

    def rows_of(array, k, count):
        return array[k * count : (k + 1) * count, :]

    for side, (ref, edge, inner) in enumerate(sides):
        vel_h, pd_h = halo(ref, 6), halo(ref, 7)
        vel_b = vel_h if side == 0 else vel_s[last]
        vel_in = vel_s[min(edge, inner)]
        w_h = plane_weights(vel_h, masks)
        w_e = plane_weights(vel_s[edge], masks)
        for s in range(shots):
            here, out = p0[s, edge], halo(ref, s)
            step = vel_b * (here - out)
            p1_h = halo(ref, 2 + s) + pd_h * step
            q_h = out + p1_h
            fixed = b1[s, edge] - pres_s[edge] * step
            change = -(pd_s[edge] * step)
            step2 = vel_b * (here + damp_s[edge] * fixed - q_h)
            base = side * 6
            halo_s[(base + s) * width_x : (base + s + 1) * width_x, :] = p1_h
            halo_s[(base + 2 + s) * width_x : (base + 3 + s) * width_x, :] = q_h
            halo_s[(base + 4 + s) * width_x : (base + 5 + s) * width_x, :] = pd_h * (
                plane_part(q_h, w_h) + step2
            )
            b1[s, edge] = fixed
            total = plane_part(change, w_e) - vel_in * change - step2
            b2[s, edge] = b2[s, edge] + change + pres_s[edge] * total
            b2[s, inner] = b2[s, inner] + pres_s[inner] * (vel_in * change)

    places = []
    for r in range(slots):
        z0 = jnp.clip(lax.div(corners[r], width_x * width_y), 0, depth - 2)
        x0 = lax.rem(lax.div(corners[r], width_y), width_x)
        start = jnp.minimum(lax.div(jnp.maximum(x0 - 1, 0), 8) * 8, width_x - WINDOW)
        places.append((z0, pl.multiple_of(start, 8)))
    _, row, _, col = split_cells(rows_in[8:9, :].astype(jnp.int32), width_x, width_y)
    live = rows_in[9:10, :]
    columns = pick_columns(col, width_y)
    slot_of = lax.div(lax.broadcasted_iota(jnp.int32, (1, LANES), 1), capsules)
    line = lax.broadcasted_iota(jnp.int32, (WINDOW, LANES), 0)
    found_rows = {}
    for r, (z0, start) in enumerate(places):
        own = jnp.where(slot_of == r, row, -1)
        for dz in range(2):
            first_row = (z0 + dz) * width_x + start
            found_rows[r, dz] = (line + first_row == own).astype(F32)
    index = {}
    for n, field in enumerate((b1, b2)):
        for r, (z0, start) in enumerate(places):
            for dz in range(2):
                damp = damp_s[z0 + dz, pl.ds(start, WINDOW), :]
                for s in range(shots):
                    k = index[n, r, dz, s] = len(index)
                    stack[k * WINDOW : (k + 1) * WINDOW, :] = (
                        damp * field[s, z0 + dz, pl.ds(start, WINDOW), :]
                    )
    found = pick(stack[...], columns, (1, 0))
    lines, lives, goals = [], [live] * 4, [blank] * 4
    for n in range(2):
        for s in range(shots):
            total = jnp.zeros((WINDOW, LANES), F32)
            for key, picked in found_rows.items():
                total += picked * rows_of(found, index[(n, *key, s)], WINDOW)
            lines.append(jnp.sum(total, axis=0, keepdims=True))
    columns_h, rows_h = [], []
    for side, (ref, _, _) in enumerate(sides):
        tiny = ref[8 * width_x : 8 * width_x + TINY, 0:LANES]
        near = tiny[4:5, :]
        picked = pick_rows(tiny[5:6, :].astype(jnp.int32), width_x).astype(F32)
        columns_h.append(pick_columns(tiny[6:7, :].astype(jnp.int32), width_y))
        rows_h.append(picked * near)
        found = pick(
            halo_s[side * 6 * width_x : (side + 1) * 6 * width_x, :], columns_h[side], (1, 0)
        )
        for s in range(shots):
            total = picked * (
                tiny[2:3, :] * rows_of(found, s, width_x)
                + tiny[3:4, :] * rows_of(found, 2 + s, width_x)
                + near * rows_of(found, 4 + s, width_x)
            )
            lines.append(tiny[s : s + 1, :] + jnp.sum(total, axis=0, keepdims=True))
            lives.append(tiny[7:8, :])
            goals.append(tiny[8 + s : 9 + s, :])
    goal_high, goal_low = halves(jnp.concatenate(goals, axis=0))
    high, low = code_high[:, 0:LANES], code_low[:, 0:LANES]
    known = rows_in[0:8, :] + (
        dot(goal_high, high, (1, 1)) + dot(goal_low, high, (1, 1)) + dot(goal_high, low, (1, 1))
    )
    got_high, got_low = halves(jnp.concatenate(lines, axis=0))
    both = (
        dot(got_high, code_high[...], (1, 0)) + dot(got_low, code_high[...], (1, 0))
        + dot(got_high, code_low[...], (1, 0))
    )
    lives = jnp.concatenate(lives, axis=0)
    coded[...] = both[:, 0:LANES] * lives
    source = both[:, LANES:] * lives - known

    parts = [None] * len(index)
    for (n, r, dz, s), k in index.items():
        line_of = n * shots + s
        parts[k] = found_rows[r, dz] * source[line_of : line_of + 1, :]
    spread[...] = pick(jnp.concatenate(parts, axis=0), columns, (1, 1))
    for side, (ref, edge, inner) in enumerate(sides):
        lines = [
            rows_h[side] * source[4 + 2 * side + s : 5 + 2 * side + s, :] for s in range(shots)
        ]
        placed = pick(jnp.concatenate(lines, axis=0), columns_h[side], (1, 1))
        vel_b = halo(ref, 6) if side == 0 else vel_s[last]
        sums = jnp.zeros((width_x, width_y), F32)
        sums_in = jnp.zeros((width_x, width_y), F32)
        for s in range(shots):
            w_h = halo(ref, 4 + s) + halo(ref, 7) * rows_of(placed, s, width_x)
            start = adj[s, edge]
            back = back_e[s, edges.index(edge)] - vel_b * (pd_s[edge] * start - w_h)
            sums += b2[s, edge] * start + b1[s, edge] * back
            sums_in += b2[s, inner] * adj[s, inner] + b1[s, inner] * back_e[s, edges.index(inner)]
        grad[edge] = -(mask[edge].astype(F32) * sums)
        grad[inner] = -(mask[inner].astype(F32) * sums_in)

    near_masks = edge_masks((WINDOW, width_y))
    for r, (z0, start) in enumerate(places):
        window = pl.ds(start, WINDOW)
        lower, upper = jnp.maximum(z0 - 1, 0), jnp.minimum(z0 + 2, last)
        vel_low = jnp.where(
            z0 > 0, vel_s[lower, window, :], below[pl.ds(6 * width_x + start, WINDOW), :]
        )
        vel = [vel_s[z0 + dz, window, :] for dz in range(2)]
        sums = [jnp.zeros((WINDOW, width_y), F32) for _ in range(4)]
        for s in range(shots):
            now, before = [
                [rows_of(spread, index[n, r, dz, s], WINDOW) for dz in range(2)] for n in (1, 0)
            ]
            w = [pd_s[z0 + dz, window, :] * now[dz] for dz in range(2)]
            between = vel[0] * (w[1] - w[0])
            outer = [vel_low * w[0], vel[1] * w[1]]
            for dz in range(2):
                total = window_part(w[dz], vel[dz], near_masks) - outer[dz]
                total += between if dz == 0 else -between
                total += damp_s[z0 + dz, window, :] * now[dz] + before[dz]
                sums[1 + dz] += (
                    b2[s, z0 + dz, window, :] * now[dz] + b1[s, z0 + dz, window, :] * total
                )
            sums[0] += b1[s, lower, window, :] * outer[0]
            sums[3] += b1[s, upper, window, :] * outer[1]
        inside = (jnp.where(z0 > 0, 1.0, 0.0), 1.0, 1.0, jnp.where(z0 + 2 < depth, 1.0, 0.0))
        for z, total, factor in zip((lower, z0, z0 + 1, upper), sums, inside):
            wall = mask[z, window, :].astype(F32)
            grad[z, window, :] = grad[z, window, :] - factor * (wall * total)
    half = depth // 2
    mine = core[0] * half
    for z in range(half):
        keep[z] = grad[mine + z]
        send[z] = grad[half - mine + z]


def body(
    pressure_init, adjoint_init, density, speed, admittance, bound_mask,
    rec_cells, rec_live, encoder, target,
):
    shots, depth, width_x, width_y = pressure_init.shape
    slots, capsules = rec_cells.shape
    steps, channels = target.shape[2:]
    slabs, peers = lax.axis_size("slab"), lax.axis_size("shot")
    field = (shots, depth, width_x, width_y)
    slab = (depth, width_x, width_y)
    half = (depth // 2, width_x, width_y)
    message = (8 * width_x + TINY, width_y)

    def ins(count, scalars=0, far=0):
        kinds = [pltpu.SMEM] * scalars + [VMEM] * (count - scalars - far) + [pltpu.HBM] * far
        return [pl.BlockSpec(memory_space=kind) for kind in kinds]

    def outs(*shapes):
        return [
            shape if isinstance(shape, jax.ShapeDtypeStruct) else jax.ShapeDtypeStruct(shape, F32)
            for shape in shapes
        ]

    params = pltpu.CompilerParams(vmem_limit_bytes=VMEM_LIMIT)
    up, down = pl.pallas_call(
        edge_kernel,
        in_specs=ins(9, 1, 6),
        out_specs=ins(2),
        out_shape=outs(message, message),
        scratch_shapes=[
            VMEM(field, F32), VMEM((shots, 2, width_x, width_y), F32),
            VMEM(slab, F32), VMEM(slab, F32), VMEM(slab, F32), VMEM(slab, jnp.int32),
            VMEM(slab, F32), VMEM(slab, F32), VMEM((14 * width_x, width_y), F32),
            pltpu.SemaphoreType.DMA((2, 6)),
        ],
        compiler_params=pltpu.CompilerParams(vmem_limit_bytes=EDGE_LIMIT),
        name="edge",
    )(
        rec_live, rec_cells, target, pressure_init, adjoint_init, density, speed, admittance,
        bound_mask,
    )

    below = lax.ppermute(up, "slab", [(i, i + 1) for i in range(slabs - 1)])
    above = lax.ppermute(down, "slab", [(i + 1, i) for i in range(slabs - 1)])

    table = jax.ShapeDtypeStruct((LANES, 2 * LANES), jnp.bfloat16)
    b1, b2, vel, pres, damp, pd, back, grad, rows, high, low = pl.pallas_call(
        middle_kernel,
        in_specs=ins(10, 1),
        out_specs=ins(11),
        out_shape=outs(
            field, field, slab, slab, slab, slab, (shots, 4, width_x, width_y), slab,
            (16, LANES), table, table,
        ),
        scratch_shapes=[VMEM(field, F32), VMEM(field, F32)],
        compiler_params=params,
        cost_estimate=pl.CostEstimate(flops=20_000_000, bytes_accessed=6_000_000, transcendentals=0),
        name="middle",
    )(
        rec_live, rec_cells, target, encoder, pressure_init, adjoint_init, density, speed,
        admittance, bound_mask,
    )

    core = lax.rem(lax.axis_index("shot"), 2)
    corners = jnp.min(rec_cells, axis=1)
    windows = steps * slots * 2 * shots * WINDOW
    keep, send, coded, _, _, _ = pl.pallas_call(
        functools.partial(last_kernel, capsules),
        in_specs=ins(18, 2),
        out_specs=ins(6),
        out_shape=outs(half, half, (8, LANES), field, field, slab),
        scratch_shapes=[
            VMEM((12 * width_x, width_y), F32), VMEM((windows, width_y), F32),
            VMEM((windows, width_y), F32),
        ],
        input_output_aliases={15: 3, 16: 4, 17: 5},
        compiler_params=params,
        name="last",
    )(
        core[None], corners, below, above, pressure_init, adjoint_init, bound_mask, vel, pres,
        damp, pd, back, rows, high, low, b1, b2, grad,
    )

    pairs = [(i, i ^ 1) for i in range(peers)]
    groups = [list(range(c, peers, 2)) for c in range(2)]
    total = keep + lax.ppermute(send, "shot", pairs)
    copies = jnp.broadcast_to(total, (peers // 2, *half))
    total = lax.all_to_all(
        copies, "shot", split_axis=0, concat_axis=0, tiled=True, axis_index_groups=groups
    ).sum(axis=0)
    other = lax.ppermute(total, "shot", pairs)
    gradient = jnp.where(
        core == 0, jnp.concatenate([total, other], 0), jnp.concatenate([other, total], 0)
    )
    signals = coded[: steps * shots, : slots * capsules]
    signals = signals.reshape(steps, shots, slots, capsules)[..., :channels]
    return jnp.transpose(signals, (2, 1, 0, 3)), gradient


def solution(mesh):
    placed = (
        P("shot", "slab", None, None), P("shot", "slab", None, None),
        P("slab", None, None), P("slab", None, None), P("slab", None, None), P("slab", None, None),
        P("slab", None), P("slab"), P(), P("slab", "shot", None, None),
    )
    return jax.shard_map(
        body, mesh=mesh, in_specs=placed,
        out_specs=(P("slab", "shot", None, None), P("slab", None, None)),
        check_vma=False,
    )
```

```python
import functools

import jax
import jax.numpy as jnp
from jax import lax
from jax.experimental import pallas as pl
from jax.experimental.pallas import tpu as pltpu
from jax.sharding import PartitionSpec as P

LANES = 128
FAR = float(1 << 20)
WINDOW = 16
VMEM_LIMIT = 20 << 20
TINY = 16
VMEM = pltpu.VMEM
F32 = jnp.float32


def dot(a, b, contract):
    return lax.dot_general(
        a, b, ((contract[:1], contract[1:]), ((), ())), preferred_element_type=F32
    )


def halves(a):
    high = a.astype(jnp.bfloat16)
    return high, (a - high.astype(F32)).astype(jnp.bfloat16)


def pick(a, onehot, contract):
    high, low = halves(a)
    return dot(high, onehot, contract) + dot(low, onehot, contract)


def edge_masks(shape):
    row = lax.broadcasted_iota(jnp.int32, shape, 0)
    col = lax.broadcasted_iota(jnp.int32, shape, 1)
    return row > 0, row < shape[0] - 1, col > 0, col < shape[1] - 1


def plane_weights(vel, masks):
    low_x, high_x, low_y, high_y = masks
    xp = jnp.where(high_x, vel, 0.0)
    xm = jnp.where(low_x, pltpu.roll(vel, 1, 0), 0.0)
    yp = jnp.where(high_y, vel, 0.0)
    ym = jnp.where(low_y, pltpu.roll(vel, 1, 1), 0.0)
    return xp, xm, yp, ym, 2.0 * vel + xm + ym


def plane_part(u, weights):
    xp, xm, yp, ym, centre = weights
    rows, cols = u.shape
    return (
        xp * pltpu.roll(u, rows - 1, 0) + xm * pltpu.roll(u, 1, 0)
        + yp * pltpu.roll(u, cols - 1, 1) + ym * pltpu.roll(u, 1, 1)
        - centre * u
    )


def pick_columns(cols, width):
    return (lax.broadcasted_iota(jnp.int32, (width, cols.shape[1]), 0) == cols).astype(jnp.bfloat16)


def pick_rows(rows, count):
    return (lax.broadcasted_iota(jnp.int32, (count, rows.shape[1]), 0) == rows).astype(F32)


def split_cells(cells, width_x, width_y):
    plane = lax.div(cells, width_x * width_y)
    row = lax.div(cells, width_y)
    return plane, row, row - plane * width_x, cells - row * width_y


def in_lanes(pieces, width, fill=0.0):
    parts = []
    for piece in pieces:
        parts.append(piece)
        if piece.shape[1] < width:
            parts.append(jnp.full((1, width - piece.shape[1]), fill, piece.dtype))
    used = width * len(pieces)
    parts.append(jnp.full((1, LANES - used), fill, pieces[0].dtype))
    return jnp.concatenate(parts, axis=1)


def live_lanes(rec_live, slots, capsules):
    slot = lax.div(lax.broadcasted_iota(jnp.int32, (1, LANES), 1), capsules)
    row = jnp.zeros((1, LANES), F32)
    for r in range(slots):
        row = jnp.where(slot == r, rec_live[r].astype(F32), row)
    return row


def cell_lanes(rec_cells):
    slots, capsules = rec_cells.shape
    return in_lanes([rec_cells[r : r + 1, :] for r in range(slots)], capsules, int(FAR))


def goal_lanes(target, s, n, capsules):
    return in_lanes([target[r, s, n : n + 1, :] for r in range(target.shape[0])], capsules)


def edge_kernel(
    live_h, cells_h, target_h, p0_h, adj_h, density_h, speed_h, admittance_h, mask_h,
    up, down, p0, adj, density, speed, admittance, mask, vel_s, pd_s, stack,
    rec_live, rec_cells, target, sems, small_sems,
):
    shots, depth, width_x, width_y = p0.shape
    slots, capsules = rec_cells.shape
    half = depth // 2
    last = depth - 1
    copies = []
    for side in range(2):
        some = pl.ds(side * half, half)
        pairs = [(h.at[some], v.at[some]) for h, v in (
            (density_h, density), (speed_h, speed), (admittance_h, admittance), (mask_h, mask))]
        pairs.insert(0, (p0_h.at[:, some], p0.at[:, some]))
        pairs.append((adj_h.at[:, some], adj.at[:, some]))
        copies.append([
            pltpu.make_async_copy(a, b, sems.at[side, k]) for k, (a, b) in enumerate(pairs)
        ])
    for copy in copies[0] + copies[1]:
        copy.start()
    smalls = [
        pltpu.make_async_copy(a, b, small_sems.at[k])
        for k, (a, b) in enumerate(((live_h, rec_live), (cells_h, rec_cells), (target_h, target)))
    ]
    for copy in smalls:
        copy.start()
    masks = edge_masks((width_x, width_y))
    for copy in smalls:
        copy.wait()
    plane, _, row_x, col = split_cells(cell_lanes(rec_cells), width_x, width_y)
    live = live_lanes(rec_live, slots, capsules)
    columns = pick_columns(col, width_y)
    rows = pick_rows(row_x, width_x)
    for side in range(2):
        for copy in copies[side]:
            copy.wait()
        if side == 0:
            out, planes, lowest, inward = down, (0, 1, 2), 0, 1
        else:
            out, planes, lowest, inward = up, (last, last - 1, last - 2), half, -1
        near, far, third = planes
        span = range(lowest, lowest + half)
        weights, pres, damp = {}, {}, {}
        for z in span:
            vel_s[z] = 0.5 / density[z]
        for z in planes:
            spd = speed[z]
            pres[z] = 0.5 * density[z] * spd * spd
            damp[z] = 1.0 - admittance[z] * mask[z].astype(F32)
            weights[z] = plane_weights(vel_s[z], masks)
        for z in (near, far):
            pd_s[z] = pres[z] * damp[z]
        wall_low = min(near, far)
        base = side * 7 * width_x

        def put(k, value):
            stack[base + k * width_x : base + (k + 1) * width_x, :] = value

        for s in range(shots):
            first = {}
            for z in planes:
                here = p0[s, z]
                total = plane_part(here, weights[z])
                if z + 1 in span:
                    total += vel_s[z] * (p0[s, z + 1] - here)
                if z - 1 in span:
                    total -= vel_s[z - 1] * (here - p0[s, z - 1])
                first[z] = damp[z] * (here + pres[z] * total)
            out[s * width_x : (s + 1) * width_x, :] = p0[s, near]
            out[(2 + s) * width_x : (3 + s) * width_x, :] = first[near]
            out[(4 + s) * width_x : (5 + s) * width_x, :] = pd_s[near] * adj[s, near]
            q_far = p0[s, far] + first[far]
            q_third = p0[s, third] + first[third]
            beyond = vel_s[min(far, third)]
            total = plane_part(q_far, weights[far]) + beyond * (q_third - q_far)
            total -= vel_s[wall_low] * q_far
            put(s, pd_s[near] * vel_s[wall_low] * q_far)
            put(4 + s, damp[far] * first[far] + pd_s[far] * total)
        out[6 * width_x : 7 * width_x, :] = vel_s[near]
        out[7 * width_x : 8 * width_x, :] = pd_s[near]
        put(2, damp[near])
        put(3, pd_s[near] * vel_s[wall_low])
        put(6, pd_s[far] * vel_s[wall_low])
        found = pick(stack[base : base + 7 * width_x, :], columns, (1, 0))
        is_near = (plane == near).astype(F32)
        is_far = (plane == far).astype(F32)

        def got(k):
            return jnp.sum(found[k * width_x : (k + 1) * width_x, :] * rows, axis=0, keepdims=True)

        tiny = [is_near * got(s) + is_far * got(4 + s) for s in range(shots)]
        tiny += [
            is_near * got(2), is_far * got(6) - is_near * got(3), is_near,
            row_x.astype(F32), col.astype(F32), live,
        ]
        tiny += [live * goal_lanes(target, s, 1, capsules) for s in range(shots)]
        tiny.append(jnp.zeros((TINY - len(tiny), LANES), F32))
        start = 8 * width_x
        out[start : start + TINY, :] = jnp.zeros((TINY, width_y), F32)
        out[start : start + TINY, 0:LANES] = jnp.concatenate(tiny, axis=0)


def middle_kernel(
    rec_live, rec_cells, target, encoder, p0, adj, density, speed, admittance, mask,
    b1, b2, vel_s, pres_s, damp_s, pd_s, back_e, grad, rows_out, code_high, code_low,
    q_s, w_s,
):
    shots, depth, width_x, width_y = p0.shape
    slots, capsules = rec_cells.shape
    steps, channels = target.shape[2:]
    masks = edge_masks((width_x, width_y))
    last = depth - 1
    edges = (0, 1, last - 1, last)
    for z in range(depth):
        dens = density[z]
        spd = speed[z]
        vel = 0.5 / dens
        pres = 0.5 * dens * spd * spd
        damp = 1.0 - admittance[z] * mask[z].astype(F32)
        vel_s[z] = vel
        pres_s[z] = pres
        damp_s[z] = damp
        pd_s[z] = pres * damp
        w = plane_weights(vel, masks)
        for s in range(shots):
            here = p0[s, z]
            total = plane_part(here, w)
            if z < last:
                total += vel * (p0[s, z + 1] - here)
            if z > 0:
                total -= vel_s[z - 1] * (here - p0[s, z - 1])
            value = here + pres * total
            b1[s, z] = value
            q_s[s, z] = here + damp * value
            w_s[s, z] = pd_s[z] * adj[s, z]
    for z in range(depth):
        vel = vel_s[z]
        w = plane_weights(vel, masks)
        sums = jnp.zeros((width_x, width_y), F32)
        for s in range(shots):
            here, weighted = q_s[s, z], w_s[s, z]
            total = plane_part(here, w)
            back = plane_part(weighted, w)
            if z < last:
                total += vel * (q_s[s, z + 1] - here)
                back += vel * (w_s[s, z + 1] - weighted)
            if z > 0:
                total -= vel_s[z - 1] * (here - q_s[s, z - 1])
                back -= vel_s[z - 1] * (weighted - w_s[s, z - 1])
            value = damp_s[z] * b1[s, z] + pres_s[z] * total
            b2[s, z] = value
            back += damp_s[z] * adj[s, z]
            if z in edges:
                back_e[s, edges.index(z)] = back
            else:
                sums += value * adj[s, z] + b1[s, z] * back
        grad[z] = -(mask[z].astype(F32) * sums)
    lane = lax.broadcasted_iota(jnp.int32, (LANES, LANES), 1)
    line = lax.broadcasted_iota(jnp.int32, (LANES, LANES), 0)
    same = (lax.div(lane, capsules) == lax.div(line, capsules)) & (line < slots * capsules)
    code = jnp.concatenate([encoder[...], jnp.zeros((capsules, capsules - channels), F32)], axis=1)
    code = jnp.concatenate([code] * (LANES // capsules), axis=1)
    code = jnp.where(same, jnp.concatenate([code] * (LANES // capsules), axis=0), 0.0)
    square = lax.dot_general(
        code, code, (((1,), (1,)), ((), ())),
        precision=lax.Precision.HIGHEST, preferred_element_type=F32,
    )
    both = jnp.concatenate([code, square], axis=1)
    code_high[...], code_low[...] = halves(both)
    live = live_lanes(rec_live, slots, capsules)
    goal = [live * goal_lanes(target, s, n, capsules) for n in range(steps) for s in range(shots)]
    goal = jnp.concatenate(goal + [jnp.zeros((8 - len(goal), LANES), F32)], axis=0)
    rows_out[0:8, :] = lax.dot_general(
        goal, code, (((1,), (1,)), ((), ())),
        precision=lax.Precision.HIGHEST, preferred_element_type=F32,
    )
    rows_out[8:16, :] = jnp.concatenate(
        [cell_lanes(rec_cells).astype(F32), live, jnp.zeros((6, LANES), F32)], axis=0
    )


def window_part(u, vel, masks):
    low_x, high_x, low_y, high_y = masks
    rows, cols = u.shape
    flow_x = vel * (jnp.where(high_x, pltpu.roll(u, rows - 1, 0), 0.0) - u)
    flow_y = vel * (jnp.where(high_y, pltpu.roll(u, cols - 1, 1), 0.0) - u)
    fall_x = flow_x - jnp.where(low_x, pltpu.roll(flow_x, 1, 0), 0.0)
    return fall_x + flow_y - jnp.where(low_y, pltpu.roll(flow_y, 1, 1), 0.0)


def last_kernel(
    capsules, core, corners, below, above, p0, adj, mask, vel_s, pres_s, damp_s, pd_s, back_e,
    rows_in, code_high, code_low, b1_in, b2_in, grad_in,
    keep, send, coded, b1, b2, grad,
    halo_s, stack, spread,
):
    shots, depth, width_x, width_y = p0.shape
    slots = corners.shape[0]
    masks = edge_masks((width_x, width_y))
    last = depth - 1
    edges = (0, 1, last - 1, last)
    sides = ((below, 0, 1), (above, last, last - 1))
    blank = jnp.zeros((1, LANES), F32)

    def halo(ref, k):
        return ref[k * width_x : (k + 1) * width_x, :]

    def rows_of(array, k, count):
        return array[k * count : (k + 1) * count, :]

    for side, (ref, edge, inner) in enumerate(sides):
        vel_h, pd_h = halo(ref, 6), halo(ref, 7)
        vel_b = vel_h if side == 0 else vel_s[last]
        vel_in = vel_s[min(edge, inner)]
        w_h = plane_weights(vel_h, masks)
        w_e = plane_weights(vel_s[edge], masks)
        for s in range(shots):
            here, out = p0[s, edge], halo(ref, s)
            step = vel_b * (here - out)
            p1_h = halo(ref, 2 + s) + pd_h * step
            q_h = out + p1_h
            fixed = b1[s, edge] - pres_s[edge] * step
            change = -(pd_s[edge] * step)
            step2 = vel_b * (here + damp_s[edge] * fixed - q_h)
            base = side * 6
            halo_s[(base + s) * width_x : (base + s + 1) * width_x, :] = p1_h
            halo_s[(base + 2 + s) * width_x : (base + 3 + s) * width_x, :] = q_h
            halo_s[(base + 4 + s) * width_x : (base + 5 + s) * width_x, :] = pd_h * (
                plane_part(q_h, w_h) + step2
            )
            b1[s, edge] = fixed
            total = plane_part(change, w_e) - vel_in * change - step2
            b2[s, edge] = b2[s, edge] + change + pres_s[edge] * total
            b2[s, inner] = b2[s, inner] + pres_s[inner] * (vel_in * change)

    places = []
    for r in range(slots):
        z0 = jnp.clip(lax.div(corners[r], width_x * width_y), 0, depth - 2)
        x0 = lax.rem(lax.div(corners[r], width_y), width_x)
        start = jnp.minimum(lax.div(jnp.maximum(x0 - 1, 0), 8) * 8, width_x - WINDOW)
        places.append((z0, pl.multiple_of(start, 8)))
    _, row, _, col = split_cells(rows_in[8:9, :].astype(jnp.int32), width_x, width_y)
    live = rows_in[9:10, :]
    columns = pick_columns(col, width_y)
    slot_of = lax.div(lax.broadcasted_iota(jnp.int32, (1, LANES), 1), capsules)
    line = lax.broadcasted_iota(jnp.int32, (WINDOW, LANES), 0)
    found_rows = {}
    for r, (z0, start) in enumerate(places):
        own = jnp.where(slot_of == r, row, -1)
        for dz in range(2):
            first_row = (z0 + dz) * width_x + start
            found_rows[r, dz] = (line + first_row == own).astype(F32)
    index = {}
    for n, field in enumerate((b1, b2)):
        for r, (z0, start) in enumerate(places):
            for dz in range(2):
                damp = damp_s[z0 + dz, pl.ds(start, WINDOW), :]
                for s in range(shots):
                    k = index[n, r, dz, s] = len(index)
                    stack[k * WINDOW : (k + 1) * WINDOW, :] = (
                        damp * field[s, z0 + dz, pl.ds(start, WINDOW), :]
                    )
    found = pick(stack[...], columns, (1, 0))
    lines, lives, goals = [], [live] * 4, [blank] * 4
    for n in range(2):
        for s in range(shots):
            total = jnp.zeros((WINDOW, LANES), F32)
            for key, picked in found_rows.items():
                total += picked * rows_of(found, index[(n, *key, s)], WINDOW)
            lines.append(jnp.sum(total, axis=0, keepdims=True))
    columns_h, rows_h = [], []
    for side, (ref, _, _) in enumerate(sides):
        tiny = ref[8 * width_x : 8 * width_x + TINY, 0:LANES]
        near = tiny[4:5, :]
        picked = pick_rows(tiny[5:6, :].astype(jnp.int32), width_x).astype(F32)
        columns_h.append(pick_columns(tiny[6:7, :].astype(jnp.int32), width_y))
        rows_h.append(picked * near)
        found = pick(
            halo_s[side * 6 * width_x : (side + 1) * 6 * width_x, :], columns_h[side], (1, 0)
        )
        for s in range(shots):
            total = picked * (
                tiny[2:3, :] * rows_of(found, s, width_x)
                + tiny[3:4, :] * rows_of(found, 2 + s, width_x)
                + near * rows_of(found, 4 + s, width_x)
            )
            lines.append(tiny[s : s + 1, :] + jnp.sum(total, axis=0, keepdims=True))
            lives.append(tiny[7:8, :])
            goals.append(tiny[8 + s : 9 + s, :])
    goal_high, goal_low = halves(jnp.concatenate(goals, axis=0))
    high, low = code_high[:, 0:LANES], code_low[:, 0:LANES]
    known = rows_in[0:8, :] + (
        dot(goal_high, high, (1, 1)) + dot(goal_low, high, (1, 1)) + dot(goal_high, low, (1, 1))
    )
    got_high, got_low = halves(jnp.concatenate(lines, axis=0))
    both = (
        dot(got_high, code_high[...], (1, 0)) + dot(got_low, code_high[...], (1, 0))
        + dot(got_high, code_low[...], (1, 0))
    )
    lives = jnp.concatenate(lives, axis=0)
    coded[...] = both[:, 0:LANES] * lives
    source = both[:, LANES:] * lives - known

    parts = [None] * len(index)
    for (n, r, dz, s), k in index.items():
        line_of = n * shots + s
        parts[k] = found_rows[r, dz] * source[line_of : line_of + 1, :]
    spread[...] = pick(jnp.concatenate(parts, axis=0), columns, (1, 1))
    for side, (ref, edge, inner) in enumerate(sides):
        lines = [
            rows_h[side] * source[4 + 2 * side + s : 5 + 2 * side + s, :] for s in range(shots)
        ]
        placed = pick(jnp.concatenate(lines, axis=0), columns_h[side], (1, 1))
        vel_b = halo(ref, 6) if side == 0 else vel_s[last]
        sums = jnp.zeros((width_x, width_y), F32)
        sums_in = jnp.zeros((width_x, width_y), F32)
        for s in range(shots):
            w_h = halo(ref, 4 + s) + halo(ref, 7) * rows_of(placed, s, width_x)
            start = adj[s, edge]
            back = back_e[s, edges.index(edge)] - vel_b * (pd_s[edge] * start - w_h)
            sums += b2[s, edge] * start + b1[s, edge] * back
            sums_in += b2[s, inner] * adj[s, inner] + b1[s, inner] * back_e[s, edges.index(inner)]
        grad[edge] = -(mask[edge].astype(F32) * sums)
        grad[inner] = -(mask[inner].astype(F32) * sums_in)

    near_masks = edge_masks((WINDOW, width_y))
    for r, (z0, start) in enumerate(places):
        window = pl.ds(start, WINDOW)
        lower, upper = jnp.maximum(z0 - 1, 0), jnp.minimum(z0 + 2, last)
        vel_low = jnp.where(
            z0 > 0, vel_s[lower, window, :], below[pl.ds(6 * width_x + start, WINDOW), :]
        )
        vel = [vel_s[z0 + dz, window, :] for dz in range(2)]
        sums = [jnp.zeros((WINDOW, width_y), F32) for _ in range(4)]
        for s in range(shots):
            now, before = [
                [rows_of(spread, index[n, r, dz, s], WINDOW) for dz in range(2)] for n in (1, 0)
            ]
            w = [pd_s[z0 + dz, window, :] * now[dz] for dz in range(2)]
            between = vel[0] * (w[1] - w[0])
            outer = [vel_low * w[0], vel[1] * w[1]]
            for dz in range(2):
                total = window_part(w[dz], vel[dz], near_masks) - outer[dz]
                total += between if dz == 0 else -between
                total += damp_s[z0 + dz, window, :] * now[dz] + before[dz]
                sums[1 + dz] += (
                    b2[s, z0 + dz, window, :] * now[dz] + b1[s, z0 + dz, window, :] * total
                )
            sums[0] += b1[s, lower, window, :] * outer[0]
            sums[3] += b1[s, upper, window, :] * outer[1]
        inside = (jnp.where(z0 > 0, 1.0, 0.0), 1.0, 1.0, jnp.where(z0 + 2 < depth, 1.0, 0.0))
        for z, total, factor in zip((lower, z0, z0 + 1, upper), sums, inside):
            wall = mask[z, window, :].astype(F32)
            grad[z, window, :] = grad[z, window, :] - factor * (wall * total)
    half = depth // 2
    mine = core[0] * half
    for z in range(half):
        keep[z] = grad[mine + z]
        send[z] = grad[half - mine + z]


def body(
    pressure_init, adjoint_init, density, speed, admittance, bound_mask,
    rec_cells, rec_live, encoder, target,
):
    shots, depth, width_x, width_y = pressure_init.shape
    slots, capsules = rec_cells.shape
    steps, channels = target.shape[2:]
    slabs, peers = lax.axis_size("slab"), lax.axis_size("shot")
    field = (shots, depth, width_x, width_y)
    slab = (depth, width_x, width_y)
    half = (depth // 2, width_x, width_y)
    message = (8 * width_x + TINY, width_y)

    def ins(count, scalars=0, far=0):
        kinds = [pltpu.SMEM] * scalars + [VMEM] * (count - scalars - far) + [pltpu.HBM] * far
        return [pl.BlockSpec(memory_space=kind) for kind in kinds]

    def outs(*shapes):
        return [
            shape if isinstance(shape, jax.ShapeDtypeStruct) else jax.ShapeDtypeStruct(shape, F32)
            for shape in shapes
        ]

    params = pltpu.CompilerParams(vmem_limit_bytes=VMEM_LIMIT)
    up, down, p0, adj, density, speed, admittance, bound_mask = pl.pallas_call(
        edge_kernel,
        in_specs=ins(9, 0, 9),
        out_specs=ins(8),
        out_shape=[
            VMEM(message, F32), VMEM(message, F32), VMEM(field, F32), VMEM(field, F32),
            VMEM(slab, F32), VMEM(slab, F32), VMEM(slab, F32), VMEM(slab, jnp.int32),
        ],
        scratch_shapes=[
            VMEM(slab, F32), VMEM(slab, F32), VMEM((14 * width_x, width_y), F32),
            pltpu.SMEM(rec_live.shape, jnp.int32), VMEM(rec_cells.shape, jnp.int32),
            VMEM(target.shape, F32),
            pltpu.SemaphoreType.DMA((2, 6)), pltpu.SemaphoreType.DMA((3,)),
        ],
        compiler_params=params,
        name="edge",
    )(
        *[
            pltpu.with_memory_space_constraint(array, pltpu.HBM)
            for array in (
                rec_live, rec_cells, target,
                pressure_init, adjoint_init, density, speed, admittance, bound_mask,
            )
        ],
    )

    even = lax.rem(lax.axis_index("slab"), 2) == 0

    def exchange(value, first):
        pairs = [(i, i + 1) for i in range(first, slabs - 1, 2)]
        return lax.ppermute(value, "slab", pairs + [(b, a) for a, b in pairs])

    inner = exchange(jnp.where(even, up, down), 0)
    outer = exchange(jnp.where(even, down, up), 1)
    below, above = jnp.where(even, outer, inner), jnp.where(even, inner, outer)

    table = jax.ShapeDtypeStruct((LANES, 2 * LANES), jnp.bfloat16)
    b1, b2, vel, pres, damp, pd, back, grad, rows, high, low = pl.pallas_call(
        middle_kernel,
        in_specs=ins(10, 1),
        out_specs=ins(11),
        out_shape=outs(
            field, field, slab, slab, slab, slab, (shots, 4, width_x, width_y), slab,
            (16, LANES), table, table,
        ),
        scratch_shapes=[VMEM(field, F32), VMEM(field, F32)],
        compiler_params=params,
        cost_estimate=pl.CostEstimate(flops=20_000_000, bytes_accessed=6_000_000, transcendentals=0),
        name="middle",
    )(
        rec_live, rec_cells, target, encoder, p0, adj, density, speed, admittance, bound_mask,
    )

    core = lax.rem(lax.axis_index("shot"), 2)
    corners = jnp.min(rec_cells, axis=1)
    windows = steps * slots * 2 * shots * WINDOW
    keep, send, coded, _, _, _ = pl.pallas_call(
        functools.partial(last_kernel, capsules),
        in_specs=ins(18, 2),
        out_specs=ins(6),
        out_shape=outs(half, half, (8, LANES), field, field, slab),
        scratch_shapes=[
            VMEM((12 * width_x, width_y), F32), VMEM((windows, width_y), F32),
            VMEM((windows, width_y), F32),
        ],
        input_output_aliases={15: 3, 16: 4, 17: 5},
        compiler_params=params,
        name="last",
    )(
        core[None], corners, below, above, p0, adj, bound_mask, vel, pres, damp, pd, back, rows, high, low, b1, b2, grad,
    )

    pairs = [(i, i ^ 1) for i in range(peers)]
    groups = [list(range(c, peers, 2)) for c in range(2)]
    total = keep + lax.ppermute(send, "shot", pairs)
    copies = jnp.broadcast_to(total, (peers // 2, *half))
    total = lax.all_to_all(
        copies, "shot", split_axis=0, concat_axis=0, tiled=True, axis_index_groups=groups
    ).sum(axis=0)
    total, coded, later = lax.optimization_barrier((total, coded, core))
    other = lax.ppermute(total, "shot", pairs)
    gradient = jnp.where(
        later == 0, jnp.concatenate([total, other], 0), jnp.concatenate([other, total], 0)
    )
    signals = coded[: steps * shots, : slots * capsules]
    signals = signals.reshape(steps, shots, slots, capsules)[..., :channels]
    return jnp.transpose(signals, (2, 1, 0, 3)), gradient


def solution(mesh):
    placed = (
        P("shot", "slab", None, None), P("shot", "slab", None, None),
        P("slab", None, None), P("slab", None, None), P("slab", None, None), P("slab", None, None),
        P("slab", None), P("slab"), P(), P("slab", "shot", None, None),
    )
    return jax.shard_map(
        body, mesh=mesh, in_specs=placed,
        out_specs=(P("slab", "shot", None, None), P("slab", None, None)),
        check_vma=False,
    )
```

```python
import functools

import jax
import jax.numpy as jnp
from jax import lax
from jax.experimental import pallas as pl
from jax.experimental.pallas import tpu as pltpu
from jax.sharding import PartitionSpec as P


LANES = 128
FAR = float(1 << 20)
WINDOW = 16
VMEM_LIMIT = 20 << 20
TINY = 16
VMEM = pltpu.VMEM
F32 = jnp.float32


def dot(a, b, contract):
    return lax.dot_general(
        a, b, ((contract[:1], contract[1:]), ((), ())), preferred_element_type=F32
    )


def halves(a):
    high = a.astype(jnp.bfloat16)
    return high, (a - high.astype(F32)).astype(jnp.bfloat16)


def pick(a, onehot, contract):
    high, low = halves(a)
    return dot(high, onehot, contract) + dot(low, onehot, contract)


def edge_masks(shape):
    row = lax.broadcasted_iota(jnp.int32, shape, 0)
    col = lax.broadcasted_iota(jnp.int32, shape, 1)
    return row > 0, row < shape[0] - 1, col > 0, col < shape[1] - 1


def plane_weights(vel, masks):
    low_x, high_x, low_y, high_y = masks
    xp = jnp.where(high_x, vel, 0.0)
    xm = jnp.where(low_x, pltpu.roll(vel, 1, 0), 0.0)
    yp = jnp.where(high_y, vel, 0.0)
    ym = jnp.where(low_y, pltpu.roll(vel, 1, 1), 0.0)
    return xp, xm, yp, ym, 2.0 * vel + xm + ym


def plane_part(u, weights):
    xp, xm, yp, ym, centre = weights
    rows, cols = u.shape
    return (
        xp * pltpu.roll(u, rows - 1, 0) + xm * pltpu.roll(u, 1, 0)
        + yp * pltpu.roll(u, cols - 1, 1) + ym * pltpu.roll(u, 1, 1)
        - centre * u
    )


def pick_columns(cols, width):
    return (lax.broadcasted_iota(jnp.int32, (width, cols.shape[1]), 0) == cols).astype(jnp.bfloat16)


def pick_rows(rows, count):
    return (lax.broadcasted_iota(jnp.int32, (count, rows.shape[1]), 0) == rows).astype(F32)


def split_cells(cells, width_x, width_y):
    plane = lax.div(cells, width_x * width_y)
    row = lax.div(cells, width_y)
    return plane, row, row - plane * width_x, cells - row * width_y


def in_lanes(pieces, width, fill=0.0):
    parts = []
    for piece in pieces:
        parts.append(piece)
        if piece.shape[1] < width:
            parts.append(jnp.full((1, width - piece.shape[1]), fill, piece.dtype))
    used = width * len(pieces)
    parts.append(jnp.full((1, LANES - used), fill, pieces[0].dtype))
    return jnp.concatenate(parts, axis=1)


def live_lanes(rec_live, slots, capsules):
    slot = lax.div(lax.broadcasted_iota(jnp.int32, (1, LANES), 1), capsules)
    row = jnp.zeros((1, LANES), F32)
    for r in range(slots):
        row = jnp.where(slot == r, rec_live[r].astype(F32), row)
    return row


def cell_lanes(rec_cells):
    slots, capsules = rec_cells.shape
    return in_lanes([rec_cells[r : r + 1, :] for r in range(slots)], capsules, int(FAR))


def goal_lanes(target, s, n, capsules):
    return in_lanes([target[r, s, n : n + 1, :] for r in range(target.shape[0])], capsules)


def edge_kernel(
    live_h, cells_h, target_h, p0_h, adj_h, density_h, speed_h, admittance_h, mask_h,
    up, down, p0, adj, density, speed, admittance, mask, vel_s, pd_s, stack,
    rec_live, rec_cells, target, sems, small_sems,
):
    shots, depth, width_x, width_y = p0.shape
    slots, capsules = rec_cells.shape
    half = depth // 2
    last = depth - 1
    copies = []
    for side in range(2):
        some = pl.ds(side * half, half)
        pairs = [(h.at[some], v.at[some]) for h, v in (
            (density_h, density), (speed_h, speed), (admittance_h, admittance), (mask_h, mask))]
        pairs.insert(0, (p0_h.at[:, some], p0.at[:, some]))
        face = pl.ds(side * last, 1)
        pairs.append((adj_h.at[:, face], adj.at[:, face]))
        copies.append([
            pltpu.make_async_copy(a, b, sems.at[side, k]) for k, (a, b) in enumerate(pairs)
        ])
    inside = pl.ds(1, depth - 2)
    rest = pltpu.make_async_copy(adj_h.at[:, inside], adj.at[:, inside], small_sems.at[3])
    smalls = [
        pltpu.make_async_copy(a, b, small_sems.at[k])
        for k, (a, b) in enumerate(((live_h, rec_live), (cells_h, rec_cells), (target_h, target)))
    ]
    for copy in smalls + copies[0] + copies[1] + [rest]:
        copy.start()
    masks = edge_masks((width_x, width_y))
    for copy in smalls:
        copy.wait()
    plane, _, row_x, col = split_cells(cell_lanes(rec_cells), width_x, width_y)
    live = live_lanes(rec_live, slots, capsules)
    columns = pick_columns(col, width_y)
    rows = pick_rows(row_x, width_x)
    for side in range(2):
        for copy in copies[side]:
            copy.wait()
        if side == 0:
            out, planes, lowest = down, (0, 1, 2), 0
        else:
            out, planes, lowest = up, (last, last - 1, last - 2), half
        near, far, third = planes
        span = range(lowest, lowest + half)
        weights, pres, damp = {}, {}, {}
        for z in span:
            vel_s[z] = 0.5 / density[z]
        for z in planes:
            spd = speed[z]
            pres[z] = 0.5 * density[z] * spd * spd
            damp[z] = 1.0 - admittance[z] * mask[z].astype(F32)
            weights[z] = plane_weights(vel_s[z], masks)
        for z in (near, far):
            pd_s[z] = pres[z] * damp[z]
        wall_low = min(near, far)
        base = side * 7 * width_x

        def put(k, value):
            stack[base + k * width_x : base + (k + 1) * width_x, :] = value

        for s in range(shots):
            first = {}
            for z in planes:
                here = p0[s, z]
                total = plane_part(here, weights[z])
                if z + 1 in span:
                    total += vel_s[z] * (p0[s, z + 1] - here)
                if z - 1 in span:
                    total -= vel_s[z - 1] * (here - p0[s, z - 1])
                first[z] = damp[z] * (here + pres[z] * total)
            out[s * width_x : (s + 1) * width_x, :] = p0[s, near]
            out[(2 + s) * width_x : (3 + s) * width_x, :] = first[near]
            out[(4 + s) * width_x : (5 + s) * width_x, :] = pd_s[near] * adj[s, near]
            q_far = p0[s, far] + first[far]
            q_third = p0[s, third] + first[third]
            beyond = vel_s[min(far, third)]
            total = plane_part(q_far, weights[far]) + beyond * (q_third - q_far)
            total -= vel_s[wall_low] * q_far
            put(s, pd_s[near] * vel_s[wall_low] * q_far)
            put(4 + s, damp[far] * first[far] + pd_s[far] * total)
        out[6 * width_x : 7 * width_x, :] = vel_s[near]
        out[7 * width_x : 8 * width_x, :] = pd_s[near]
        put(2, damp[near])
        put(3, pd_s[near] * vel_s[wall_low])
        put(6, pd_s[far] * vel_s[wall_low])
        found = pick(stack[base : base + 7 * width_x, :], columns, (1, 0))
        is_near = (plane == near).astype(F32)
        is_far = (plane == far).astype(F32)

        def got(k):
            return jnp.sum(found[k * width_x : (k + 1) * width_x, :] * rows, axis=0, keepdims=True)

        tiny = [is_near * got(s) + is_far * got(4 + s) for s in range(shots)]
        tiny += [
            is_near * got(2), is_far * got(6) - is_near * got(3), is_near,
            row_x.astype(F32), col.astype(F32), live,
        ]
        tiny += [live * goal_lanes(target, s, 1, capsules) for s in range(shots)]
        tiny.append(jnp.zeros((TINY - len(tiny), LANES), F32))
        start = 8 * width_x
        out[start : start + TINY, :] = jnp.zeros((TINY, width_y), F32)
        out[start : start + TINY, 0:LANES] = jnp.concatenate(tiny, axis=0)
    rest.wait()


def middle_kernel(
    rec_live, rec_cells, target, encoder, p0, adj, density, speed, admittance, mask,
    b1, b2, vel_s, pres_s, damp_s, pd_s, back_e, grad, rows_out, code_high, code_low,
    q_s, w_s,
):
    shots, depth, width_x, width_y = p0.shape
    slots, capsules = rec_cells.shape
    steps, channels = target.shape[2:]
    masks = edge_masks((width_x, width_y))
    last = depth - 1
    edges = (0, 1, last - 1, last)
    for z in range(depth):
        dens = density[z]
        spd = speed[z]
        vel = 0.5 / dens
        pres = 0.5 * dens * spd * spd
        damp = 1.0 - admittance[z] * mask[z].astype(F32)
        vel_s[z] = vel
        pres_s[z] = pres
        damp_s[z] = damp
        pd_s[z] = pres * damp
        w = plane_weights(vel, masks)
        for s in range(shots):
            here = p0[s, z]
            total = plane_part(here, w)
            if z < last:
                total += vel * (p0[s, z + 1] - here)
            if z > 0:
                total -= vel_s[z - 1] * (here - p0[s, z - 1])
            value = here + pres * total
            b1[s, z] = value
            q_s[s, z] = here + damp * value
            w_s[s, z] = pd_s[z] * adj[s, z]
    for z in range(depth):
        vel = vel_s[z]
        w = plane_weights(vel, masks)
        sums = jnp.zeros((width_x, width_y), F32)
        for s in range(shots):
            here, weighted = q_s[s, z], w_s[s, z]
            total = plane_part(here, w)
            back = plane_part(weighted, w)
            if z < last:
                total += vel * (q_s[s, z + 1] - here)
                back += vel * (w_s[s, z + 1] - weighted)
            if z > 0:
                total -= vel_s[z - 1] * (here - q_s[s, z - 1])
                back -= vel_s[z - 1] * (weighted - w_s[s, z - 1])
            value = damp_s[z] * b1[s, z] + pres_s[z] * total
            b2[s, z] = value
            back += damp_s[z] * adj[s, z]
            if z in edges:
                back_e[s, edges.index(z)] = back
            else:
                sums += value * adj[s, z] + b1[s, z] * back
        grad[z] = -(mask[z].astype(F32) * sums)
    lane = lax.broadcasted_iota(jnp.int32, (LANES, LANES), 1)
    line = lax.broadcasted_iota(jnp.int32, (LANES, LANES), 0)
    same = (lax.div(lane, capsules) == lax.div(line, capsules)) & (line < slots * capsules)
    code = jnp.concatenate([encoder[...], jnp.zeros((capsules, capsules - channels), F32)], axis=1)
    code = jnp.concatenate([code] * (LANES // capsules), axis=1)
    code = jnp.where(same, jnp.concatenate([code] * (LANES // capsules), axis=0), 0.0)
    square = lax.dot_general(
        code, code, (((1,), (1,)), ((), ())),
        precision=lax.Precision.HIGHEST, preferred_element_type=F32,
    )
    both = jnp.concatenate([code, square], axis=1)
    code_high[...], code_low[...] = halves(both)
    live = live_lanes(rec_live, slots, capsules)
    goal = [live * goal_lanes(target, s, n, capsules) for n in range(steps) for s in range(shots)]
    goal = jnp.concatenate(goal + [jnp.zeros((8 - len(goal), LANES), F32)], axis=0)
    rows_out[0:8, :] = lax.dot_general(
        goal, code, (((1,), (1,)), ((), ())),
        precision=lax.Precision.HIGHEST, preferred_element_type=F32,
    )
    rows_out[8:16, :] = jnp.concatenate(
        [cell_lanes(rec_cells).astype(F32), live, jnp.zeros((6, LANES), F32)], axis=0
    )


def window_part(u, vel, masks):
    low_x, high_x, low_y, high_y = masks
    rows, cols = u.shape
    flow_x = vel * (jnp.where(high_x, pltpu.roll(u, rows - 1, 0), 0.0) - u)
    flow_y = vel * (jnp.where(high_y, pltpu.roll(u, cols - 1, 1), 0.0) - u)
    fall_x = flow_x - jnp.where(low_x, pltpu.roll(flow_x, 1, 0), 0.0)
    return fall_x + flow_y - jnp.where(low_y, pltpu.roll(flow_y, 1, 1), 0.0)


def last_kernel(
    capsules, core, corners, below, above, p0, adj, mask, vel_s, pres_s, damp_s, pd_s, back_e,
    rows_in, code_high, code_low, b1_in, b2_in, grad_in,
    keep, send, coded, b1, b2, grad,
    halo_s, stack, spread,
):
    shots, depth, width_x, width_y = p0.shape
    slots = corners.shape[0]
    masks = edge_masks((width_x, width_y))
    last = depth - 1
    edges = (0, 1, last - 1, last)
    sides = ((below, 0, 1), (above, last, last - 1))
    blank = jnp.zeros((1, LANES), F32)

    def halo(ref, k):
        return ref[k * width_x : (k + 1) * width_x, :]

    def rows_of(array, k, count):
        return array[k * count : (k + 1) * count, :]

    for side, (ref, edge, inner) in enumerate(sides):
        vel_h, pd_h = halo(ref, 6), halo(ref, 7)
        vel_b = vel_h if side == 0 else vel_s[last]
        vel_in = vel_s[min(edge, inner)]
        w_h = plane_weights(vel_h, masks)
        w_e = plane_weights(vel_s[edge], masks)
        for s in range(shots):
            here, out = p0[s, edge], halo(ref, s)
            step = vel_b * (here - out)
            p1_h = halo(ref, 2 + s) + pd_h * step
            q_h = out + p1_h
            fixed = b1[s, edge] - pres_s[edge] * step
            change = -(pd_s[edge] * step)
            step2 = vel_b * (here + damp_s[edge] * fixed - q_h)
            base = side * 6
            halo_s[(base + s) * width_x : (base + s + 1) * width_x, :] = p1_h
            halo_s[(base + 2 + s) * width_x : (base + 3 + s) * width_x, :] = q_h
            halo_s[(base + 4 + s) * width_x : (base + 5 + s) * width_x, :] = pd_h * (
                plane_part(q_h, w_h) + step2
            )
            b1[s, edge] = fixed
            total = plane_part(change, w_e) - vel_in * change - step2
            b2[s, edge] = b2[s, edge] + change + pres_s[edge] * total
            b2[s, inner] = b2[s, inner] + pres_s[inner] * (vel_in * change)

    places = []
    for r in range(slots):
        z0 = jnp.clip(lax.div(corners[r], width_x * width_y), 0, depth - 2)
        x0 = lax.rem(lax.div(corners[r], width_y), width_x)
        start = jnp.minimum(lax.div(jnp.maximum(x0 - 1, 0), 8) * 8, width_x - WINDOW)
        places.append((z0, pl.multiple_of(start, 8)))
    _, row, _, col = split_cells(rows_in[8:9, :].astype(jnp.int32), width_x, width_y)
    live = rows_in[9:10, :]
    columns = pick_columns(col, width_y)
    slot_of = lax.div(lax.broadcasted_iota(jnp.int32, (1, LANES), 1), capsules)
    line = lax.broadcasted_iota(jnp.int32, (WINDOW, LANES), 0)
    found_rows = {}
    for r, (z0, start) in enumerate(places):
        own = jnp.where(slot_of == r, row, -1)
        for dz in range(2):
            first_row = (z0 + dz) * width_x + start
            found_rows[r, dz] = (line + first_row == own).astype(F32)
    index = {}
    for n, field in enumerate((b1, b2)):
        for r, (z0, start) in enumerate(places):
            for dz in range(2):
                damp = damp_s[z0 + dz, pl.ds(start, WINDOW), :]
                for s in range(shots):
                    k = index[n, r, dz, s] = len(index)
                    stack[k * WINDOW : (k + 1) * WINDOW, :] = (
                        damp * field[s, z0 + dz, pl.ds(start, WINDOW), :]
                    )
    found = pick(stack[...], columns, (1, 0))
    lines, lives, goals = [], [live] * 4, [blank] * 4
    for n in range(2):
        for s in range(shots):
            total = jnp.zeros((WINDOW, LANES), F32)
            for key, picked in found_rows.items():
                total += picked * rows_of(found, index[(n, *key, s)], WINDOW)
            lines.append(jnp.sum(total, axis=0, keepdims=True))
    columns_h, rows_h = [], []
    for side, (ref, _, _) in enumerate(sides):
        tiny = ref[8 * width_x : 8 * width_x + TINY, 0:LANES]
        near = tiny[4:5, :]
        picked = pick_rows(tiny[5:6, :].astype(jnp.int32), width_x).astype(F32)
        columns_h.append(pick_columns(tiny[6:7, :].astype(jnp.int32), width_y))
        rows_h.append(picked * near)
        found = pick(
            halo_s[side * 6 * width_x : (side + 1) * 6 * width_x, :], columns_h[side], (1, 0)
        )
        for s in range(shots):
            total = picked * (
                tiny[2:3, :] * rows_of(found, s, width_x)
                + tiny[3:4, :] * rows_of(found, 2 + s, width_x)
                + near * rows_of(found, 4 + s, width_x)
            )
            lines.append(tiny[s : s + 1, :] + jnp.sum(total, axis=0, keepdims=True))
            lives.append(tiny[7:8, :])
            goals.append(tiny[8 + s : 9 + s, :])
    goal_high, goal_low = halves(jnp.concatenate(goals, axis=0))
    high, low = code_high[:, 0:LANES], code_low[:, 0:LANES]
    known = rows_in[0:8, :] + (
        dot(goal_high, high, (1, 1)) + dot(goal_low, high, (1, 1)) + dot(goal_high, low, (1, 1))
    )
    got_high, got_low = halves(jnp.concatenate(lines, axis=0))
    both = (
        dot(got_high, code_high[...], (1, 0)) + dot(got_low, code_high[...], (1, 0))
        + dot(got_high, code_low[...], (1, 0))
    )
    lives = jnp.concatenate(lives, axis=0)
    coded[...] = both[:, 0:LANES] * lives
    source = both[:, LANES:] * lives - known

    parts = [None] * len(index)
    for (n, r, dz, s), k in index.items():
        line_of = n * shots + s
        parts[k] = found_rows[r, dz] * source[line_of : line_of + 1, :]
    spread[...] = pick(jnp.concatenate(parts, axis=0), columns, (1, 1))
    for side, (ref, edge, inner) in enumerate(sides):
        lines = [
            rows_h[side] * source[4 + 2 * side + s : 5 + 2 * side + s, :] for s in range(shots)
        ]
        placed = pick(jnp.concatenate(lines, axis=0), columns_h[side], (1, 1))
        vel_b = halo(ref, 6) if side == 0 else vel_s[last]
        sums = jnp.zeros((width_x, width_y), F32)
        sums_in = jnp.zeros((width_x, width_y), F32)
        for s in range(shots):
            w_h = halo(ref, 4 + s) + halo(ref, 7) * rows_of(placed, s, width_x)
            start = adj[s, edge]
            back = back_e[s, edges.index(edge)] - vel_b * (pd_s[edge] * start - w_h)
            sums += b2[s, edge] * start + b1[s, edge] * back
            sums_in += b2[s, inner] * adj[s, inner] + b1[s, inner] * back_e[s, edges.index(inner)]
        grad[edge] = -(mask[edge].astype(F32) * sums)
        grad[inner] = -(mask[inner].astype(F32) * sums_in)

    near_masks = edge_masks((WINDOW, width_y))
    for r, (z0, start) in enumerate(places):
        window = pl.ds(start, WINDOW)
        lower, upper = jnp.maximum(z0 - 1, 0), jnp.minimum(z0 + 2, last)
        vel_low = jnp.where(
            z0 > 0, vel_s[lower, window, :], below[pl.ds(6 * width_x + start, WINDOW), :]
        )
        vel = [vel_s[z0 + dz, window, :] for dz in range(2)]
        sums = [jnp.zeros((WINDOW, width_y), F32) for _ in range(4)]
        for s in range(shots):
            now, before = [
                [rows_of(spread, index[n, r, dz, s], WINDOW) for dz in range(2)] for n in (1, 0)
            ]
            w = [pd_s[z0 + dz, window, :] * now[dz] for dz in range(2)]
            between = vel[0] * (w[1] - w[0])
            outer = [vel_low * w[0], vel[1] * w[1]]
            for dz in range(2):
                total = window_part(w[dz], vel[dz], near_masks) - outer[dz]
                total += between if dz == 0 else -between
                total += damp_s[z0 + dz, window, :] * now[dz] + before[dz]
                sums[1 + dz] += (
                    b2[s, z0 + dz, window, :] * now[dz] + b1[s, z0 + dz, window, :] * total
                )
            sums[0] += b1[s, lower, window, :] * outer[0]
            sums[3] += b1[s, upper, window, :] * outer[1]
        inside = (jnp.where(z0 > 0, 1.0, 0.0), 1.0, 1.0, jnp.where(z0 + 2 < depth, 1.0, 0.0))
        for z, total, factor in zip((lower, z0, z0 + 1, upper), sums, inside):
            wall = mask[z, window, :].astype(F32)
            grad[z, window, :] = grad[z, window, :] - factor * (wall * total)
    half = depth // 2
    mine = core[0] * half
    for z in range(half):
        keep[z] = grad[mine + z]
        send[z] = grad[half - mine + z]


def join_kernel(core, mine, other, out, sems):
    half = mine.shape[0]
    start = core[0] * half
    copies = [
        pltpu.make_async_copy(mine, out.at[pl.ds(start, half)], sems.at[0]),
        pltpu.make_async_copy(other, out.at[pl.ds(half - start, half)], sems.at[1]),
    ]
    for copy in copies:
        copy.start()
    for copy in copies:
        copy.wait()


def body(
    pressure_init, adjoint_init, density, speed, admittance, bound_mask,
    rec_cells, rec_live, encoder, target,
):
    shots, depth, width_x, width_y = pressure_init.shape
    slots, capsules = rec_cells.shape
    steps, channels = target.shape[2:]
    slabs, peers = lax.axis_size("slab"), lax.axis_size("shot")
    field = (shots, depth, width_x, width_y)
    slab = (depth, width_x, width_y)
    half = (depth // 2, width_x, width_y)
    message = (8 * width_x + TINY, width_y)

    def ins(count, scalars=0, far=0):
        kinds = [pltpu.SMEM] * scalars + [VMEM] * (count - scalars - far) + [pltpu.HBM] * far
        return [pl.BlockSpec(memory_space=kind) for kind in kinds]

    def outs(*shapes):
        return [
            shape if isinstance(shape, jax.ShapeDtypeStruct) else jax.ShapeDtypeStruct(shape, F32)
            for shape in shapes
        ]

    params = pltpu.CompilerParams(vmem_limit_bytes=VMEM_LIMIT)
    up, down, p0, adj, density, speed, admittance, bound_mask = pl.pallas_call(
        edge_kernel,
        in_specs=ins(9, 0, 9),
        out_specs=ins(8),
        out_shape=[
            VMEM(message, F32), VMEM(message, F32), VMEM(field, F32), VMEM(field, F32),
            VMEM(slab, F32), VMEM(slab, F32), VMEM(slab, F32), VMEM(slab, jnp.int32),
        ],
        scratch_shapes=[
            VMEM(slab, F32), VMEM(slab, F32), VMEM((14 * width_x, width_y), F32),
            pltpu.SMEM(rec_live.shape, jnp.int32), VMEM(rec_cells.shape, jnp.int32),
            VMEM(target.shape, F32),
            pltpu.SemaphoreType.DMA((2, 6)), pltpu.SemaphoreType.DMA((4,)),
        ],
        compiler_params=params,
        name="edge",
    )(
        *[
            pltpu.with_memory_space_constraint(array, pltpu.HBM)
            for array in (
                rec_live, rec_cells, target,
                pressure_init, adjoint_init, density, speed, admittance, bound_mask,
            )
        ],
    )

    even = lax.rem(lax.axis_index("slab"), 2) == 0

    def exchange(value, first):
        pairs = [(i, i + 1) for i in range(first, slabs - 1, 2)]
        return lax.ppermute(value, "slab", pairs + [(b, a) for a, b in pairs])

    outer = exchange(jnp.where(even, down, up), 1)
    inner = exchange(jnp.where(even, up, down), 0)
    below, above = jnp.where(even, outer, inner), jnp.where(even, inner, outer)

    table = jax.ShapeDtypeStruct((LANES, 2 * LANES), jnp.bfloat16)
    b1, b2, vel, pres, damp, pd, back, grad, rows, high, low = pl.pallas_call(
        middle_kernel,
        in_specs=ins(10, 1),
        out_specs=ins(11),
        out_shape=outs(
            field, field, slab, slab, slab, slab, (shots, 4, width_x, width_y), slab,
            (16, LANES), table, table,
        ),
        scratch_shapes=[VMEM(field, F32), VMEM(field, F32)],
        compiler_params=params,
        cost_estimate=pl.CostEstimate(flops=20_000_000, bytes_accessed=6_000_000, transcendentals=0),
        name="middle",
    )(
        rec_live, rec_cells, target, encoder, p0, adj, density, speed, admittance, bound_mask,
    )

    core = lax.rem(lax.axis_index("shot"), 2)
    corners = jnp.min(rec_cells, axis=1)
    windows = steps * slots * 2 * shots * WINDOW
    keep, send, coded, _, _, _ = pl.pallas_call(
        functools.partial(last_kernel, capsules),
        in_specs=ins(18, 2),
        out_specs=ins(6),
        out_shape=outs(half, half, (8, LANES), field, field, slab),
        scratch_shapes=[
            VMEM((12 * width_x, width_y), F32), VMEM((windows, width_y), F32),
            VMEM((windows, width_y), F32),
        ],
        input_output_aliases={15: 3, 16: 4, 17: 5},
        compiler_params=params,
        name="last",
    )(
        core[None], corners, below, above, p0, adj, bound_mask, vel, pres, damp, pd, back, rows, high, low, b1, b2, grad,
    )

    pairs = [(i, i ^ 1) for i in range(peers)]
    groups = [list(range(c, peers, 2)) for c in range(2)]
    total = keep + lax.ppermute(send, "shot", pairs)
    copies = jnp.broadcast_to(total, (peers // 2, *half))
    total = lax.all_to_all(
        copies, "shot", split_axis=0, concat_axis=0, tiled=True, axis_index_groups=groups
    ).sum(axis=0)
    total, coded, later = lax.optimization_barrier((total, coded, core))
    other = lax.ppermute(total, "shot", pairs)
    gradient = pl.pallas_call(
        join_kernel,
        in_specs=ins(3, 1),
        out_specs=pl.BlockSpec(memory_space=pltpu.HBM),
        out_shape=pltpu.HBM(slab, F32),
        scratch_shapes=[pltpu.SemaphoreType.DMA((2,))],
        compiler_params=params,
        name="join",
    )(later[None], total, other)
    signals = coded[: steps * shots, : slots * capsules]
    signals = signals.reshape(steps, shots, slots, capsules)[..., :channels]
    return jnp.transpose(signals, (2, 1, 0, 3)), gradient


def solution(mesh):
    placed = (
        P("shot", "slab", None, None), P("shot", "slab", None, None),
        P("slab", None, None), P("slab", None, None), P("slab", None, None), P("slab", None, None),
        P("slab", None), P("slab"), P(), P("slab", "shot", None, None),
    )
    return jax.shard_map(
        body, mesh=mesh, in_specs=placed,
        out_specs=(P("slab", "shot", None, None), P("slab", None, None)),
        check_vma=False,
    )
```

```python
import functools

import jax
import jax.numpy as jnp
from jax import lax
from jax.experimental import pallas as pl
from jax.experimental.pallas import tpu as pltpu
from jax.sharding import PartitionSpec as P


LANES = 128
FAR = float(1 << 20)
WINDOW = 16
VMEM_LIMIT = 20 << 20
TINY = 16
VMEM = pltpu.VMEM
F32 = jnp.float32


def dot(a, b, contract):
    return lax.dot_general(
        a, b, ((contract[:1], contract[1:]), ((), ())), preferred_element_type=F32
    )


def halves(a):
    high = a.astype(jnp.bfloat16)
    return high, (a - high.astype(F32)).astype(jnp.bfloat16)


def pick(a, onehot, contract):
    high, low = halves(a)
    return dot(high, onehot, contract) + dot(low, onehot, contract)


def edge_masks(shape):
    row = lax.broadcasted_iota(jnp.int32, shape, 0)
    col = lax.broadcasted_iota(jnp.int32, shape, 1)
    return row > 0, row < shape[0] - 1, col > 0, col < shape[1] - 1


def plane_weights(vel, masks):
    low_x, high_x, low_y, high_y = masks
    xp = jnp.where(high_x, vel, 0.0)
    xm = jnp.where(low_x, pltpu.roll(vel, 1, 0), 0.0)
    yp = jnp.where(high_y, vel, 0.0)
    ym = jnp.where(low_y, pltpu.roll(vel, 1, 1), 0.0)
    return xp, xm, yp, ym, 2.0 * vel + xm + ym


def plane_part(u, weights):
    xp, xm, yp, ym, centre = weights
    rows, cols = u.shape
    return (
        xp * pltpu.roll(u, rows - 1, 0) + xm * pltpu.roll(u, 1, 0)
        + yp * pltpu.roll(u, cols - 1, 1) + ym * pltpu.roll(u, 1, 1)
        - centre * u
    )


def pick_columns(cols, width):
    return (lax.broadcasted_iota(jnp.int32, (width, cols.shape[1]), 0) == cols).astype(jnp.bfloat16)


def pick_rows(rows, count):
    return (lax.broadcasted_iota(jnp.int32, (count, rows.shape[1]), 0) == rows).astype(F32)


def split_cells(cells, width_x, width_y):
    plane = lax.div(cells, width_x * width_y)
    row = lax.div(cells, width_y)
    return plane, row, row - plane * width_x, cells - row * width_y


def in_lanes(pieces, width, fill=0.0):
    parts = []
    for piece in pieces:
        parts.append(piece)
        if piece.shape[1] < width:
            parts.append(jnp.full((1, width - piece.shape[1]), fill, piece.dtype))
    used = width * len(pieces)
    parts.append(jnp.full((1, LANES - used), fill, pieces[0].dtype))
    return jnp.concatenate(parts, axis=1)


def live_lanes(rec_live, slots, capsules):
    slot = lax.div(lax.broadcasted_iota(jnp.int32, (1, LANES), 1), capsules)
    row = jnp.zeros((1, LANES), F32)
    for r in range(slots):
        row = jnp.where(slot == r, rec_live[r].astype(F32), row)
    return row


def cell_lanes(rec_cells):
    slots, capsules = rec_cells.shape
    return in_lanes([rec_cells[r : r + 1, :] for r in range(slots)], capsules, int(FAR))


def goal_lanes(target, s, n, capsules):
    return in_lanes([target[r, s, n : n + 1, :] for r in range(target.shape[0])], capsules)


def edge_kernel(
    core_ref, live_h, cells_h, target_h, p0_h, adj_h, density_h, speed_h, admittance_h, mask_h,
    face, sent, fields, density, speed, admittance, mask, vel_s, pd_s, stack,
    both, rec_live, rec_cells, target, sems, small_sems,
):
    p0, adj = fields.at[0], fields.at[1]
    shots, depth, width_x, width_y = p0.shape
    slots, capsules = rec_cells.shape
    half = depth // 2
    last = depth - 1
    copies = []
    for side in range(2):
        some = pl.ds(side * half, half)
        pairs = [(h.at[some], v.at[some]) for h, v in (
            (density_h, density), (speed_h, speed), (admittance_h, admittance), (mask_h, mask))]
        pairs.insert(0, (p0_h.at[:, some], p0.at[:, some]))
        outmost = pl.ds(side * last, 1)
        pairs.append((adj_h.at[:, outmost], adj.at[:, outmost]))
        copies.append([
            pltpu.make_async_copy(a, b, sems.at[side, k]) for k, (a, b) in enumerate(pairs)
        ])
    inside = pl.ds(1, depth - 2)
    rest = pltpu.make_async_copy(adj_h.at[:, inside], adj.at[:, inside], small_sems.at[3])
    smalls = [
        pltpu.make_async_copy(a, b, small_sems.at[k])
        for k, (a, b) in enumerate(((live_h, rec_live), (cells_h, rec_cells), (target_h, target)))
    ]
    for copy in smalls + copies[0] + copies[1] + [rest]:
        copy.start()
    masks = edge_masks((width_x, width_y))
    for copy in smalls:
        copy.wait()
    plane, _, row_x, col = split_cells(cell_lanes(rec_cells), width_x, width_y)
    live = live_lanes(rec_live, slots, capsules)
    columns = pick_columns(col, width_y)
    rows = pick_rows(row_x, width_x)
    for side in range(2):
        for copy in copies[side]:
            copy.wait()
        out = both.at[side]
        if side == 0:
            planes, lowest = (0, 1, 2), 0
        else:
            planes, lowest = (last, last - 1, last - 2), half
        near, far, third = planes
        span = range(lowest, lowest + half)
        weights, pres, damp = {}, {}, {}
        for z in span:
            vel_s[z] = 0.5 / density[z]
        for z in planes:
            spd = speed[z]
            pres[z] = 0.5 * density[z] * spd * spd
            damp[z] = 1.0 - admittance[z] * mask[z].astype(F32)
            weights[z] = plane_weights(vel_s[z], masks)
        for z in (near, far):
            pd_s[z] = pres[z] * damp[z]
        wall_low = min(near, far)
        base = side * 7 * width_x

        def put(k, value):
            stack[base + k * width_x : base + (k + 1) * width_x, :] = value

        for s in range(shots):
            first = {}
            for z in planes:
                here = p0[s, z]
                total = plane_part(here, weights[z])
                if z + 1 in span:
                    total += vel_s[z] * (p0[s, z + 1] - here)
                if z - 1 in span:
                    total -= vel_s[z - 1] * (here - p0[s, z - 1])
                first[z] = damp[z] * (here + pres[z] * total)
            out[s * width_x : (s + 1) * width_x, :] = p0[s, near]
            out[(2 + s) * width_x : (3 + s) * width_x, :] = first[near]
            out[(4 + s) * width_x : (5 + s) * width_x, :] = pd_s[near] * adj[s, near]
            q_far = p0[s, far] + first[far]
            q_third = p0[s, third] + first[third]
            beyond = vel_s[min(far, third)]
            total = plane_part(q_far, weights[far]) + beyond * (q_third - q_far)
            total -= vel_s[wall_low] * q_far
            put(s, pd_s[near] * vel_s[wall_low] * q_far)
            put(4 + s, damp[far] * first[far] + pd_s[far] * total)
        out[6 * width_x : 7 * width_x, :] = vel_s[near]
        out[7 * width_x : 8 * width_x, :] = pd_s[near]
        put(2, damp[near])
        put(3, pd_s[near] * vel_s[wall_low])
        put(6, pd_s[far] * vel_s[wall_low])
        found = pick(stack[base : base + 7 * width_x, :], columns, (1, 0))
        is_near = (plane == near).astype(F32)
        is_far = (plane == far).astype(F32)

        def got(k):
            return jnp.sum(found[k * width_x : (k + 1) * width_x, :] * rows, axis=0, keepdims=True)

        tiny = [is_near * got(s) + is_far * got(4 + s) for s in range(shots)]
        tiny += [
            is_near * got(2), is_far * got(6) - is_near * got(3), is_near,
            row_x.astype(F32), col.astype(F32), live,
        ]
        tiny += [live * goal_lanes(target, s, n, capsules) for n in (1, 0) for s in range(shots)]
        tiny.append(cell_lanes(rec_cells).astype(F32))
        tiny.append(jnp.zeros((TINY - len(tiny), LANES), F32))
        start = 8 * width_x
        out[start : start + TINY, :] = jnp.zeros((TINY, width_y), F32)
        out[start : start + TINY, 0:LANES] = jnp.concatenate(tiny, axis=0)
    core = core_ref[0]
    moves = [
        pltpu.make_async_copy(both.at[core], face.at[pl.ds(0, both.shape[1])], small_sems.at[4]),
        pltpu.make_async_copy(both.at[1 - core], sent, small_sems.at[5]),
    ]
    for copy in moves:
        copy.start()
    for copy in [*moves, rest]:
        copy.wait()


def pack_kernel(got, face_in, face, sems):
    planes = got.shape[0] - TINY
    width_x = planes // 8
    second = got.shape[0]
    copies = [
        pltpu.make_async_copy(
            got.at[pl.ds(0, 6 * width_x)], face.at[pl.ds(second, 6 * width_x)], sems.at[0]
        ),
        pltpu.make_async_copy(
            got.at[pl.ds(planes, TINY)], face.at[pl.ds(second + 6 * width_x, TINY)], sems.at[1]
        ),
    ]
    for copy in copies:
        copy.start()
    for copy in copies:
        copy.wait()


def middle_kernel(
    capsules, core_ref, message, encoder, others, fields,
    density, speed, admittance, mask,
    b1, b2, vel_s, pres_s, damp_s, pd_s, back_e, grad, rows_out, code_high, code_low, corners,
    q_s, w_s,
):
    _, pair, depth, width_x, width_y = fields.shape
    shots = 2 * pair
    slots, steps, channels = corners.shape[0], 2, encoder.shape[1]
    masks = edge_masks((width_x, width_y))
    core = core_ref[0]
    half = depth // 2

    def plane_at(d):
        return d + core * (depth - 1 - 2 * d)

    def coupling(d):
        return vel_s[d + core * (depth - 2 - 2 * d)]

    def value_of(kind, s, z):
        return (others if s < pair else fields)[kind, s % pair, z]

    for z in range(depth):
        dens = density[z]
        spd = speed[z]
        pres = 0.5 * dens * spd * spd
        damp = 1.0 - admittance[z] * mask[z].astype(F32)
        vel_s[z] = 0.5 / dens
        pres_s[z] = pres
        damp_s[z] = damp
        pd_s[z] = pres * damp
    for d in range(depth - 1):
        z = plane_at(d)
        w = plane_weights(vel_s[z], masks)
        inwards, outwards = coupling(d), coupling(d - 1) if d > 0 else None
        for s in range(shots):
            here = value_of(0, s, z)
            total = plane_part(here, w) + inwards * (value_of(0, s, plane_at(d + 1)) - here)
            if d > 0:
                total += outwards * (value_of(0, s, plane_at(d - 1)) - here)
            value = here + pres_s[z] * total
            b1[s, z] = value
            q_s[s, d] = here + damp_s[z] * value
            if d <= half:
                w_s[s, d] = pd_s[z] * value_of(1, s, z)
    for d in range(depth - 2):
        z = plane_at(d)
        w = plane_weights(vel_s[z], masks)
        inwards, outwards = coupling(d), coupling(d - 1) if d > 0 else None
        sums = jnp.zeros((width_x, width_y), F32)
        for s in range(shots):
            here = q_s[s, d]
            total = plane_part(here, w) + inwards * (q_s[s, d + 1] - here)
            if d > 0:
                total += outwards * (q_s[s, d - 1] - here)
            value = damp_s[z] * b1[s, z] + pres_s[z] * total
            b2[s, z] = value
            if d >= half:
                continue
            weighted, start = w_s[s, d], value_of(1, s, z)
            back = plane_part(weighted, w) + inwards * (w_s[s, d + 1] - weighted)
            if d > 0:
                back += outwards * (w_s[s, d - 1] - weighted)
            back += damp_s[z] * start
            if d < 2:
                back_e[s, d] = back
            else:
                sums += value * start + b1[s, z] * back
        if d < half:
            grad[z] = -(mask[z].astype(F32) * sums)
        else:
            grad[z] = sums
    grad[plane_at(depth - 2)] = jnp.zeros((width_x, width_y), F32)
    lane = lax.broadcasted_iota(jnp.int32, (LANES, LANES), 1)
    line = lax.broadcasted_iota(jnp.int32, (LANES, LANES), 0)
    same = (lax.div(lane, capsules) == lax.div(line, capsules)) & (line < slots * capsules)
    code = jnp.concatenate([encoder[...], jnp.zeros((capsules, capsules - channels), F32)], axis=1)
    code = jnp.concatenate([code] * (LANES // capsules), axis=1)
    code = jnp.where(same, jnp.concatenate([code] * (LANES // capsules), axis=0), 0.0)
    square = lax.dot_general(
        code, code, (((1,), (1,)), ((), ())),
        precision=lax.Precision.HIGHEST, preferred_element_type=F32,
    )
    both = jnp.concatenate([code, square], axis=1)
    code_high[...], code_low[...] = halves(both)
    own = message[8 * width_x : 8 * width_x + TINY, 0:LANES]
    start = message.shape[0] - TINY
    other = message[start : start + TINY, 0:LANES]
    goal = []
    for n in range(steps):
        first = 10 if n == 0 else 8
        goal += [tiny[first : first + pair, :] for tiny in (other, own)]
    cells = own[12:13, :]
    slot_of = lax.div(lax.broadcasted_iota(jnp.int32, (1, LANES), 1), capsules)
    for r in range(slots):
        corners[r] = jnp.min(jnp.where(slot_of == r, cells, FAR)).astype(jnp.int32)
    goal = jnp.concatenate(goal, axis=0)
    rows_out[0:8, :] = lax.dot_general(
        goal, code, (((1,), (1,)), ((), ())),
        precision=lax.Precision.HIGHEST, preferred_element_type=F32,
    )
    rows_out[8:16, :] = jnp.concatenate(
        [cells, own[7:8, :], jnp.zeros((6, LANES), F32)], axis=0
    )


def window_part(u, vel, masks):
    low_x, high_x, low_y, high_y = masks
    rows, cols = u.shape
    flow_x = vel * (jnp.where(high_x, pltpu.roll(u, rows - 1, 0), 0.0) - u)
    flow_y = vel * (jnp.where(high_y, pltpu.roll(u, cols - 1, 1), 0.0) - u)
    fall_x = flow_x - jnp.where(low_x, pltpu.roll(flow_x, 1, 0), 0.0)
    return fall_x + flow_y - jnp.where(low_y, pltpu.roll(flow_y, 1, 1), 0.0)


def last_kernel(
    capsules, core_ref, corners, halo, others, fields, mask, vel_s, pres_s, damp_s, pd_s, back_e,
    rows_in, code_high, code_low, b1_in, b2_in, grad_in,
    out, coded, coded_other, b1, b2, grad,
    halo_s, stack, spread,
):
    _, pair, depth, width_x, width_y = fields.shape
    shots = 2 * pair
    slots = corners.shape[0]
    masks = edge_masks((width_x, width_y))
    core = core_ref[0]
    half = depth // 2
    last = depth - 1
    edge, inner = core * last, 1 + core * (last - 2)
    second = 8 * width_x + TINY

    def value_of(kind, s, z):
        return (others if s < pair else fields)[kind, s % pair, z]

    def face(k, s):
        start = (second if s >= pair else 0) + (k + s % pair) * width_x
        return halo[start : start + width_x, :]

    def rows_of(array, k, count):
        return array[k * count : (k + 1) * count, :]

    vel_h, pd_h = rows_of(halo, 6, width_x), rows_of(halo, 7, width_x)
    vel_b = jnp.where(core == 0, vel_h, vel_s[last])
    vel_in = vel_s[core * (depth - 2)]
    w_h = plane_weights(vel_h, masks)
    w_e = plane_weights(vel_s[edge], masks)
    for s in range(shots):
        here, beyond = value_of(0, s, edge), face(0, s)
        step = vel_b * (here - beyond)
        p1_h = face(2, s) + pd_h * step
        q_h = beyond + p1_h
        fixed = b1[s, edge] - pres_s[edge] * step
        change = -(pd_s[edge] * step)
        step2 = vel_b * (here + damp_s[edge] * fixed - q_h)
        halo_s[s * width_x : (s + 1) * width_x, :] = p1_h
        halo_s[(shots + s) * width_x : (shots + s + 1) * width_x, :] = q_h
        halo_s[(2 * shots + s) * width_x : (2 * shots + s + 1) * width_x, :] = pd_h * (
            plane_part(q_h, w_h) + step2
        )
        b1[s, edge] = fixed
        total = plane_part(change, w_e) - vel_in * change - step2
        b2[s, edge] = b2[s, edge] + change + pres_s[edge] * total
        b2[s, inner] = b2[s, inner] + pres_s[inner] * (vel_in * change)

    places = []
    low, high = 2 * core, 4 + 2 * core
    for r in range(slots):
        z0 = jnp.clip(lax.div(corners[r], width_x * width_y), low, high)
        x0 = lax.rem(lax.div(corners[r], width_y), width_x)
        start = jnp.minimum(lax.div(jnp.maximum(x0 - 1, 0), 8) * 8, width_x - WINDOW)
        places.append((z0, pl.multiple_of(start, 8)))
    _, row, _, col = split_cells(rows_in[8:9, :].astype(jnp.int32), width_x, width_y)
    live = rows_in[9:10, :]
    columns = pick_columns(col, width_y)
    slot_of = lax.div(lax.broadcasted_iota(jnp.int32, (1, LANES), 1), capsules)
    line = lax.broadcasted_iota(jnp.int32, (WINDOW, LANES), 0)
    mine = jnp.zeros((1, LANES), F32)
    found_rows = {}
    for r, (z0, start) in enumerate(places):
        own = jnp.where(slot_of == r, row, -1)
        upper = jnp.where(lax.div(corners[r], width_x * width_y) >= half, 1, 0)
        mine = jnp.where(slot_of == r, jnp.where(upper == core, 1.0, 0.0), mine)
        for dz in range(2):
            first_row = (z0 + dz) * width_x + start
            found_rows[r, dz] = (line + first_row == own).astype(F32)
    index = {}
    for n, field in enumerate((b1, b2)):
        for r, (z0, start) in enumerate(places):
            for dz in range(2):
                damp = damp_s[z0 + dz, pl.ds(start, WINDOW), :]
                for s in range(shots):
                    k = index[n, r, dz, s] = len(index)
                    stack[k * WINDOW : (k + 1) * WINDOW, :] = (
                        damp * field[s, z0 + dz, pl.ds(start, WINDOW), :]
                    )
    found = pick(stack[...], columns, (1, 0))
    blank = jnp.zeros((1, LANES), F32)
    lines, goals = [], []
    for n in range(2):
        for s in range(shots):
            total = jnp.zeros((WINDOW, LANES), F32)
            for key, picked in found_rows.items():
                total += picked * rows_of(found, index[(n, *key, s)], WINDOW)
            lines.append(jnp.sum(total, axis=0, keepdims=True))
    start = 8 * width_x
    tiny = halo[start : start + TINY, 0:LANES]
    start = second + 6 * width_x
    tiny_second = halo[start : start + TINY, 0:LANES]
    near = tiny[4:5, :]
    picked = pick_rows(tiny[5:6, :].astype(jnp.int32), width_x).astype(F32)
    columns_h = pick_columns(tiny[6:7, :].astype(jnp.int32), width_y)
    rows_h = picked * near
    found = pick(halo_s[...], columns_h, (1, 0))
    for s in range(shots):
        own_tiny = tiny if s < pair else tiny_second
        total = picked * (
            tiny[2:3, :] * rows_of(found, s, width_x)
            + tiny[3:4, :] * rows_of(found, shots + s, width_x)
            + near * rows_of(found, 2 * shots + s, width_x)
        )
        k = s % pair
        lines.append(own_tiny[k : k + 1, :] + jnp.sum(total, axis=0, keepdims=True))
        goals.append(own_tiny[8 + k : 9 + k, :])
    lines += [blank] * 4
    goal_high, goal_low = halves(jnp.concatenate(goals + [blank] * 4, axis=0))
    high, low = code_high[:, 0:LANES], code_low[:, 0:LANES]
    known = jnp.concatenate([
        rows_in[0:8, :],
        dot(goal_high, high, (1, 1)) + dot(goal_low, high, (1, 1)) + dot(goal_high, low, (1, 1)),
    ], axis=0)
    got_high, got_low = halves(jnp.concatenate(lines, axis=0))
    both = (
        dot(got_high, code_high[...], (1, 0)) + dot(got_low, code_high[...], (1, 0))
        + dot(got_high, code_low[...], (1, 0))
    )
    lives = jnp.concatenate([live] * 8 + [tiny[7:8, :]] * 8, axis=0)
    signals = both[0:8, 0:LANES] * (live * mine)
    for ref, first in ((coded_other, 0), (coded, pair)):
        ref[...] = jnp.zeros(ref.shape, F32)
        for n in range(2):
            ref[n * pair : (n + 1) * pair, 0:LANES] = (
                signals[n * shots + first : n * shots + first + pair, :]
            )
    source = both[:, LANES:] * lives - known

    parts = [None] * len(index)
    for (n, r, dz, s), k in index.items():
        line_of = n * shots + s
        parts[k] = found_rows[r, dz] * source[line_of : line_of + 1, :]
    spread[...] = pick(jnp.concatenate(parts, axis=0), columns, (1, 1))
    lines = [rows_h * source[8 + s : 9 + s, :] for s in range(shots)]
    placed = pick(jnp.concatenate(lines, axis=0), columns_h, (1, 1))
    sums = jnp.zeros((width_x, width_y), F32)
    sums_in = jnp.zeros((width_x, width_y), F32)
    for s in range(shots):
        weighted = face(4, s) + pd_h * rows_of(placed, s, width_x)
        start = value_of(1, s, edge)
        back = back_e[s, 0] - vel_b * (pd_s[edge] * start - weighted)
        sums += b2[s, edge] * start + b1[s, edge] * back
        sums_in += b2[s, inner] * value_of(1, s, inner) + b1[s, inner] * back_e[s, 1]
    grad[edge] = -(mask[edge].astype(F32) * sums)
    grad[inner] = -(mask[inner].astype(F32) * sums_in)

    near_masks = edge_masks((WINDOW, width_y))
    for r, (z0, start) in enumerate(places):
        window = pl.ds(start, WINDOW)
        lower, upper = jnp.maximum(z0 - 1, 0), jnp.minimum(z0 + 2, last)
        vel_low = jnp.where(
            z0 > 0, vel_s[lower, window, :], halo[pl.ds(6 * width_x + start, WINDOW), :]
        )
        vel = [vel_s[z0 + dz, window, :] for dz in range(2)]
        sums = [jnp.zeros((WINDOW, width_y), F32) for _ in range(4)]
        for s in range(shots):
            now, before = [
                [rows_of(spread, index[n, r, dz, s], WINDOW) for dz in range(2)] for n in (1, 0)
            ]
            w = [pd_s[z0 + dz, window, :] * now[dz] for dz in range(2)]
            between = vel[0] * (w[1] - w[0])
            outer = [vel_low * w[0], vel[1] * w[1]]
            for dz in range(2):
                total = window_part(w[dz], vel[dz], near_masks) - outer[dz]
                total += between if dz == 0 else -between
                total += damp_s[z0 + dz, window, :] * now[dz] + before[dz]
                sums[1 + dz] += (
                    b2[s, z0 + dz, window, :] * now[dz] + b1[s, z0 + dz, window, :] * total
                )
            sums[0] += b1[s, lower, window, :] * outer[0]
            sums[3] += b1[s, upper, window, :] * outer[1]
        inside = (jnp.where(z0 > 0, 1.0, 0.0), 1.0, 1.0, jnp.where(z0 + 2 < depth, 1.0, 0.0))
        for z, total, factor in zip((lower, z0, z0 + 1, upper), sums, inside):
            wall = mask[z, window, :].astype(F32)
            grad[z, window, :] = grad[z, window, :] - factor * (wall * total)
    for z in range(half):
        out[z * width_x : (z + 1) * width_x, :] = grad[core * half + z]


def join_kernel(core, mine, other, coded, out, signals, signals_s, sems):
    half = mine.shape[0]
    start = core[0] * half
    slots, shots, steps, channels = signals_s.shape
    copies = [
        pltpu.make_async_copy(mine, out.at[pl.ds(start, half)], sems.at[0]),
        pltpu.make_async_copy(
            other.at[pl.ds(0, half)], out.at[pl.ds(half - start, half)], sems.at[1]
        ),
    ]
    for copy in copies:
        copy.start()
    total = coded[...] + other[half : half + 8, :]
    for r in range(slots):
        for s in range(shots):
            for n in range(steps):
                line = n * shots + s
                signals_s[r, s, n : n + 1, :] = total[line : line + 1, r * 32 : r * 32 + channels]
    copies.append(pltpu.make_async_copy(signals_s, signals, sems.at[2]))
    copies[-1].start()
    for copy in copies:
        copy.wait()


def body(
    pressure_init, adjoint_init, density, speed, admittance, bound_mask,
    rec_cells, rec_live, encoder, target,
):
    shots, depth, width_x, width_y = pressure_init.shape
    slots, capsules = rec_cells.shape
    steps, channels = target.shape[2:]
    slabs, peers = lax.axis_size("slab"), lax.axis_size("shot")
    field = (shots, depth, width_x, width_y)
    slab = (depth, width_x, width_y)
    message = (8 * width_x + TINY, width_y)

    def ins(count, scalars=0, far=0):
        kinds = [pltpu.SMEM] * scalars + [VMEM] * (count - scalars - far) + [pltpu.HBM] * far
        return [pl.BlockSpec(memory_space=kind) for kind in kinds]

    def outs(*shapes):
        return [
            shape if isinstance(shape, jax.ShapeDtypeStruct) else jax.ShapeDtypeStruct(shape, F32)
            for shape in shapes
        ]

    params = pltpu.CompilerParams(vmem_limit_bytes=VMEM_LIMIT)
    core = lax.rem(lax.axis_index("shot"), 2)
    longer = (message[0] + 6 * width_x + TINY, width_y)
    face, sent, fields, density, speed, admittance, bound_mask = pl.pallas_call(
        edge_kernel,
        in_specs=ins(10, 1, 9),
        out_specs=ins(7),
        out_shape=[
            VMEM(longer, F32), VMEM(message, F32), VMEM((2, *field), F32),
            VMEM(slab, F32), VMEM(slab, F32), VMEM(slab, F32), VMEM(slab, jnp.int32),
        ],
        scratch_shapes=[
            VMEM(slab, F32), VMEM(slab, F32), VMEM((14 * width_x, width_y), F32),
            VMEM((2, *message), F32),
            pltpu.SMEM(rec_live.shape, jnp.int32), VMEM(rec_cells.shape, jnp.int32),
            VMEM(target.shape, F32),
            pltpu.SemaphoreType.DMA((2, 6)), pltpu.SemaphoreType.DMA((6,)),
        ],
        compiler_params=params,
        name="edge",
    )(
        core[None],
        *[
            pltpu.with_memory_space_constraint(array, pltpu.HBM)
            for array in (
                rec_live, rec_cells, target,
                pressure_init, adjoint_init, density, speed, admittance, bound_mask,
            )
        ],
    )

    pairs = [(i, i ^ 1) for i in range(peers)]
    facing = []
    for i in range(slabs - 1):
        for j in range(0, peers, 2):
            ends = (i * peers + j + 1, (i + 1) * peers + j)
            facing += [ends, ends[::-1]]
    got = lax.ppermute(sent, "shot", pairs)
    others = lax.ppermute(fields, "shot", pairs)
    face = pl.pallas_call(
        pack_kernel,
        in_specs=ins(2),
        out_specs=pl.BlockSpec(memory_space=VMEM),
        out_shape=VMEM(longer, F32),
        scratch_shapes=[pltpu.SemaphoreType.DMA((2,))],
        input_output_aliases={1: 0},
        compiler_params=params,
        name="pack",
    )(got, face)
    halo = lax.ppermute(face, ("slab", "shot"), facing)

    table = jax.ShapeDtypeStruct((LANES, 2 * LANES), jnp.bfloat16)
    four = (2 * shots, *slab)
    rows_plane = (width_x, width_y)
    b1, b2, vel, pres, damp, pd, back, grad, rows, high, low, corners = pl.pallas_call(
        functools.partial(middle_kernel, capsules),
        in_specs=ins(9, 1),
        out_specs=[*ins(11), *ins(1, 1)],
        out_shape=outs(
            four, four, slab, slab, slab, slab, (2 * shots, 2, *rows_plane), slab,
            (16, LANES), table, table, jax.ShapeDtypeStruct((slots,), jnp.int32),
        ),
        scratch_shapes=[
            VMEM((2 * shots, depth - 1, *rows_plane), F32),
            VMEM((2 * shots, depth // 2 + 1, *rows_plane), F32),
        ],
        compiler_params=params,
        cost_estimate=pl.CostEstimate(flops=30_000_000, bytes_accessed=9_000_000, transcendentals=0),
        name="middle",
    )(
        core[None], face, encoder, others, fields, density, speed, admittance, bound_mask,
    )

    windows = steps * slots * 2 * 2 * shots * WINDOW
    half = (depth // 2 * width_x, width_y)
    line = (8, width_y)
    total, coded, coded_other, _, _, _ = pl.pallas_call(
        functools.partial(last_kernel, capsules),
        in_specs=ins(17, 2),
        out_specs=ins(6),
        out_shape=outs(half, line, line, four, four, slab),
        scratch_shapes=[
            VMEM((6 * shots * width_x, width_y), F32), VMEM((windows, width_y), F32),
            VMEM((windows, width_y), F32),
        ],
        input_output_aliases={14: 3, 15: 4, 16: 5},
        compiler_params=params,
        name="last",
    )(
        core[None], corners, halo, others, fields, bound_mask, vel, pres, damp, pd, back,
        rows, high, low, b1, b2, grad,
    )

    groups = [list(range(c, peers, 2)) for c in range(2)]
    copies = jnp.broadcast_to(total, (peers // 2, *half))
    total = lax.all_to_all(
        copies, "shot", split_axis=0, concat_axis=0, tiled=True, axis_index_groups=groups
    ).reshape(peers // 2, *half).sum(axis=0)
    total, coded, coded_other, later = lax.optimization_barrier((total, coded, coded_other, core))
    other = lax.ppermute(jnp.concatenate([total, coded_other], axis=0), "shot", pairs)
    gradient, recording = pl.pallas_call(
        join_kernel,
        in_specs=ins(4, 1),
        out_specs=[pl.BlockSpec(memory_space=pltpu.HBM)] * 2,
        out_shape=[
            pltpu.HBM((depth * width_x, width_y), F32),
            pltpu.HBM((slots, shots, steps, channels), F32),
        ],
        scratch_shapes=[
            VMEM((slots, shots, steps, channels), F32), pltpu.SemaphoreType.DMA((3,)),
        ],
        compiler_params=params,
        name="join",
    )(later[None], total, other, coded)
    return recording, gradient.reshape(slab)


def solution(mesh):
    placed = (
        P("shot", "slab", None, None), P("shot", "slab", None, None),
        P("slab", None, None), P("slab", None, None), P("slab", None, None), P("slab", None, None),
        P("slab", None), P("slab"), P(), P("slab", "shot", None, None),
    )
    return jax.shard_map(
        body, mesh=mesh, in_specs=placed,
        out_specs=(P("slab", "shot", None, None), P("slab", None, None)),
        check_vma=False,
    )
```

```python
import functools

import jax
import jax.numpy as jnp
from jax import lax
from jax.experimental import pallas as pl
from jax.experimental.pallas import tpu as pltpu
from jax.sharding import PartitionSpec as P


LANES = 128
FAR = float(1 << 20)
WINDOW = 16
VMEM_LIMIT = 20 << 20
TINY = 16
VMEM = pltpu.VMEM
F32 = jnp.float32


def dot(a, b, contract):
    return lax.dot_general(
        a, b, ((contract[:1], contract[1:]), ((), ())), preferred_element_type=F32
    )


def halves(a):
    high = a.astype(jnp.bfloat16)
    return high, (a - high.astype(F32)).astype(jnp.bfloat16)


def side_by_side(a):
    return jnp.concatenate(halves(a), axis=1)


def doubled(onehot, axis):
    return jnp.concatenate([onehot, onehot], axis=axis)


def edge_masks(shape):
    row = lax.broadcasted_iota(jnp.int32, shape, 0)
    col = lax.broadcasted_iota(jnp.int32, shape, 1)
    return row > 0, row < shape[0] - 1, col > 0, col < shape[1] - 1


def plane_weights(vel, masks):
    low_x, high_x, low_y, high_y = masks
    xp = jnp.where(high_x, vel, 0.0)
    xm = jnp.where(low_x, pltpu.roll(vel, 1, 0), 0.0)
    yp = jnp.where(high_y, vel, 0.0)
    ym = jnp.where(low_y, pltpu.roll(vel, 1, 1), 0.0)
    return xp, xm, yp, ym, 2.0 * vel + xm + ym


def plane_part(u, weights):
    xp, xm, yp, ym, centre = weights
    rows, cols = u.shape
    return (
        xp * pltpu.roll(u, rows - 1, 0) + xm * pltpu.roll(u, 1, 0)
        + yp * pltpu.roll(u, cols - 1, 1) + ym * pltpu.roll(u, 1, 1)
        - centre * u
    )


def pick_columns(cols, width):
    return (lax.broadcasted_iota(jnp.int32, (width, cols.shape[1]), 0) == cols).astype(jnp.bfloat16)


def pick_rows(rows, count):
    return (lax.broadcasted_iota(jnp.int32, (count, rows.shape[1]), 0) == rows).astype(F32)


def split_cells(cells, width_x, width_y):
    plane = lax.div(cells, width_x * width_y)
    row = lax.div(cells, width_y)
    return plane, row, row - plane * width_x, cells - row * width_y


def in_lanes(pieces, width, fill=0.0):
    parts = []
    for piece in pieces:
        parts.append(piece)
        if piece.shape[1] < width:
            parts.append(jnp.full((1, width - piece.shape[1]), fill, piece.dtype))
    used = width * len(pieces)
    parts.append(jnp.full((1, LANES - used), fill, pieces[0].dtype))
    return jnp.concatenate(parts, axis=1)


def live_lanes(rec_live, slots, capsules):
    slot = lax.div(lax.broadcasted_iota(jnp.int32, (1, LANES), 1), capsules)
    row = jnp.zeros((1, LANES), F32)
    for r in range(slots):
        row = jnp.where(slot == r, rec_live[r].astype(F32), row)
    return row


def cell_lanes(rec_cells):
    slots, capsules = rec_cells.shape
    return in_lanes([rec_cells[r : r + 1, :] for r in range(slots)], capsules, int(FAR))


def goal_lanes(target, s, n, capsules):
    return in_lanes([target[r, s, n : n + 1, :] for r in range(target.shape[0])], capsules)


def edge_kernel(
    core_ref, live_h, cells_h, target_h, p0_h, adj_h, density_h, speed_h, admittance_h, mask_h,
    face, sent, fields, density, speed, admittance, mask, vel_s, pd_s, stack,
    both, rec_live, rec_cells, target, sems, small_sems,
):
    p0, adj = fields.at[0], fields.at[1]
    shots, depth, width_x, width_y = p0.shape
    slots, capsules = rec_cells.shape
    half = depth // 2
    last = depth - 1
    copies = []
    for side in range(2):
        some = pl.ds(side * half, half)
        pairs = [(h.at[some], v.at[some]) for h, v in (
            (density_h, density), (speed_h, speed), (admittance_h, admittance), (mask_h, mask))]
        pairs.insert(0, (p0_h.at[:, some], p0.at[:, some]))
        outmost = pl.ds(side * last, 1)
        pairs.append((adj_h.at[:, outmost], adj.at[:, outmost]))
        copies.append([
            pltpu.make_async_copy(a, b, sems.at[side, k]) for k, (a, b) in enumerate(pairs)
        ])
    inside = pl.ds(1, depth - 2)
    rest = pltpu.make_async_copy(adj_h.at[:, inside], adj.at[:, inside], small_sems.at[3])
    smalls = [
        pltpu.make_async_copy(a, b, small_sems.at[k])
        for k, (a, b) in enumerate(((live_h, rec_live), (cells_h, rec_cells), (target_h, target)))
    ]
    for copy in smalls + copies[0] + copies[1] + [rest]:
        copy.start()
    masks = edge_masks((width_x, width_y))
    for copy in smalls:
        copy.wait()
    plane, _, row_x, col = split_cells(cell_lanes(rec_cells), width_x, width_y)
    live = live_lanes(rec_live, slots, capsules)
    columns = doubled(pick_columns(col, width_y), 0)
    rows = pick_rows(row_x, width_x)
    for side in range(2):
        for copy in copies[side]:
            copy.wait()
        out = both.at[side]
        if side == 0:
            planes, lowest = (0, 1, 2), 0
        else:
            planes, lowest = (last, last - 1, last - 2), half
        near, far, third = planes
        span = range(lowest, lowest + half)
        weights, pres, damp = {}, {}, {}
        for z in span:
            vel_s[z] = 0.5 / density[z]
        for z in planes:
            spd = speed[z]
            pres[z] = 0.5 * density[z] * spd * spd
            damp[z] = 1.0 - admittance[z] * mask[z].astype(F32)
            weights[z] = plane_weights(vel_s[z], masks)
        for z in (near, far):
            pd_s[z] = pres[z] * damp[z]
        wall_low = min(near, far)
        base = side * 7 * width_x

        def put(k, value):
            stack[base + k * width_x : base + (k + 1) * width_x, :] = side_by_side(value)

        for s in range(shots):
            first = {}
            for z in planes:
                here = p0[s, z]
                total = plane_part(here, weights[z])
                if z + 1 in span:
                    total += vel_s[z] * (p0[s, z + 1] - here)
                if z - 1 in span:
                    total -= vel_s[z - 1] * (here - p0[s, z - 1])
                first[z] = damp[z] * (here + pres[z] * total)
            out[s * width_x : (s + 1) * width_x, :] = p0[s, near]
            out[(2 + s) * width_x : (3 + s) * width_x, :] = first[near]
            out[(4 + s) * width_x : (5 + s) * width_x, :] = pd_s[near] * adj[s, near]
            q_far = p0[s, far] + first[far]
            q_third = p0[s, third] + first[third]
            beyond = vel_s[min(far, third)]
            total = plane_part(q_far, weights[far]) + beyond * (q_third - q_far)
            total -= vel_s[wall_low] * q_far
            put(s, pd_s[near] * vel_s[wall_low] * q_far)
            put(4 + s, damp[far] * first[far] + pd_s[far] * total)
        out[6 * width_x : 7 * width_x, :] = vel_s[near]
        out[7 * width_x : 8 * width_x, :] = pd_s[near]
        put(2, damp[near])
        put(3, pd_s[near] * vel_s[wall_low])
        put(6, pd_s[far] * vel_s[wall_low])
        found = dot(stack[base : base + 7 * width_x, :], columns, (1, 0))
        is_near = (plane == near).astype(F32)
        is_far = (plane == far).astype(F32)

        def got(k):
            return jnp.sum(found[k * width_x : (k + 1) * width_x, :] * rows, axis=0, keepdims=True)

        tiny = [is_near * got(s) + is_far * got(4 + s) for s in range(shots)]
        tiny += [
            is_near * got(2), is_far * got(6) - is_near * got(3), is_near,
            row_x.astype(F32), col.astype(F32), live,
        ]
        tiny += [live * goal_lanes(target, s, n, capsules) for n in (1, 0) for s in range(shots)]
        tiny.append(cell_lanes(rec_cells).astype(F32))
        tiny.append(jnp.zeros((TINY - len(tiny), LANES), F32))
        start = 8 * width_x
        out[start : start + TINY, :] = jnp.zeros((TINY, width_y), F32)
        out[start : start + TINY, 0:LANES] = jnp.concatenate(tiny, axis=0)
    core = core_ref[0]
    moves = [
        pltpu.make_async_copy(both.at[core], face.at[pl.ds(0, both.shape[1])], small_sems.at[4]),
        pltpu.make_async_copy(both.at[1 - core], sent, small_sems.at[5]),
    ]
    for copy in moves:
        copy.start()
    for copy in [*moves, rest]:
        copy.wait()


def pack_kernel(got, face_in, face, sems):
    planes = got.shape[0] - TINY
    width_x = planes // 8
    second = got.shape[0]
    copies = [
        pltpu.make_async_copy(
            got.at[pl.ds(0, 6 * width_x)], face.at[pl.ds(second, 6 * width_x)], sems.at[0]
        ),
        pltpu.make_async_copy(
            got.at[pl.ds(planes, TINY)], face.at[pl.ds(second + 6 * width_x, TINY)], sems.at[1]
        ),
    ]
    for copy in copies:
        copy.start()
    for copy in copies:
        copy.wait()


def middle_kernel(
    capsules, core_ref, message, encoder, others, fields,
    density, speed, admittance, mask,
    b1, b2, vel_s, pres_s, damp_s, pd_s, back_e, grad, rows_out, code_high, code_low, corners,
    q_s, w_s,
):
    _, pair, depth, width_x, width_y = fields.shape
    shots = 2 * pair
    slots, steps, channels = corners.shape[0], 2, encoder.shape[1]
    masks = edge_masks((width_x, width_y))
    core = core_ref[0]
    half = depth // 2

    def plane_at(d):
        return d + core * (depth - 1 - 2 * d)

    def coupling(d):
        return vel_s[d + core * (depth - 2 - 2 * d)]

    def value_of(kind, s, z):
        return (others if s < pair else fields)[kind, s % pair, z]

    for z in range(depth):
        dens = density[z]
        spd = speed[z]
        pres = 0.5 * dens * spd * spd
        damp = 1.0 - admittance[z] * mask[z].astype(F32)
        vel_s[z] = 0.5 / dens
        pres_s[z] = pres
        damp_s[z] = damp
        pd_s[z] = pres * damp
    for d in range(depth - 1):
        z = plane_at(d)
        w = plane_weights(vel_s[z], masks)
        inwards, outwards = coupling(d), coupling(d - 1) if d > 0 else None
        for s in range(shots):
            here = value_of(0, s, z)
            total = plane_part(here, w) + inwards * (value_of(0, s, plane_at(d + 1)) - here)
            if d > 0:
                total += outwards * (value_of(0, s, plane_at(d - 1)) - here)
            value = here + pres_s[z] * total
            b1[s, z] = value
            q_s[s, d] = here + damp_s[z] * value
            if d <= half:
                w_s[s, d] = pd_s[z] * value_of(1, s, z)
    for d in range(depth - 2):
        z = plane_at(d)
        w = plane_weights(vel_s[z], masks)
        inwards, outwards = coupling(d), coupling(d - 1) if d > 0 else None
        sums = jnp.zeros((width_x, width_y), F32)
        for s in range(shots):
            here = q_s[s, d]
            total = plane_part(here, w) + inwards * (q_s[s, d + 1] - here)
            if d > 0:
                total += outwards * (q_s[s, d - 1] - here)
            value = damp_s[z] * b1[s, z] + pres_s[z] * total
            b2[s, z] = value
            if d >= half:
                continue
            weighted, start = w_s[s, d], value_of(1, s, z)
            back = plane_part(weighted, w) + inwards * (w_s[s, d + 1] - weighted)
            if d > 0:
                back += outwards * (w_s[s, d - 1] - weighted)
            back += damp_s[z] * start
            if d < 2:
                back_e[s, d] = back
            else:
                sums += value * start + b1[s, z] * back
        if d < half:
            grad[z] = -(mask[z].astype(F32) * sums)
        else:
            grad[z] = sums
    grad[plane_at(depth - 2)] = jnp.zeros((width_x, width_y), F32)
    lane = lax.broadcasted_iota(jnp.int32, (LANES, LANES), 1)
    line = lax.broadcasted_iota(jnp.int32, (LANES, LANES), 0)
    same = (lax.div(lane, capsules) == lax.div(line, capsules)) & (line < slots * capsules)
    code = jnp.concatenate([encoder[...], jnp.zeros((capsules, capsules - channels), F32)], axis=1)
    code = jnp.concatenate([code] * (LANES // capsules), axis=1)
    code = jnp.where(same, jnp.concatenate([code] * (LANES // capsules), axis=0), 0.0)
    square = lax.dot_general(
        code, code, (((1,), (1,)), ((), ())),
        precision=lax.Precision.HIGHEST, preferred_element_type=F32,
    )
    both = jnp.concatenate([code, square], axis=1)
    code_high[...], code_low[...] = halves(both)
    own = message[8 * width_x : 8 * width_x + TINY, 0:LANES]
    start = message.shape[0] - TINY
    other = message[start : start + TINY, 0:LANES]
    goal = []
    for n in range(steps):
        first = 10 if n == 0 else 8
        goal += [tiny[first : first + pair, :] for tiny in (other, own)]
    cells = own[12:13, :]
    slot_of = lax.div(lax.broadcasted_iota(jnp.int32, (1, LANES), 1), capsules)
    for r in range(slots):
        corners[r] = jnp.min(jnp.where(slot_of == r, cells, FAR)).astype(jnp.int32)
    goal = jnp.concatenate(goal, axis=0)
    rows_out[0:8, :] = lax.dot_general(
        goal, code, (((1,), (1,)), ((), ())),
        precision=lax.Precision.HIGHEST, preferred_element_type=F32,
    )
    rows_out[8:16, :] = jnp.concatenate(
        [cells, own[7:8, :], jnp.zeros((6, LANES), F32)], axis=0
    )


def window_part(u, vel, masks):
    low_x, high_x, low_y, high_y = masks
    rows, cols = u.shape
    flow_x = vel * (jnp.where(high_x, pltpu.roll(u, rows - 1, 0), 0.0) - u)
    flow_y = vel * (jnp.where(high_y, pltpu.roll(u, cols - 1, 1), 0.0) - u)
    fall_x = flow_x - jnp.where(low_x, pltpu.roll(flow_x, 1, 0), 0.0)
    return fall_x + flow_y - jnp.where(low_y, pltpu.roll(flow_y, 1, 1), 0.0)


def last_kernel(
    capsules, core_ref, corners, halo, others, fields, mask, vel_s, pres_s, damp_s, pd_s, back_e,
    rows_in, code_high, code_low, b1_in, b2_in, grad_in,
    out, coded, coded_other, b1, b2, grad,
    halo_s, stack, spread,
):
    _, pair, depth, width_x, width_y = fields.shape
    shots = 2 * pair
    slots = corners.shape[0]
    masks = edge_masks((width_x, width_y))
    core = core_ref[0]
    half = depth // 2
    last = depth - 1
    edge, inner = core * last, 1 + core * (last - 2)
    second = 8 * width_x + TINY

    def value_of(kind, s, z):
        return (others if s < pair else fields)[kind, s % pair, z]

    def face(k, s):
        start = (second if s >= pair else 0) + (k + s % pair) * width_x
        return halo[start : start + width_x, :]

    def rows_of(array, k, count):
        return array[k * count : (k + 1) * count, :]

    vel_h, pd_h = rows_of(halo, 6, width_x), rows_of(halo, 7, width_x)
    vel_b = jnp.where(core == 0, vel_h, vel_s[last])
    vel_in = vel_s[core * (depth - 2)]
    w_h = plane_weights(vel_h, masks)
    w_e = plane_weights(vel_s[edge], masks)
    for s in range(shots):
        here, beyond = value_of(0, s, edge), face(0, s)
        step = vel_b * (here - beyond)
        p1_h = face(2, s) + pd_h * step
        q_h = beyond + p1_h
        fixed = b1[s, edge] - pres_s[edge] * step
        change = -(pd_s[edge] * step)
        step2 = vel_b * (here + damp_s[edge] * fixed - q_h)
        halo_s[s * width_x : (s + 1) * width_x, :] = side_by_side(p1_h)
        halo_s[(shots + s) * width_x : (shots + s + 1) * width_x, :] = side_by_side(q_h)
        halo_s[(2 * shots + s) * width_x : (2 * shots + s + 1) * width_x, :] = side_by_side(
            pd_h * (plane_part(q_h, w_h) + step2)
        )
        b1[s, edge] = fixed
        total = plane_part(change, w_e) - vel_in * change - step2
        b2[s, edge] = b2[s, edge] + change + pres_s[edge] * total
        b2[s, inner] = b2[s, inner] + pres_s[inner] * (vel_in * change)

    places = []
    low, high = 2 * core, 4 + 2 * core
    for r in range(slots):
        z0 = jnp.clip(lax.div(corners[r], width_x * width_y), low, high)
        x0 = lax.rem(lax.div(corners[r], width_y), width_x)
        start = jnp.minimum(lax.div(jnp.maximum(x0 - 1, 0), 8) * 8, width_x - WINDOW)
        places.append((z0, pl.multiple_of(start, 8)))
    _, row, _, col = split_cells(rows_in[8:9, :].astype(jnp.int32), width_x, width_y)
    live = rows_in[9:10, :]
    columns = pick_columns(col, width_y)
    slot_of = lax.div(lax.broadcasted_iota(jnp.int32, (1, LANES), 1), capsules)
    line = lax.broadcasted_iota(jnp.int32, (WINDOW, LANES), 0)
    mine = jnp.zeros((1, LANES), F32)
    found_rows = {}
    for r, (z0, start) in enumerate(places):
        own = jnp.where(slot_of == r, row, -1)
        upper = jnp.where(lax.div(corners[r], width_x * width_y) >= half, 1, 0)
        mine = jnp.where(slot_of == r, jnp.where(upper == core, 1.0, 0.0), mine)
        for dz in range(2):
            first_row = (z0 + dz) * width_x + start
            found_rows[r, dz] = (line + first_row == own).astype(F32)
    index = {}
    for n, field in enumerate((b1, b2)):
        for r, (z0, start) in enumerate(places):
            for dz in range(2):
                damp = damp_s[z0 + dz, pl.ds(start, WINDOW), :]
                for s in range(shots):
                    k = index[n, r, dz, s] = len(index)
                    stack[k * WINDOW : (k + 1) * WINDOW, :] = side_by_side(
                        damp * field[s, z0 + dz, pl.ds(start, WINDOW), :]
                    )
    found = dot(stack[...], doubled(columns, 0), (1, 0))
    blank = jnp.zeros((1, LANES), F32)
    lines, goals = [], []
    for n in range(2):
        for s in range(shots):
            total = jnp.zeros((WINDOW, LANES), F32)
            for key, picked in found_rows.items():
                total += picked * rows_of(found, index[(n, *key, s)], WINDOW)
            lines.append(jnp.sum(total, axis=0, keepdims=True))
    start = 8 * width_x
    tiny = halo[start : start + TINY, 0:LANES]
    start = second + 6 * width_x
    tiny_second = halo[start : start + TINY, 0:LANES]
    near = tiny[4:5, :]
    picked = pick_rows(tiny[5:6, :].astype(jnp.int32), width_x).astype(F32)
    columns_h = pick_columns(tiny[6:7, :].astype(jnp.int32), width_y)
    rows_h = picked * near
    found = dot(halo_s[...], doubled(columns_h, 0), (1, 0))
    for s in range(shots):
        own_tiny = tiny if s < pair else tiny_second
        total = picked * (
            tiny[2:3, :] * rows_of(found, s, width_x)
            + tiny[3:4, :] * rows_of(found, shots + s, width_x)
            + near * rows_of(found, 2 * shots + s, width_x)
        )
        k = s % pair
        lines.append(own_tiny[k : k + 1, :] + jnp.sum(total, axis=0, keepdims=True))
        goals.append(own_tiny[8 + k : 9 + k, :])
    lines += [blank] * 4
    goal_high, goal_low = halves(jnp.concatenate(goals + [blank] * 4, axis=0))
    high, low = code_high[:, 0:LANES], code_low[:, 0:LANES]
    known = jnp.concatenate([
        rows_in[0:8, :],
        dot(goal_high, high, (1, 1)) + dot(goal_low, high, (1, 1)) + dot(goal_high, low, (1, 1)),
    ], axis=0)
    got_high, got_low = halves(jnp.concatenate(lines, axis=0))
    both = (
        dot(got_high, code_high[...], (1, 0)) + dot(got_low, code_high[...], (1, 0))
        + dot(got_high, code_low[...], (1, 0))
    )
    lives = jnp.concatenate([live] * 8 + [tiny[7:8, :]] * 8, axis=0)
    signals = both[0:8, 0:LANES] * (live * mine)
    for ref, first in ((coded_other, 0), (coded, pair)):
        ref[...] = jnp.zeros(ref.shape, F32)
        for n in range(2):
            ref[n * pair : (n + 1) * pair, 0:LANES] = (
                signals[n * shots + first : n * shots + first + pair, :]
            )
    source = both[:, LANES:] * lives - known

    parts = [None] * len(index)
    for (n, r, dz, s), k in index.items():
        line_of = n * shots + s
        parts[k] = side_by_side(found_rows[r, dz] * source[line_of : line_of + 1, :])
    spread[...] = dot(jnp.concatenate(parts, axis=0), doubled(columns, 1), (1, 1))
    lines = [side_by_side(rows_h * source[8 + s : 9 + s, :]) for s in range(shots)]
    placed = dot(jnp.concatenate(lines, axis=0), doubled(columns_h, 1), (1, 1))
    sums = jnp.zeros((width_x, width_y), F32)
    sums_in = jnp.zeros((width_x, width_y), F32)
    for s in range(shots):
        weighted = face(4, s) + pd_h * rows_of(placed, s, width_x)
        start = value_of(1, s, edge)
        back = back_e[s, 0] - vel_b * (pd_s[edge] * start - weighted)
        sums += b2[s, edge] * start + b1[s, edge] * back
        sums_in += b2[s, inner] * value_of(1, s, inner) + b1[s, inner] * back_e[s, 1]
    grad[edge] = -(mask[edge].astype(F32) * sums)
    grad[inner] = -(mask[inner].astype(F32) * sums_in)

    near_masks = edge_masks((WINDOW, width_y))
    for r, (z0, start) in enumerate(places):
        window = pl.ds(start, WINDOW)
        lower, upper = jnp.maximum(z0 - 1, 0), jnp.minimum(z0 + 2, last)
        vel_low = jnp.where(
            z0 > 0, vel_s[lower, window, :], halo[pl.ds(6 * width_x + start, WINDOW), :]
        )
        vel = [vel_s[z0 + dz, window, :] for dz in range(2)]
        sums = [jnp.zeros((WINDOW, width_y), F32) for _ in range(4)]
        for s in range(shots):
            now, before = [
                [rows_of(spread, index[n, r, dz, s], WINDOW) for dz in range(2)] for n in (1, 0)
            ]
            w = [pd_s[z0 + dz, window, :] * now[dz] for dz in range(2)]
            between = vel[0] * (w[1] - w[0])
            outer = [vel_low * w[0], vel[1] * w[1]]
            for dz in range(2):
                total = window_part(w[dz], vel[dz], near_masks) - outer[dz]
                total += between if dz == 0 else -between
                total += damp_s[z0 + dz, window, :] * now[dz] + before[dz]
                sums[1 + dz] += (
                    b2[s, z0 + dz, window, :] * now[dz] + b1[s, z0 + dz, window, :] * total
                )
            sums[0] += b1[s, lower, window, :] * outer[0]
            sums[3] += b1[s, upper, window, :] * outer[1]
        inside = (jnp.where(z0 > 0, 1.0, 0.0), 1.0, 1.0, jnp.where(z0 + 2 < depth, 1.0, 0.0))
        for z, total, factor in zip((lower, z0, z0 + 1, upper), sums, inside):
            wall = mask[z, window, :].astype(F32)
            grad[z, window, :] = grad[z, window, :] - factor * (wall * total)
    for z in range(half):
        out[z * width_x : (z + 1) * width_x, :] = grad[core * half + z]


def join_kernel(core, mine, other, coded, out, signals, signals_s, sems):
    half = mine.shape[0]
    start = core[0] * half
    slots, shots, steps, channels = signals_s.shape
    copies = [
        pltpu.make_async_copy(mine, out.at[pl.ds(start, half)], sems.at[0]),
        pltpu.make_async_copy(
            other.at[pl.ds(0, half)], out.at[pl.ds(half - start, half)], sems.at[1]
        ),
    ]
    for copy in copies:
        copy.start()
    total = coded[...] + other[half : half + 8, :]
    for r in range(slots):
        for s in range(shots):
            for n in range(steps):
                line = n * shots + s
                signals_s[r, s, n : n + 1, :] = total[line : line + 1, r * 32 : r * 32 + channels]
    copies.append(pltpu.make_async_copy(signals_s, signals, sems.at[2]))
    copies[-1].start()
    for copy in copies:
        copy.wait()


def body(
    pressure_init, adjoint_init, density, speed, admittance, bound_mask,
    rec_cells, rec_live, encoder, target,
):
    shots, depth, width_x, width_y = pressure_init.shape
    slots, capsules = rec_cells.shape
    steps, channels = target.shape[2:]
    slabs, peers = lax.axis_size("slab"), lax.axis_size("shot")
    field = (shots, depth, width_x, width_y)
    slab = (depth, width_x, width_y)
    message = (8 * width_x + TINY, width_y)

    def ins(count, scalars=0, far=0):
        kinds = [pltpu.SMEM] * scalars + [VMEM] * (count - scalars - far) + [pltpu.HBM] * far
        return [pl.BlockSpec(memory_space=kind) for kind in kinds]

    def outs(*shapes):
        return [
            shape if isinstance(shape, jax.ShapeDtypeStruct) else jax.ShapeDtypeStruct(shape, F32)
            for shape in shapes
        ]

    params = pltpu.CompilerParams(vmem_limit_bytes=VMEM_LIMIT)
    core = lax.rem(lax.axis_index("shot"), 2)
    longer = (message[0] + 6 * width_x + TINY, width_y)
    face, sent, fields, density, speed, admittance, bound_mask = pl.pallas_call(
        edge_kernel,
        in_specs=ins(10, 1, 9),
        out_specs=ins(7),
        out_shape=[
            VMEM(longer, F32), VMEM(message, F32), VMEM((2, *field), F32),
            VMEM(slab, F32), VMEM(slab, F32), VMEM(slab, F32), VMEM(slab, jnp.int32),
        ],
        scratch_shapes=[
            VMEM(slab, F32), VMEM(slab, F32), VMEM((14 * width_x, 2 * width_y), jnp.bfloat16),
            VMEM((2, *message), F32),
            pltpu.SMEM(rec_live.shape, jnp.int32), VMEM(rec_cells.shape, jnp.int32),
            VMEM(target.shape, F32),
            pltpu.SemaphoreType.DMA((2, 6)), pltpu.SemaphoreType.DMA((6,)),
        ],
        compiler_params=params,
        name="edge",
    )(
        core[None],
        *[
            pltpu.with_memory_space_constraint(array, pltpu.HBM)
            for array in (
                rec_live, rec_cells, target,
                pressure_init, adjoint_init, density, speed, admittance, bound_mask,
            )
        ],
    )

    pairs = [(i, i ^ 1) for i in range(peers)]
    facing = []
    for i in range(slabs - 1):
        for j in range(0, peers, 2):
            ends = (i * peers + j + 1, (i + 1) * peers + j)
            facing += [ends, ends[::-1]]
    got = lax.ppermute(sent, "shot", pairs)
    others = lax.ppermute(fields, "shot", pairs)
    face = pl.pallas_call(
        pack_kernel,
        in_specs=ins(2),
        out_specs=pl.BlockSpec(memory_space=VMEM),
        out_shape=VMEM(longer, F32),
        scratch_shapes=[pltpu.SemaphoreType.DMA((2,))],
        input_output_aliases={1: 0},
        compiler_params=params,
        name="pack",
    )(got, face)
    halo = lax.ppermute(face, ("slab", "shot"), facing)

    table = jax.ShapeDtypeStruct((LANES, 2 * LANES), jnp.bfloat16)
    four = (2 * shots, *slab)
    rows_plane = (width_x, width_y)
    b1, b2, vel, pres, damp, pd, back, grad, rows, high, low, corners = pl.pallas_call(
        functools.partial(middle_kernel, capsules),
        in_specs=ins(9, 1),
        out_specs=[*ins(11), *ins(1, 1)],
        out_shape=outs(
            four, four, slab, slab, slab, slab, (2 * shots, 2, *rows_plane), slab,
            (16, LANES), table, table, jax.ShapeDtypeStruct((slots,), jnp.int32),
        ),
        scratch_shapes=[
            VMEM((2 * shots, depth - 1, *rows_plane), F32),
            VMEM((2 * shots, depth // 2 + 1, *rows_plane), F32),
        ],
        compiler_params=params,
        cost_estimate=pl.CostEstimate(flops=30_000_000, bytes_accessed=9_000_000, transcendentals=0),
        name="middle",
    )(
        core[None], face, encoder, others, fields, density, speed, admittance, bound_mask,
    )

    windows = steps * slots * 2 * 2 * shots * WINDOW
    half = (depth // 2 * width_x, width_y)
    line = (8, width_y)
    total, coded, coded_other, _, _, _ = pl.pallas_call(
        functools.partial(last_kernel, capsules),
        in_specs=ins(17, 2),
        out_specs=ins(6),
        out_shape=outs(half, line, line, four, four, slab),
        scratch_shapes=[
            VMEM((6 * shots * width_x, 2 * width_y), jnp.bfloat16),
            VMEM((windows, 2 * width_y), jnp.bfloat16), VMEM((windows, width_y), F32),
        ],
        input_output_aliases={14: 3, 15: 4, 16: 5},
        compiler_params=params,
        name="last",
    )(
        core[None], corners, halo, others, fields, bound_mask, vel, pres, damp, pd, back,
        rows, high, low, b1, b2, grad,
    )

    groups = [list(range(c, peers, 2)) for c in range(2)]
    copies = jnp.broadcast_to(total, (peers // 2, *half))
    total = lax.all_to_all(
        copies, "shot", split_axis=0, concat_axis=0, tiled=True, axis_index_groups=groups
    ).reshape(peers // 2, *half).sum(axis=0)
    total, coded, coded_other, later = lax.optimization_barrier((total, coded, coded_other, core))
    other = lax.ppermute(jnp.concatenate([total, coded_other], axis=0), "shot", pairs)
    gradient, recording = pl.pallas_call(
        join_kernel,
        in_specs=ins(4, 1),
        out_specs=[pl.BlockSpec(memory_space=pltpu.HBM)] * 2,
        out_shape=[
            pltpu.HBM((depth * width_x, width_y), F32),
            pltpu.HBM((slots, shots, steps, channels), F32),
        ],
        scratch_shapes=[
            VMEM((slots, shots, steps, channels), F32), pltpu.SemaphoreType.DMA((3,)),
        ],
        compiler_params=params,
        name="join",
    )(later[None], total, other, coded)
    return recording, gradient.reshape(slab)


def solution(mesh):
    placed = (
        P("shot", "slab", None, None), P("shot", "slab", None, None),
        P("slab", None, None), P("slab", None, None), P("slab", None, None), P("slab", None, None),
        P("slab", None), P("slab"), P(), P("slab", "shot", None, None),
    )
    return jax.shard_map(
        body, mesh=mesh, in_specs=placed,
        out_specs=(P("slab", "shot", None, None), P("slab", None, None)),
        check_vma=False,
    )
```

```python
import functools

import jax
import jax.numpy as jnp
from jax import lax
from jax.experimental import pallas as pl
from jax.experimental.pallas import tpu as pltpu
from jax.sharding import PartitionSpec as P


LANES = 128
FAR = float(1 << 20)
WINDOW = 16
VMEM_LIMIT = 20 << 20
TINY = 16
VMEM = pltpu.VMEM
F32 = jnp.float32


def dot(a, b, contract):
    return lax.dot_general(
        a, b, ((contract[:1], contract[1:]), ((), ())), preferred_element_type=F32
    )


def halves(a):
    high = a.astype(jnp.bfloat16)
    return high, (a - high.astype(F32)).astype(jnp.bfloat16)


def side_by_side(a):
    return jnp.concatenate(halves(a), axis=1)


def doubled(onehot, axis):
    return jnp.concatenate([onehot, onehot], axis=axis)


def edge_masks(shape):
    row = lax.broadcasted_iota(jnp.int32, shape, 0)
    col = lax.broadcasted_iota(jnp.int32, shape, 1)
    return row > 0, row < shape[0] - 1, col > 0, col < shape[1] - 1


def plane_weights(vel, masks):
    low_x, high_x, low_y, high_y = masks
    xp = jnp.where(high_x, vel, 0.0)
    xm = jnp.where(low_x, pltpu.roll(vel, 1, 0), 0.0)
    yp = jnp.where(high_y, vel, 0.0)
    ym = jnp.where(low_y, pltpu.roll(vel, 1, 1), 0.0)
    return xp, xm, yp, ym, 2.0 * vel + xm + ym


def plane_part(u, weights):
    xp, xm, yp, ym, centre = weights
    rows, cols = u.shape
    return (
        xp * pltpu.roll(u, rows - 1, 0) + xm * pltpu.roll(u, 1, 0)
        + yp * pltpu.roll(u, cols - 1, 1) + ym * pltpu.roll(u, 1, 1)
        - centre * u
    )


def pick_columns(cols, width):
    return (lax.broadcasted_iota(jnp.int32, (width, cols.shape[1]), 0) == cols).astype(jnp.bfloat16)


def pick_rows(rows, count):
    return (lax.broadcasted_iota(jnp.int32, (count, rows.shape[1]), 0) == rows).astype(F32)


def split_cells(cells, width_x, width_y):
    plane = lax.div(cells, width_x * width_y)
    row = lax.div(cells, width_y)
    return plane, row, row - plane * width_x, cells - row * width_y


def in_lanes(pieces, width, fill=0.0):
    parts = []
    for piece in pieces:
        parts.append(piece)
        if piece.shape[1] < width:
            parts.append(jnp.full((1, width - piece.shape[1]), fill, piece.dtype))
    used = width * len(pieces)
    parts.append(jnp.full((1, LANES - used), fill, pieces[0].dtype))
    return jnp.concatenate(parts, axis=1)


def live_lanes(rec_live, slots, capsules):
    slot = lax.div(lax.broadcasted_iota(jnp.int32, (1, LANES), 1), capsules)
    row = jnp.zeros((1, LANES), F32)
    for r in range(slots):
        row = jnp.where(slot == r, rec_live[r].astype(F32), row)
    return row


def cell_lanes(rec_cells):
    slots, capsules = rec_cells.shape
    return in_lanes([rec_cells[r : r + 1, :] for r in range(slots)], capsules, int(FAR))


def goal_lanes(target, s, n, capsules):
    return in_lanes([target[r, s, n : n + 1, :] for r in range(target.shape[0])], capsules)


def edge_kernel(
    core_ref, live_h, cells_h, target_h, p0_h, adj_h, density_h, speed_h, admittance_h, mask_h,
    face, sent, fields, density, speed, admittance, mask, vel_s, pd_s, stack,
    both, rec_live, rec_cells, target, sems, small_sems,
):
    p0, adj = fields.at[0], fields.at[1]
    shots, depth, width_x, width_y = p0.shape
    slots, capsules = rec_cells.shape
    half = depth // 2
    last = depth - 1
    copies = []
    for side in range(2):
        some = pl.ds(side * half, half)
        pairs = [(h.at[some], v.at[some]) for h, v in (
            (density_h, density), (speed_h, speed), (admittance_h, admittance), (mask_h, mask))]
        pairs.insert(0, (p0_h.at[:, some], p0.at[:, some]))
        outmost = pl.ds(side * last, 1)
        pairs.append((adj_h.at[:, outmost], adj.at[:, outmost]))
        copies.append([
            pltpu.make_async_copy(a, b, sems.at[side, k]) for k, (a, b) in enumerate(pairs)
        ])
    inside = pl.ds(1, depth - 2)
    rest = pltpu.make_async_copy(adj_h.at[:, inside], adj.at[:, inside], small_sems.at[3])
    smalls = [
        pltpu.make_async_copy(a, b, small_sems.at[k])
        for k, (a, b) in enumerate(((live_h, rec_live), (cells_h, rec_cells), (target_h, target)))
    ]
    for copy in smalls + copies[0] + copies[1] + [rest]:
        copy.start()
    masks = edge_masks((width_x, width_y))
    for copy in smalls:
        copy.wait()
    plane, _, row_x, col = split_cells(cell_lanes(rec_cells), width_x, width_y)
    live = live_lanes(rec_live, slots, capsules)
    columns = doubled(pick_columns(col, width_y), 0)
    rows = pick_rows(row_x, width_x)
    for side in range(2):
        for copy in copies[side]:
            copy.wait()
        out = both.at[side]
        if side == 0:
            planes, lowest = (0, 1, 2), 0
        else:
            planes, lowest = (last, last - 1, last - 2), half
        near, far, third = planes
        span = range(lowest, lowest + half)
        weights, pres, damp = {}, {}, {}
        for z in span:
            vel_s[z] = 0.5 / density[z]
        for z in planes:
            spd = speed[z]
            pres[z] = 0.5 * density[z] * spd * spd
            damp[z] = 1.0 - admittance[z] * mask[z].astype(F32)
            weights[z] = plane_weights(vel_s[z], masks)
        for z in (near, far):
            pd_s[z] = pres[z] * damp[z]
        wall_low = min(near, far)
        base = side * 7 * width_x

        def put(k, value):
            stack[base + k * width_x : base + (k + 1) * width_x, :] = side_by_side(value)

        for s in range(shots):
            first = {}
            for z in planes:
                here = p0[s, z]
                total = plane_part(here, weights[z])
                if z + 1 in span:
                    total += vel_s[z] * (p0[s, z + 1] - here)
                if z - 1 in span:
                    total -= vel_s[z - 1] * (here - p0[s, z - 1])
                first[z] = damp[z] * (here + pres[z] * total)
            out[s * width_x : (s + 1) * width_x, :] = p0[s, near]
            out[(2 + s) * width_x : (3 + s) * width_x, :] = first[near]
            out[(4 + s) * width_x : (5 + s) * width_x, :] = pd_s[near] * adj[s, near]
            q_far = p0[s, far] + first[far]
            q_third = p0[s, third] + first[third]
            beyond = vel_s[min(far, third)]
            total = plane_part(q_far, weights[far]) + beyond * (q_third - q_far)
            total -= vel_s[wall_low] * q_far
            put(s, pd_s[near] * vel_s[wall_low] * q_far)
            put(4 + s, damp[far] * first[far] + pd_s[far] * total)
        out[6 * width_x : 7 * width_x, :] = vel_s[near]
        out[7 * width_x : 8 * width_x, :] = pd_s[near]
        put(2, damp[near])
        put(3, pd_s[near] * vel_s[wall_low])
        put(6, pd_s[far] * vel_s[wall_low])
        found = dot(stack[base : base + 7 * width_x, :], columns, (1, 0))
        is_near = (plane == near).astype(F32)
        is_far = (plane == far).astype(F32)

        def got(k):
            return jnp.sum(found[k * width_x : (k + 1) * width_x, :] * rows, axis=0, keepdims=True)

        tiny = [is_near * got(s) + is_far * got(4 + s) for s in range(shots)]
        tiny += [
            is_near * got(2), is_far * got(6) - is_near * got(3), is_near,
            row_x.astype(F32), col.astype(F32), live,
        ]
        tiny += [live * goal_lanes(target, s, n, capsules) for n in (1, 0) for s in range(shots)]
        tiny.append(cell_lanes(rec_cells).astype(F32))
        tiny.append(jnp.zeros((TINY - len(tiny), LANES), F32))
        start = 8 * width_x
        out[start : start + TINY, :] = jnp.zeros((TINY, width_y), F32)
        out[start : start + TINY, 0:LANES] = jnp.concatenate(tiny, axis=0)
    core = core_ref[0]
    moves = [
        pltpu.make_async_copy(both.at[core], face.at[pl.ds(0, both.shape[1])], small_sems.at[4]),
        pltpu.make_async_copy(both.at[1 - core], sent, small_sems.at[5]),
    ]
    for copy in moves:
        copy.start()
    for copy in [*moves, rest]:
        copy.wait()


def pack_kernel(got, face_in, face, sems):
    planes = got.shape[0] - TINY
    width_x = planes // 8
    second = got.shape[0]
    copies = [
        pltpu.make_async_copy(
            got.at[pl.ds(0, 6 * width_x)], face.at[pl.ds(second, 6 * width_x)], sems.at[0]
        ),
        pltpu.make_async_copy(
            got.at[pl.ds(planes, TINY)], face.at[pl.ds(second + 6 * width_x, TINY)], sems.at[1]
        ),
    ]
    for copy in copies:
        copy.start()
    for copy in copies:
        copy.wait()


def two_steps(
    core, fields, mask, vel_s, pres_s, damp_s, pd_s, b1, b2, back_e, q_s, w_s, grad, known
):
    _, shots, depth, width_x, width_y = fields.shape
    masks = edge_masks((width_x, width_y))
    half = depth // 2

    def plane_at(d):
        return d + core * (depth - 1 - 2 * d)

    def coupling(d):
        return vel_s[d + core * (depth - 2 - 2 * d)]

    for d in range(depth - 1):
        z = plane_at(d)
        w = plane_weights(vel_s[z], masks)
        inwards, outwards = coupling(d), coupling(d - 1) if d > 0 else None
        for s in range(shots):
            here = fields[0, s, z]
            total = plane_part(here, w) + inwards * (fields[0, s, plane_at(d + 1)] - here)
            if d > 0:
                total += outwards * (fields[0, s, plane_at(d - 1)] - here)
            value = here + pres_s[z] * total
            b1[s, z] = value
            q_s[s, d] = here + damp_s[z] * value
            if d <= half:
                w_s[s, d] = pd_s[z] * fields[1, s, z]
    for d in range(depth - 2):
        z = plane_at(d)
        w = plane_weights(vel_s[z], masks)
        inwards, outwards = coupling(d), coupling(d - 1) if d > 0 else None
        sums = jnp.zeros((width_x, width_y), F32)
        for s in range(shots):
            here = q_s[s, d]
            total = plane_part(here, w) + inwards * (q_s[s, d + 1] - here)
            if d > 0:
                total += outwards * (q_s[s, d - 1] - here)
            value = damp_s[z] * b1[s, z] + pres_s[z] * total
            b2[s, z] = value
            if d >= half:
                continue
            weighted, start = w_s[s, d], fields[1, s, z]
            back = plane_part(weighted, w) + inwards * (w_s[s, d + 1] - weighted)
            if d > 0:
                back += outwards * (w_s[s, d - 1] - weighted)
            back += damp_s[z] * start
            if d < 2:
                back_e[s, d] = back
            else:
                sums += value * start + b1[s, z] * back
        sums = -(mask[z].astype(F32) * sums) if d < half else sums
        grad[z] = sums if known is None else known[z] + sums
    grad[plane_at(depth - 2)] = jnp.zeros((width_x, width_y), F32)


def other_kernel(
    core_ref, fields, mask, vel_s, pres_s, damp_s, pd_s, known, b1, b2, back_e, grad, q_s, w_s
):
    two_steps(core_ref[0], fields, mask, vel_s, pres_s, damp_s, pd_s, b1, b2, back_e, q_s, w_s, grad, known)


def middle_kernel(
    capsules, core_ref, message, encoder, fields, density, speed, admittance, mask,
    b1, b2, vel_s, pres_s, damp_s, pd_s, back_e, grad, rows_out, code_high, code_low, corners,
    q_s, w_s,
):
    _, pair, depth, width_x, _ = fields.shape
    slots, steps, channels = corners.shape[0], 2, encoder.shape[1]
    for z in range(depth):
        dens = density[z]
        spd = speed[z]
        pres = 0.5 * dens * spd * spd
        damp = 1.0 - admittance[z] * mask[z].astype(F32)
        vel_s[z] = 0.5 / dens
        pres_s[z] = pres
        damp_s[z] = damp
        pd_s[z] = pres * damp
    two_steps(core_ref[0], fields, mask, vel_s, pres_s, damp_s, pd_s, b1, b2, back_e, q_s, w_s, grad, None)
    lane = lax.broadcasted_iota(jnp.int32, (LANES, LANES), 1)
    line = lax.broadcasted_iota(jnp.int32, (LANES, LANES), 0)
    same = (lax.div(lane, capsules) == lax.div(line, capsules)) & (line < slots * capsules)
    code = jnp.concatenate([encoder[...], jnp.zeros((capsules, capsules - channels), F32)], axis=1)
    code = jnp.concatenate([code] * (LANES // capsules), axis=1)
    code = jnp.where(same, jnp.concatenate([code] * (LANES // capsules), axis=0), 0.0)
    square = lax.dot_general(
        code, code, (((1,), (1,)), ((), ())),
        precision=lax.Precision.HIGHEST, preferred_element_type=F32,
    )
    both = jnp.concatenate([code, square], axis=1)
    code_high[...], code_low[...] = halves(both)
    own = message[8 * width_x : 8 * width_x + TINY, 0:LANES]
    start = message.shape[0] - TINY
    other = message[start : start + TINY, 0:LANES]
    goal = []
    for n in range(steps):
        first = 10 if n == 0 else 8
        goal += [tiny[first : first + pair, :] for tiny in (other, own)]
    cells = own[12:13, :]
    slot_of = lax.div(lax.broadcasted_iota(jnp.int32, (1, LANES), 1), capsules)
    for r in range(slots):
        corners[r] = jnp.min(jnp.where(slot_of == r, cells, FAR)).astype(jnp.int32)
    goal = jnp.concatenate(goal, axis=0)
    rows_out[0:8, :] = lax.dot_general(
        goal, code, (((1,), (1,)), ((), ())),
        precision=lax.Precision.HIGHEST, preferred_element_type=F32,
    )
    rows_out[8:16, :] = jnp.concatenate(
        [cells, own[7:8, :], jnp.zeros((6, LANES), F32)], axis=0
    )


def window_part(u, vel, masks):
    low_x, high_x, low_y, high_y = masks
    rows, cols = u.shape
    flow_x = vel * (jnp.where(high_x, pltpu.roll(u, rows - 1, 0), 0.0) - u)
    flow_y = vel * (jnp.where(high_y, pltpu.roll(u, cols - 1, 1), 0.0) - u)
    fall_x = flow_x - jnp.where(low_x, pltpu.roll(flow_x, 1, 0), 0.0)
    return fall_x + flow_y - jnp.where(low_y, pltpu.roll(flow_y, 1, 1), 0.0)


def last_kernel(
    capsules, core_ref, corners, halo, others, fields, mask, vel_s, pres_s, damp_s, pd_s, back_e,
    back_o, rows_in, code_high, code_low, b1_in, b2_in, b1_own_in, b2_own_in, grad_in,
    out, coded, coded_other, b1_other, b2_other, b1_own, b2_own, grad,
    halo_s, stack, spread,
):
    _, pair, depth, width_x, width_y = fields.shape
    shots = 2 * pair
    slots = corners.shape[0]
    masks = edge_masks((width_x, width_y))
    core = core_ref[0]
    half = depth // 2
    last = depth - 1
    edge, inner = core * last, 1 + core * (last - 2)
    second = 8 * width_x + TINY

    def value_of(kind, s, z):
        return (others if s < pair else fields)[kind, s % pair, z]

    def edge_back(s, d):
        return (back_e if s < pair else back_o)[s % pair, d]

    def b1(s):
        return (b1_other if s < pair else b1_own).at[s % pair]

    def b2(s):
        return (b2_other if s < pair else b2_own).at[s % pair]

    def face(k, s):
        start = (second if s >= pair else 0) + (k + s % pair) * width_x
        return halo[start : start + width_x, :]

    def rows_of(array, k, count):
        return array[k * count : (k + 1) * count, :]

    vel_h, pd_h = rows_of(halo, 6, width_x), rows_of(halo, 7, width_x)
    vel_b = jnp.where(core == 0, vel_h, vel_s[last])
    vel_in = vel_s[core * (depth - 2)]
    w_h = plane_weights(vel_h, masks)
    w_e = plane_weights(vel_s[edge], masks)
    for s in range(shots):
        here, beyond = value_of(0, s, edge), face(0, s)
        step = vel_b * (here - beyond)
        p1_h = face(2, s) + pd_h * step
        q_h = beyond + p1_h
        fixed = b1(s)[edge] - pres_s[edge] * step
        change = -(pd_s[edge] * step)
        step2 = vel_b * (here + damp_s[edge] * fixed - q_h)
        halo_s[s * width_x : (s + 1) * width_x, :] = side_by_side(p1_h)
        halo_s[(shots + s) * width_x : (shots + s + 1) * width_x, :] = side_by_side(q_h)
        halo_s[(2 * shots + s) * width_x : (2 * shots + s + 1) * width_x, :] = side_by_side(
            pd_h * (plane_part(q_h, w_h) + step2)
        )
        b1(s)[edge] = fixed
        total = plane_part(change, w_e) - vel_in * change - step2
        b2(s)[edge] = b2(s)[edge] + change + pres_s[edge] * total
        b2(s)[inner] = b2(s)[inner] + pres_s[inner] * (vel_in * change)

    places = []
    low, high = 2 * core, 4 + 2 * core
    for r in range(slots):
        z0 = jnp.clip(lax.div(corners[r], width_x * width_y), low, high)
        x0 = lax.rem(lax.div(corners[r], width_y), width_x)
        start = jnp.minimum(lax.div(jnp.maximum(x0 - 1, 0), 8) * 8, width_x - WINDOW)
        places.append((z0, pl.multiple_of(start, 8)))
    _, row, _, col = split_cells(rows_in[8:9, :].astype(jnp.int32), width_x, width_y)
    live = rows_in[9:10, :]
    columns = pick_columns(col, width_y)
    slot_of = lax.div(lax.broadcasted_iota(jnp.int32, (1, LANES), 1), capsules)
    line = lax.broadcasted_iota(jnp.int32, (WINDOW, LANES), 0)
    mine = jnp.zeros((1, LANES), F32)
    found_rows = {}
    for r, (z0, start) in enumerate(places):
        own = jnp.where(slot_of == r, row, -1)
        upper = jnp.where(lax.div(corners[r], width_x * width_y) >= half, 1, 0)
        mine = jnp.where(slot_of == r, jnp.where(upper == core, 1.0, 0.0), mine)
        for dz in range(2):
            first_row = (z0 + dz) * width_x + start
            found_rows[r, dz] = (line + first_row == own).astype(F32)
    index = {}
    for n, field in enumerate((b1, b2)):
        for r, (z0, start) in enumerate(places):
            for dz in range(2):
                damp = damp_s[z0 + dz, pl.ds(start, WINDOW), :]
                for s in range(shots):
                    k = index[n, r, dz, s] = len(index)
                    stack[k * WINDOW : (k + 1) * WINDOW, :] = side_by_side(
                        damp * field(s)[z0 + dz, pl.ds(start, WINDOW), :]
                    )
    found = dot(stack[...], doubled(columns, 0), (1, 0))
    blank = jnp.zeros((1, LANES), F32)
    lines, goals = [], []
    for n in range(2):
        for s in range(shots):
            total = jnp.zeros((WINDOW, LANES), F32)
            for key, picked in found_rows.items():
                total += picked * rows_of(found, index[(n, *key, s)], WINDOW)
            lines.append(jnp.sum(total, axis=0, keepdims=True))
    start = 8 * width_x
    tiny = halo[start : start + TINY, 0:LANES]
    start = second + 6 * width_x
    tiny_second = halo[start : start + TINY, 0:LANES]
    near = tiny[4:5, :]
    picked = pick_rows(tiny[5:6, :].astype(jnp.int32), width_x).astype(F32)
    columns_h = pick_columns(tiny[6:7, :].astype(jnp.int32), width_y)
    rows_h = picked * near
    found = dot(halo_s[...], doubled(columns_h, 0), (1, 0))
    for s in range(shots):
        own_tiny = tiny if s < pair else tiny_second
        total = picked * (
            tiny[2:3, :] * rows_of(found, s, width_x)
            + tiny[3:4, :] * rows_of(found, shots + s, width_x)
            + near * rows_of(found, 2 * shots + s, width_x)
        )
        k = s % pair
        lines.append(own_tiny[k : k + 1, :] + jnp.sum(total, axis=0, keepdims=True))
        goals.append(own_tiny[8 + k : 9 + k, :])
    lines += [blank] * 4
    goal_high, goal_low = halves(jnp.concatenate(goals + [blank] * 4, axis=0))
    high, low = code_high[:, 0:LANES], code_low[:, 0:LANES]
    known = jnp.concatenate([
        rows_in[0:8, :],
        dot(goal_high, high, (1, 1)) + dot(goal_low, high, (1, 1)) + dot(goal_high, low, (1, 1)),
    ], axis=0)
    got_high, got_low = halves(jnp.concatenate(lines, axis=0))
    both = (
        dot(got_high, code_high[...], (1, 0)) + dot(got_low, code_high[...], (1, 0))
        + dot(got_high, code_low[...], (1, 0))
    )
    lives = jnp.concatenate([live] * 8 + [tiny[7:8, :]] * 8, axis=0)
    signals = both[0:8, 0:LANES] * (live * mine)
    for ref, first in ((coded_other, 0), (coded, pair)):
        ref[...] = jnp.zeros(ref.shape, F32)
        for n in range(2):
            ref[n * pair : (n + 1) * pair, 0:LANES] = (
                signals[n * shots + first : n * shots + first + pair, :]
            )
    source = both[:, LANES:] * lives - known

    parts = [None] * len(index)
    for (n, r, dz, s), k in index.items():
        line_of = n * shots + s
        parts[k] = side_by_side(found_rows[r, dz] * source[line_of : line_of + 1, :])
    spread[...] = dot(jnp.concatenate(parts, axis=0), doubled(columns, 1), (1, 1))
    lines = [side_by_side(rows_h * source[8 + s : 9 + s, :]) for s in range(shots)]
    placed = dot(jnp.concatenate(lines, axis=0), doubled(columns_h, 1), (1, 1))
    sums = jnp.zeros((width_x, width_y), F32)
    sums_in = jnp.zeros((width_x, width_y), F32)
    for s in range(shots):
        weighted = face(4, s) + pd_h * rows_of(placed, s, width_x)
        start = value_of(1, s, edge)
        back = edge_back(s, 0) - vel_b * (pd_s[edge] * start - weighted)
        sums += b2(s)[edge] * start + b1(s)[edge] * back
        sums_in += b2(s)[inner] * value_of(1, s, inner) + b1(s)[inner] * edge_back(s, 1)
    grad[edge] = -(mask[edge].astype(F32) * sums)
    grad[inner] = -(mask[inner].astype(F32) * sums_in)

    near_masks = edge_masks((WINDOW, width_y))
    for r, (z0, start) in enumerate(places):
        window = pl.ds(start, WINDOW)
        lower, upper = jnp.maximum(z0 - 1, 0), jnp.minimum(z0 + 2, last)
        vel_low = jnp.where(
            z0 > 0, vel_s[lower, window, :], halo[pl.ds(6 * width_x + start, WINDOW), :]
        )
        vel = [vel_s[z0 + dz, window, :] for dz in range(2)]
        sums = [jnp.zeros((WINDOW, width_y), F32) for _ in range(4)]
        for s in range(shots):
            now, before = [
                [rows_of(spread, index[n, r, dz, s], WINDOW) for dz in range(2)] for n in (1, 0)
            ]
            w = [pd_s[z0 + dz, window, :] * now[dz] for dz in range(2)]
            between = vel[0] * (w[1] - w[0])
            outer = [vel_low * w[0], vel[1] * w[1]]
            for dz in range(2):
                total = window_part(w[dz], vel[dz], near_masks) - outer[dz]
                total += between if dz == 0 else -between
                total += damp_s[z0 + dz, window, :] * now[dz] + before[dz]
                sums[1 + dz] += (
                    b2(s)[z0 + dz, window, :] * now[dz] + b1(s)[z0 + dz, window, :] * total
                )
            sums[0] += b1(s)[lower, window, :] * outer[0]
            sums[3] += b1(s)[upper, window, :] * outer[1]
        inside = (jnp.where(z0 > 0, 1.0, 0.0), 1.0, 1.0, jnp.where(z0 + 2 < depth, 1.0, 0.0))
        for z, total, factor in zip((lower, z0, z0 + 1, upper), sums, inside):
            wall = mask[z, window, :].astype(F32)
            grad[z, window, :] = grad[z, window, :] - factor * (wall * total)
    for z in range(half):
        out[z * width_x : (z + 1) * width_x, :] = grad[core * half + z]


def join_kernel(core, mine, other, coded, out, signals, signals_s, sems):
    half = mine.shape[0]
    start = core[0] * half
    slots, shots, steps, channels = signals_s.shape
    copies = [
        pltpu.make_async_copy(mine, out.at[pl.ds(start, half)], sems.at[0]),
        pltpu.make_async_copy(
            other.at[pl.ds(0, half)], out.at[pl.ds(half - start, half)], sems.at[1]
        ),
    ]
    for copy in copies:
        copy.start()
    total = coded[...] + other[half : half + 8, :]
    for r in range(slots):
        for s in range(shots):
            for n in range(steps):
                line = n * shots + s
                signals_s[r, s, n : n + 1, :] = total[line : line + 1, r * 32 : r * 32 + channels]
    copies.append(pltpu.make_async_copy(signals_s, signals, sems.at[2]))
    copies[-1].start()
    for copy in copies:
        copy.wait()


def body(
    pressure_init, adjoint_init, density, speed, admittance, bound_mask,
    rec_cells, rec_live, encoder, target,
):
    shots, depth, width_x, width_y = pressure_init.shape
    slots, capsules = rec_cells.shape
    steps, channels = target.shape[2:]
    slabs, peers = lax.axis_size("slab"), lax.axis_size("shot")
    field = (shots, depth, width_x, width_y)
    slab = (depth, width_x, width_y)
    message = (8 * width_x + TINY, width_y)

    def ins(count, scalars=0, far=0):
        kinds = [pltpu.SMEM] * scalars + [VMEM] * (count - scalars - far) + [pltpu.HBM] * far
        return [pl.BlockSpec(memory_space=kind) for kind in kinds]

    def outs(*shapes):
        return [
            shape if isinstance(shape, jax.ShapeDtypeStruct) else jax.ShapeDtypeStruct(shape, F32)
            for shape in shapes
        ]

    params = pltpu.CompilerParams(vmem_limit_bytes=VMEM_LIMIT)
    core = lax.rem(lax.axis_index("shot"), 2)
    longer = (message[0] + 6 * width_x + TINY, width_y)
    face, sent, fields, density, speed, admittance, bound_mask = pl.pallas_call(
        edge_kernel,
        in_specs=ins(10, 1, 9),
        out_specs=ins(7),
        out_shape=[
            VMEM(longer, F32), VMEM(message, F32), VMEM((2, *field), F32),
            VMEM(slab, F32), VMEM(slab, F32), VMEM(slab, F32), VMEM(slab, jnp.int32),
        ],
        scratch_shapes=[
            VMEM(slab, F32), VMEM(slab, F32), VMEM((14 * width_x, 2 * width_y), jnp.bfloat16),
            VMEM((2, *message), F32),
            pltpu.SMEM(rec_live.shape, jnp.int32), VMEM(rec_cells.shape, jnp.int32),
            VMEM(target.shape, F32),
            pltpu.SemaphoreType.DMA((2, 6)), pltpu.SemaphoreType.DMA((6,)),
        ],
        compiler_params=params,
        name="edge",
    )(
        core[None],
        *[
            pltpu.with_memory_space_constraint(array, pltpu.HBM)
            for array in (
                rec_live, rec_cells, target,
                pressure_init, adjoint_init, density, speed, admittance, bound_mask,
            )
        ],
    )

    pairs = [(i, i ^ 1) for i in range(peers)]
    facing = []
    for i in range(slabs - 1):
        for j in range(0, peers, 2):
            ends = (i * peers + j + 1, (i + 1) * peers + j)
            facing += [ends, ends[::-1]]
    got = lax.ppermute(sent, "shot", pairs)
    others = lax.ppermute(fields, "shot", pairs)
    face = pl.pallas_call(
        pack_kernel,
        in_specs=ins(2),
        out_specs=pl.BlockSpec(memory_space=VMEM),
        out_shape=VMEM(longer, F32),
        scratch_shapes=[pltpu.SemaphoreType.DMA((2,))],
        input_output_aliases={1: 0},
        compiler_params=params,
        name="pack",
    )(got, face)
    halo = lax.ppermute(face, ("slab", "shot"), facing)

    table = jax.ShapeDtypeStruct((LANES, 2 * LANES), jnp.bfloat16)
    rows_plane = (width_x, width_y)
    edge_planes = (shots, 2, *rows_plane)
    work = [
        VMEM((shots, depth - 1, *rows_plane), F32),
        VMEM((shots, depth // 2 + 1, *rows_plane), F32),
    ]
    cost = pl.CostEstimate(flops=15_000_000, bytes_accessed=5_000_000, transcendentals=0)
    b1, b2, vel, pres, damp, pd, back, grad, rows, high, low, corners = pl.pallas_call(
        functools.partial(middle_kernel, capsules),
        in_specs=ins(8, 1),
        out_specs=[*ins(11), *ins(1, 1)],
        out_shape=outs(
            field, field, slab, slab, slab, slab, edge_planes, slab,
            (16, LANES), table, table, jax.ShapeDtypeStruct((slots,), jnp.int32),
        ),
        scratch_shapes=work,
        compiler_params=params,
        cost_estimate=cost,
        name="middle",
    )(core[None], face, encoder, fields, density, speed, admittance, bound_mask)
    b1_other, b2_other, back_other, grad = pl.pallas_call(
        other_kernel,
        in_specs=ins(8, 1),
        out_specs=ins(4),
        out_shape=outs(field, field, edge_planes, slab),
        scratch_shapes=work,
        compiler_params=params,
        cost_estimate=cost,
        name="other",
    )(core[None], others, bound_mask, vel, pres, damp, pd, grad)

    windows = steps * slots * 2 * 2 * shots * WINDOW
    half = (depth // 2 * width_x, width_y)
    line = (8, width_y)
    total, coded, coded_other, *_ = pl.pallas_call(
        functools.partial(last_kernel, capsules),
        in_specs=ins(20, 2),
        out_specs=ins(8),
        out_shape=outs(half, line, line, field, field, field, field, slab),
        scratch_shapes=[
            VMEM((6 * shots * width_x, 2 * width_y), jnp.bfloat16),
            VMEM((windows, 2 * width_y), jnp.bfloat16), VMEM((windows, width_y), F32),
        ],
        input_output_aliases={15: 3, 16: 4, 17: 5, 18: 6, 19: 7},
        compiler_params=params,
        name="last",
    )(
        core[None], corners, halo, others, fields, bound_mask, vel, pres, damp, pd, back_other,
        back, rows, high, low, b1_other, b2_other, b1, b2, grad,
    )

    groups = [list(range(c, peers, 2)) for c in range(2)]
    copies = jnp.broadcast_to(total, (peers // 2, *half))
    total = lax.all_to_all(
        copies, "shot", split_axis=0, concat_axis=0, tiled=True, axis_index_groups=groups
    ).reshape(peers // 2, *half).sum(axis=0)
    total, coded, coded_other, later = lax.optimization_barrier((total, coded, coded_other, core))
    other = lax.ppermute(jnp.concatenate([total, coded_other], axis=0), "shot", pairs)
    gradient, recording = pl.pallas_call(
        join_kernel,
        in_specs=ins(4, 1),
        out_specs=[pl.BlockSpec(memory_space=pltpu.HBM)] * 2,
        out_shape=[
            pltpu.HBM((depth * width_x, width_y), F32),
            pltpu.HBM((slots, shots, steps, channels), F32),
        ],
        scratch_shapes=[
            VMEM((slots, shots, steps, channels), F32), pltpu.SemaphoreType.DMA((3,)),
        ],
        compiler_params=params,
        name="join",
    )(later[None], total, other, coded)
    return recording, gradient.reshape(slab)


def solution(mesh):
    placed = (
        P("shot", "slab", None, None), P("shot", "slab", None, None),
        P("slab", None, None), P("slab", None, None), P("slab", None, None), P("slab", None, None),
        P("slab", None), P("slab"), P(), P("slab", "shot", None, None),
    )
    return jax.shard_map(
        body, mesh=mesh, in_specs=placed,
        out_specs=(P("slab", "shot", None, None), P("slab", None, None)),
        check_vma=False,
    )
```
